32 devices in a mesh: seq: 2 (over x), ctx: 16 (over z, y, core).
Axes of the slice: x: 2, y: 2, z: 4, core: 2. Of those that a mesh axis runs over, the one named last changes fastest.
Arguments:
- inputs: bfloat16 [2, 2048, 768], P('seq', 'ctx'), may hold values from -6 to 6
- lengths: int32 [2], P('seq'), may hold values from 512 to 2048, as said below
- cotangent: bfloat16 [2, 2048, 768], P('seq', 'ctx'), may hold values from -6 to 6
- w_qkv: bfloat16 [768, 2304], P(('seq', 'ctx')), may hold values from -0.21875 to 0.21875
- w_out: bfloat16 [768, 768], P(('seq', 'ctx')), may hold values from -6 to 6
- w_in: bfloat16 [768, 3072], P(('seq', 'ctx')), may hold values from -0.21875 to 0.21875
- w_back: bfloat16 [3072, 768], P(('seq', 'ctx')), may hold values from -0.109375 to 0.109375
- vectors: bfloat16 [768, 8], P(('seq', 'ctx')), may hold values from -1 to 2
- ffn_bias: bfloat16 [3072], P(('seq', 'ctx')), may hold values from -2 to 2
Outputs:
- result: bfloat16 [2, 2048, 768], P('seq', 'ctx')
- grad_inputs: float32 [2, 2048, 768], P('seq', 'ctx')
- grad_w_qkv: float32 [768, 2304], P(('seq', 'ctx'))
- grad_w_out: float32 [768, 768], P(('seq', 'ctx'))
- grad_w_in: float32 [768, 3072], P(('seq', 'ctx'))
- grad_w_back: float32 [3072, 768], P(('seq', 'ctx'))
- grad_vectors: float32 [768, 8], P(('seq', 'ctx'))
- grad_ffn_bias: float32 [3072], P(('seq', 'ctx'))
The draws below stay inside these ranges and needn't reach their ends.
Inputs may be any that keep to these rules, and one draw needn't show every extreme that they name: `lengths`: one sequence of each draw is full.
All inputs are finite; a program needn't handle non-finite values.
Results may differ from the reference program's by a relative error of at most 0.025.
Values may be sent and summed in bfloat16 or wider, within the bound.
A program may use at most 448 MiB of HBM per device.

```python
import jax
import jax.numpy as jnp
from jax import lax

D = 768
HEADS = 12
HEAD = 64
FF = 3072
LEN = 2048
SEQS = 2


def draw_lengths(key, part):
    left_key, right_key = jax.random.split(key)
    drawn_lengths = jax.random.randint(left_key, (SEQS,), LEN // 4, LEN + 1)
    chosen = jax.random.randint(right_key, (), 0, SEQS)
    return jnp.where(jnp.arange(SEQS) == chosen, LEN, drawn_lengths).astype(jnp.int32)


def draw_vectors(key, part):
    normal_draw = jnp.clip(jax.random.normal(key, (D, 8), jnp.float32), -6.0, 6.0)
    column = jnp.arange(8)[None, :]
    is_gain = (column == 3) | (column == 6)
    bias_scale = jnp.where(column == 1, 0.3 * (3.0 / LEN) ** 0.5, 0.1)
    drawn_values = jnp.where(is_gain, 1.0 + 0.1 * normal_draw, bias_scale * normal_draw)
    return drawn_values.astype(jnp.bfloat16)


def raised(drawn, own_key, source, target, parts, factor):
    owner, partner = [(jnp.arange(drawn.shape[axis_at]) // (drawn.shape[axis_at] // parts)).reshape([-1 if axis == axis_at else 1 for axis in range(drawn.ndim)]) for axis_at in (source, target)]
    chosen = jax.random.permutation(own_key, parts)[partner]
    strong = (owner == chosen) | (owner == (partner + parts // 2) % parts)
    return jnp.where(strong, factor * drawn, drawn)


def levels(key, dims, pieces, low, top_value):
    def one(dim, shards_of):
        heights = jax.random.uniform(jax.random.fold_in(jax.random.fold_in(key, 6), dim), (shards_of,), jnp.float32, low / len(pieces), top_value / len(pieces))
        return jnp.repeat(jnp.exp(heights), dims[dim] // shards_of).reshape((-1,) + (1,) * (len(dims) - dim - 1))

    gain = one(*pieces[0])
    for cut in pieces[1:]:
        gain = gain * one(*cut)
    return gain


def noise(key, shape, width, limit, pieces=(), held_as=jnp.bfloat16):
    gain = levels(key, shape, pieces, -0.22, 0.18) if pieces else 1.0
    drawn = jax.random.normal(key, shape, jnp.float32) * width * gain
    return jnp.minimum(jnp.maximum(drawn, -limit), limit).astype(held_as)


def heavy_noise(key, shape, deviation, reach, cuts, heavy, held_as=jnp.bfloat16):
    array = deviation * jax.random.normal(key, shape, jnp.float32)
    if cuts:
        array = array * levels(key, shape, cuts, -0.22, 0.18)
    return jnp.clip(raised(array, jax.random.fold_in(key, 3), *heavy), -reach, reach).astype(held_as)


def setup_inputs(seed: int = 0) -> dict:
    seeds = jax.random.split(jax.random.key(seed), 10)
    inputs = heavy_noise(seeds[0], (SEQS, LEN, D), 1.0, 6.0, ((0, 2), (1, 16)), (1, 2, 16, 2.0))
    lengths = draw_lengths(jax.random.fold_in(seeds[9], 71), 0)
    cotangent = noise(seeds[2], (SEQS, LEN, D), 1.0, 6.0, ((0, 2), (1, 16)))
    w_qkv = noise(seeds[3], (D, 3 * D), D ** -0.5, 0.21875, ((0, 32),))
    w_out = noise(seeds[4], (D, D), (max(1, LEN // (3 * D)) ** 0.5), 6.0, ((0, 32),))
    w_in = noise(seeds[5], (D, FF), D ** -0.5, 0.21875, ((0, 32),))
    w_back = noise(seeds[6], (FF, D), FF ** -0.5, 0.109375, ((0, 32),))
    vectors = draw_vectors(jax.random.fold_in(seeds[9], 71), 0)
    ffn_bias = noise(seeds[8], (FF,), 0.3, 2.0, ((0, 32),))
    return {"inputs": inputs, "lengths": lengths, "cotangent": cotangent, "w_qkv": w_qkv, "w_out": w_out, "w_in": w_in, "w_back": w_back, "vectors": vectors, "ffn_bias": ffn_bias}


EPSILON = 1e-12
MASKED = -1e+30
HIGHEST = lax.Precision.HIGHEST

@jax.custom_vjp
def low(v):
    return lax.optimization_barrier(v.astype(jnp.bfloat16)).astype(jnp.float32)

@jax.custom_vjp
def low_back(v):
    return v

def low_keep(v):
    return (low(v), None)

def low_pass(kept, grad):
    return (grad,)

def back_keep(v):
    return (v, None)

def back_low(kept, grad):
    return (low(grad),)
low.defvjp(low_keep, low_pass)
low_back.defvjp(back_keep, back_low)

def matmul(left_side, right_side):
    return jnp.dot(left_side, right_side, precision=HIGHEST, preferred_element_type=jnp.float32)

def layer_norm(values_in, norm_gain, norm_shift):
    average = lax.optimization_barrier(jnp.mean(values_in, axis=-1, keepdims=True))
    centred = values_in - average
    spread = lax.optimization_barrier(jnp.mean(centred * centred, axis=-1, keepdims=True))
    return centred * lax.rsqrt(spread + EPSILON) * norm_gain + norm_shift

def attention(queries, key_rows, value_rows, length):
    total_rows = queries.shape[0]
    block_rows = min(512, total_rows)
    key_heads = key_rows.reshape(total_rows, HEADS, HEAD)
    value_heads = value_rows.reshape(total_rows, HEADS, HEAD)
    usable = (jnp.arange(total_rows, dtype=jnp.int32) < length)[None, None, :]

    def one_block(query_block):
        query_heads = query_block.reshape(block_rows, HEADS, HEAD)
        scores = low_back(jnp.einsum('qhd,khd->hqk', query_heads, key_heads, precision=HIGHEST) * HEAD ** (-0.5))
        masked = jnp.where(usable, scores, MASKED)
        row_top = lax.optimization_barrier(jnp.max(masked, axis=-1, keepdims=True))
        expanded = jnp.exp(masked - row_top)
        soft_weights = expanded / lax.optimization_barrier(jnp.sum(expanded, axis=-1, keepdims=True))
        attended = jnp.einsum('hqk,khd->qhd', low(soft_weights), value_heads, precision=HIGHEST)
        return attended.reshape(block_rows, HEADS * HEAD)
    blocks = lax.map(jax.checkpoint(one_block), queries.reshape(total_rows // block_rows, block_rows, HEADS * HEAD))
    return blocks.reshape(total_rows, HEADS * HEAD)

def encode(own_inputs, length, w_qkv, w_out, w_in, w_back, vectors, ffn_bias):
    model_width = own_inputs.shape[1]
    projected = matmul(own_inputs, w_qkv)
    queries = low_back(low(projected[:, :model_width] + vectors[:, 0]))
    key_rows = low_back(low(projected[:, model_width:2 * model_width]))
    value_rows = low_back(low(projected[:, 2 * model_width:] + vectors[:, 1]))
    attended = low_back(low(attention(queries, key_rows, value_rows, length)))
    branch = low_back(matmul(attended, w_out) + vectors[:, 2])
    normed_first = layer_norm(own_inputs + branch, vectors[:, 3], vectors[:, 4])
    hidden = low_back(matmul(low(normed_first), w_in) + ffn_bias)
    active = low(jax.nn.gelu(hidden, approximate=False))
    second = low_back(matmul(active, w_back) + vectors[:, 5])
    return layer_norm(normed_first + second, vectors[:, 6], vectors[:, 7])

def reference(inputs, lengths, cotangent, w_qkv, w_out, w_in, w_back, vectors, ffn_bias):
    weights_f = tuple((weight_arg.astype(jnp.float32) for weight_arg in (w_qkv, w_out, w_in, w_back, vectors, ffn_bias)))
    inputs_f = inputs.astype(jnp.float32)

    def forward(inputs_all, *params):

        def one_sequence(sequence_pair):
            return encode(sequence_pair[0], sequence_pair[1], *params)
        return lax.map(one_sequence, (inputs_all, lengths))
    result, pullback = jax.vjp(forward, inputs_f, *weights_f)
    valid_rows = (jnp.arange(LEN, dtype=jnp.int32)[None, :] < lengths[:, None]).astype(jnp.float32)
    grads_all = pullback(cotangent.astype(jnp.float32) * valid_rows[:, :, None])
    return (result.astype(jnp.bfloat16), grads_all[0], grads_all[1], grads_all[2], grads_all[3], grads_all[4], grads_all[5], grads_all[6])
```

```python
import functools, math
import jax, jax.numpy as jnp
from jax import lax
from jax.experimental import pallas as pl
from jax.experimental.pallas import tpu as pltpu

MESH = pl.DeviceIdType.MESH

class Grid:
    def __init__(self, seqs, ctx):
        self.seqs, self.ctx = seqs, ctx
        self.depth = ctx // 4
    def here(self):
        s, i = lax.axis_index("seq"), lax.axis_index("ctx")
        return s, i // 4, (i // 2) % 2, i % 2

def cid(z, y, c):
    return (z * 2 + y) * 2 + c

def greet(grid, with_seq):
    s, z, y, c = grid.here()
    bar = pltpu.get_barrier_semaphore()
    def hello(p):
        pl.semaphore_signal(bar, inc=1, device_id=p, device_id_type=MESH)
    peers = [(s, cid(z, 1 - y, c)), (s, cid(z, y, 1 - c))]
    if with_seq:
        peers += [(1 - s, cid(z, y, c))]
    for p in peers:
        hello(p)
    @pl.when(z > 0)
    def _():
        hello((s, cid(z - 1, y, c)))
    @pl.when(z < grid.depth - 1)
    def _():
        hello((s, cid(z + 1, y, c)))
    ends = jnp.where(z > 0, 1, 0) + jnp.where(z < grid.depth - 1, 1, 0)
    pl.semaphore_wait(bar, len(peers) + ends)

def each(n, body):
    if n <= 4:
        for k in range(n):
            body(k)
    else:
        lax.fori_loop(0, n, lambda k, _: (body(k), None)[1], None)

class Gather:
    def __init__(self, grid, src, dst, send, zsend, recv, local, order, cols=None):
        self.g, self.src, self.dst = grid, src, dst
        self.send, self.zsend, self.recv, self.local, self.order = send, zsend, recv, local, order
        self.cols = cols
        self.s, self.z, self.y, self.c = grid.here()
        self.rest = order[1:]
    def view(self, b):
        return self.dst.at[b] if self.cols is None else self.dst.at[b, :, self.cols]
    def own(self):
        return self.src.at[0] if self.cols is None else self.src.at[0, :, self.cols]
    def push(self, src, b, dev, sem):
        pltpu.make_async_remote_copy(src, self.view(b), sem, self.recv.at[b], device_id=dev, device_id_type=MESH).start()
    def wait(self, b, sem=None):
        v = self.view(b)
        pltpu.make_async_copy(v, v, self.recv.at[b] if sem is None else sem).wait()
    def dev(self, dim):
        if dim == 'x': return (1 - self.s, cid(self.z, self.y, self.c))
        if dim == 'y': return (self.s, cid(self.z, 1 - self.y, self.c))
        if dim == 'c': return (self.s, cid(self.z, self.y, 1 - self.c))
        return (self.s, cid(self.z + (1 if dim == '+' else -1), self.y, self.c))
    def at(self, flips, z):
        s = 1 - self.s if 'x' in flips else self.s
        y = 1 - self.y if 'y' in flips else self.y
        c = 1 - self.c if 'c' in flips else self.c
        return cid(z, y, c) + (s * self.g.ctx if 'x' in self.order else 0)
    def zpush(self, src, b, z, side):
        ok = self.z < self.g.depth - 1 if side == '+' else self.z > 0
        @pl.when(ok)
        def _():
            self.push(src, b, self.dev(side), self.zsend.at[0 if side == '+' else 1, z])
    def start(self):
        own = self.at('', self.z)
        for side in '+-':
            self.zpush(self.own(), own, self.z, side)
        for dim in self.rest + 'c':
            self.push(self.own(), own, self.dev(dim), self.send)
        pltpu.make_async_copy(self.own(), self.view(own), self.local).start()
    def sides(self, d, body):
        if isinstance(d, int) and d == 0:
            body(self.z, '')
            return
        @pl.when(self.z - d >= 0)
        def _():
            body(self.z - d, '-')
        @pl.when(self.z + d < self.g.depth)
        def _():
            body(self.z + d, '+')
    def line(self, d):
        def go(z, side):
            b = self.at('', z)
            self.wait(b)
            self.zpush(self.view(b), b, z, '+' if side == '-' else '-')
            for k in self.rest + 'c':
                self.push(self.view(b), b, self.dev(k), self.send)
        self.sides(d, go)
    def cross(self, flips, dims, d):
        def go(z, side):
            b = self.at(flips, z)
            self.wait(b)
            for k in dims:
                self.push(self.view(b), b, self.dev(k), self.send)
        self.sides(d, go)
    def step(self, t):
        r = self.rest
        if t < self.g.depth:
            self.line(t)
        if 1 <= t <= self.g.depth:
            self.cross(r[0], r[1:] + 'c', t - 1)
        if len(r) > 1:
            if 1 <= t <= self.g.depth:
                self.cross(r[1], 'c', t - 1)
            if 2 <= t <= self.g.depth + 1:
                self.cross(r, 'c', t - 2)
    def steps(self):
        return self.g.depth + len(self.rest)
    def finish(self):
        r = self.rest
        sets = ['', r[0]] + ([r[1], r] if len(r) > 1 else [])
        for f in sets:
            def go(k, f=f):
                self.wait(self.at(f + 'c', k))
            each(self.g.depth, go)
        self.wait(self.at('', self.z), self.local)
        def sent(k):
            for side in '+-':
                n = 0 if side == '+' else 1
                ok = (jnp.logical_and(self.z < self.g.depth - 1, k <= self.z) if side == '+'
                      else jnp.logical_and(self.z > 0, k >= self.z))
                @pl.when(ok)
                def _():
                    self.wait(self.at('', k), self.zsend.at[n, k])
        each(self.g.depth, sent)
        p = self.g.depth
        n = p + (2 * p if len(r) > 1 else 0) + (4 * p if len(r) > 1 else 2 * p)
        v = self.dst.at[pl.ds(0, n)] if self.cols is None else self.dst.at[pl.ds(0, n), :, self.cols]
        pltpu.make_async_copy(v, v, self.send).wait()

def run_gathers(jobs):
    for job in jobs: job.start()
    for t in range(1, max(j.steps() for j in jobs)):
        for job in jobs:
            job.step(t)
    for job in jobs: job.finish()

def gather_kernel(grid, plan, n_in, *refs):
    ins, outs = refs[:n_in], refs[n_in:2 * n_in]
    send, zsend, recv, local = refs[2 * n_in:]
    greet(grid, any('x' in p[1] for p in plan))
    jobs = [Gather(grid, ins[i], outs[i], send.at[j], zsend.at[j], recv.at[j], local.at[j], order, cols) for j, (i, order, cols) in enumerate(plan)]
    run_gathers(jobs)

def gather_sems(grid, plan):
    n = max(grid.ctx * (grid.seqs if 'x' in order else 1) for _, order, _ in plan)
    k = len(plan)
    return [pltpu.SemaphoreType.DMA((k,)), pltpu.SemaphoreType.DMA((k, 2, grid.depth)), pltpu.SemaphoreType.DMA((k, n)), pltpu.SemaphoreType.DMA((k,))]

def gather(grid, arrays, plan, name, cid_):
    full = {}
    for i, order, cols in plan:
        full[i] = grid.ctx * (grid.seqs if 'x' in order else 1)
    outs = [jax.ShapeDtypeStruct((full[i],) + a.shape[1:], a.dtype) for i, a in enumerate(arrays)]
    return pl.pallas_call(
        functools.partial(gather_kernel, grid, plan, len(arrays)),
        out_shape=outs,
        in_specs=[pl.BlockSpec(memory_space=pltpu.VMEM)] * len(arrays),
        out_specs=[pl.BlockSpec(memory_space=pl.ANY)] * len(arrays),
        scratch_shapes=gather_sems(grid, plan),
        compiler_params=pltpu.CompilerParams(collective_id=cid_, has_side_effects=True),
        name=name,
    )(*arrays)
from jax.sharding import PartitionSpec as P

def f32(x):
    return x.astype(jnp.float32)

class Scatter:
    def __init__(self, grid, src, out, bufs, send, zsend, recvs, order):
        self.g, self.src, self.out = grid, src, out
        self.bufc, self.buf1, self.buf2, self.bufz = bufs
        self.send, self.zsend, self.order = send, zsend, order
        self.rc, self.r1, self.r2, self.rz = recvs
        self.dims = order[:0:-1]
        self.two = len(self.dims) > 1
        self.s, self.z, self.y, self.c = grid.here()
    at = Gather.at
    dev = Gather.dev
    def flips(self, f):
        return ''.join(d for d, on in zip(self.dims, f) if on)
    def idx(self, f, z):
        k = 0
        for on in f:
            k = k * 2 + on
        return k * self.g.depth + z
    def push(self, src, dst, recv, dim):
        pltpu.make_async_remote_copy(src, dst, self.send, recv, device_id=self.dev(dim), device_id_type=MESH).start()
    def wait(self, ref, sem):
        pltpu.make_async_copy(ref, ref, sem).wait()
    def combos(self):
        return [(1, 1), (1, 0), (0, 1), (0, 0)] if self.two else [(1,), (0,)]
    def far(self, d, body):
        @pl.when(self.z + d < self.g.depth)
        def _():
            body(self.z + d, '+')
        @pl.when(self.z >= d)
        def _():
            body(self.z - d, '-')
    def start(self):
        for f in self.combos():
            def go(z, side, f=f):
                k = self.idx(f, z)
                self.push(self.src.at[self.at(self.flips(f) + 'c', z)], self.bufc.at[k], self.rc.at[k], 'c')
            def loop(k, _, go=go):
                self.far(self.g.depth - 1 - k, go)
                return _
            lax.fori_loop(0, self.g.depth - 1, loop, None)
            go(self.z, '')
    def stage1(self, f, d):
        def go(z, side):
            k = self.idx(f, z)
            buf = self.bufc.at[k]
            self.wait(buf, self.rc.at[k])
            buf[...] = (f32(self.src[self.at(self.flips(f), z)]) + f32(buf[...])).astype(buf.dtype)
            j = self.idx(f[1:], z)
            self.push(buf, self.buf1.at[j], self.r1.at[j], self.dims[0])
        self.far(d, go) if d is not None else go(self.z, '')
    def stage2(self, d):
        def go(z, side):
            k, j = self.idx((0, 1), z), self.idx((1,), z)
            bufc, buf = self.bufc.at[k], self.buf1.at[j]
            self.wait(bufc, self.rc.at[k])
            self.wait(buf, self.r1.at[j])
            buf[...] = (f32(self.src[self.at(self.dims[1], z)]) + f32(bufc[...]) + f32(buf[...])).astype(buf.dtype)
            self.push(buf, self.buf2.at[z], self.r2.at[z], self.dims[1])
        self.far(d, go) if d is not None else go(self.z, '')
    def merged(self, z):
        k = self.idx((0,) * len(self.dims), z)
        bufc, buf1 = self.bufc.at[k], self.buf1.at[z]
        self.wait(bufc, self.rc.at[k])
        self.wait(buf1, self.r1.at[z])
        acc = f32(self.src[self.at('', z)]) + f32(bufc[...]) + f32(buf1[...])
        if self.two:
            buf2 = self.buf2.at[z]
            self.wait(buf2, self.r2.at[z])
            acc = acc + f32(buf2[...])
        return acc, bufc
    def chain(self, d):
        top = self.g.depth - 1
        def go(zz, side):
            n = 0 if side == '+' else 1
            more = self.z > 0 if side == '+' else self.z < top
            acc, keep = self.merged(zz)
            keep[...] = acc.astype(keep.dtype)
            buf = self.bufz.at[n, zz]
            @pl.when(more)
            def _():
                self.wait(buf, self.rz.at[n, zz])
                keep[...] = (f32(keep[...]) + f32(buf[...])).astype(keep.dtype)
            pltpu.make_async_remote_copy(keep, buf, self.zsend.at[n, zz], self.rz.at[n, zz], device_id=self.dev(side), device_id_type=MESH).start()
        self.far(d, go)
    def total(self):
        top = self.g.depth - 1
        acc, _ = self.merged(self.z)
        self.out[0] = acc
        for n, ok in ((0, self.z > 0), (1, self.z < top)):
            @pl.when(ok)
            def _(n=n):
                buf = self.bufz.at[n, self.z]
                self.wait(buf, self.rz.at[n, self.z])
                self.out[0] += f32(buf[...])
    def finish(self):
        def sent(k):
            for n, ok in ((0, k > self.z), (1, k < self.z)):
                @pl.when(ok)
                def _(n=n):
                    self.wait(self.bufz.at[n, k], self.zsend.at[n, k])
        each(self.g.depth, sent)
        p = self.g.depth
        n = (4 + 2 + 1) * p if self.two else (2 + 1) * p
        v = self.src.at[pl.ds(0, n)]
        self.wait(v, self.send)

def run_scatters(jobs):
    depth = jobs[0].g.depth
    for job in jobs: job.start()
    def sweep(step, own):
        def loop(k, _):
            for job in jobs: step(job, depth - 1 - k)
            return _
        lax.fori_loop(0, depth - 1, loop, None)
        for job in jobs: own(job)
    sweep(lambda j, d: j.stage1(j.combos()[0], d), lambda j: j.stage1(j.combos()[0], None))
    sweep(lambda j, d: j.stage1((1, 0), d) if j.two else None, lambda j: j.stage1((1, 0), None) if j.two else None)
    sweep(lambda j, d: j.stage2(d) if j.two else None, lambda j: j.stage2(None) if j.two else None)
    sweep(lambda j, d: j.chain(d), lambda j: j.total())
    for job in jobs: job.finish()

def scatter_scratch(grid, shape, dtype, order):
    p = grid.depth
    two = len(order) > 2
    n1, nc = (2 * p, 4 * p) if two else (p, 2 * p)
    D = pltpu.SemaphoreType.DMA
    return [pltpu.VMEM((nc,) + shape, dtype), pltpu.VMEM((n1,) + shape, dtype), pltpu.VMEM((p if two else 1,) + (shape if two else (8, 128)), dtype), pltpu.VMEM((2, p) + shape, dtype),
            D(()), D((2, p)), D((nc,)), D((n1,)), D((p,)), D((2, p))]

def scatter_kernel(grid, orders, *refs):
    m = len(orders)
    ins, outs, rest = refs[:m], refs[m:2 * m], refs[2 * m:]
    greet(grid, any('x' in o for o in orders))
    jobs = []
    for j, order in enumerate(orders):
        r = rest[10 * j:10 * j + 10]
        jobs.append(Scatter(grid, ins[j], outs[j], r[:4], r[4], r[5], r[6:10], order))
    run_scatters(jobs)

def scatter(grid, arrays, orders, name, cid_):
    scratch = []
    for a, o in zip(arrays, orders):
        scratch += scatter_scratch(grid, a.shape[1:], a.dtype, o)
    V = pl.BlockSpec(memory_space=pltpu.VMEM)
    return pl.pallas_call(
        functools.partial(scatter_kernel, grid, tuple(orders)),
        out_shape=[jax.ShapeDtypeStruct((1,) + a.shape[1:], jnp.float32) for a in arrays],
        in_specs=[V] * len(arrays), out_specs=[V] * len(arrays),
        scratch_shapes=scratch,
        compiler_params=pltpu.CompilerParams(collective_id=cid_, has_side_effects=True, vmem_limit_bytes=60 * 2**20),
        name=name,
    )(*arrays)

def pair_stack(x, half):
    lane = lax.broadcasted_iota(jnp.int32, x.shape, 1)
    zero = jnp.zeros_like(x)
    return jnp.concatenate((jnp.where(lane < half, x, zero), jnp.where(lane < half, zero, x)), axis=0)

def pair_join(x, half):
    r = x.shape[0] // 2
    lane = lax.broadcasted_iota(jnp.int32, (r, x.shape[1]), 1)
    return jnp.where(lane < half, x[:r], x[r:])

def nt(a, b):
    return lax.dot_general(a, b, (((1,), (1,)), ((), ())), preferred_element_type=jnp.float32)

def nn(a, b):
    return lax.dot_general(a, b, (((1,), (0,)), ((), ())), preferred_element_type=jnp.float32)

def tn(a, b):
    return lax.dot_general(a, b, (((0,), (0,)), ((), ())), preferred_element_type=jnp.float32)

def as_row(col):
    return jnp.transpose(jnp.broadcast_to(col, (col.shape[0], 128)))[0:1]

MASKED = -1e30

def forward_kernel(half, tiles, len_ref, q_ref, k_ref, v_ref, o_ref, lse_ref, top_ref, sum_ref, acc_ref):
    t = pl.program_id(1)
    q2 = pair_stack(q_ref[...], half)
    s = nt(q2, k_ref[...])
    wide = s.shape[1]
    col = lax.broadcasted_iota(jnp.int32, (1, wide), 1) + t * wide
    s = jnp.where(col < len_ref[0], s, MASKED)
    top = jnp.max(s, axis=1, keepdims=True)
    if tiles > 1:
        old = jnp.where(t == 0, MASKED, top_ref[...])
        top = jnp.maximum(old, top)
    p = jnp.exp(s - top)
    total = jnp.sum(p, axis=1, keepdims=True)
    acc = nn(p.astype(jnp.bfloat16), v_ref[...])
    if tiles > 1:
        factor = jnp.where(t == 0, 0.0, jnp.exp(old - top))
        total = total + jnp.where(t == 0, 0.0, sum_ref[...]) * factor
        acc = acc + jnp.where(t == 0, 0.0, acc_ref[...]) * factor
        top_ref[...], sum_ref[...], acc_ref[...] = top, total, acc
    @pl.when(t == tiles - 1)
    def _():
        o_ref[...] = pair_join(acc / total, half)
        lse_ref[0] = as_row(top + jnp.log(total))

def attend(q, k, v, length, heads, tile):
    rows, width = q.shape
    size = width // heads
    total, pairs = k.shape[0], heads // 2
    tiles = total // tile
    wide = 2 * size
    return pl.pallas_call(
        functools.partial(forward_kernel, size, tiles),
        grid_spec=pltpu.PrefetchScalarGridSpec(
            num_scalar_prefetch=1, grid=(pairs, tiles),
            in_specs=[pl.BlockSpec((rows, wide), lambda p, t, n: (0, p)),
                      pl.BlockSpec((tile, wide), lambda p, t, n: (t, p)),
                      pl.BlockSpec((tile, wide), lambda p, t, n: (t, p))],
            out_specs=[pl.BlockSpec((rows, wide), lambda p, t, n: (0, p)),
                       pl.BlockSpec((1, 1, 2 * rows), lambda p, t, n: (p, 0, 0))],
            scratch_shapes=[pltpu.VMEM((2 * rows, 1), jnp.float32), pltpu.VMEM((2 * rows, 1), jnp.float32), pltpu.VMEM((2 * rows, wide), jnp.float32)]),
        out_shape=[jax.ShapeDtypeStruct((rows, width), jnp.float32), jax.ShapeDtypeStruct((pairs, 1, 2 * rows), jnp.float32)],
        name="attend",
    )(length, q, k, v)

def backward_kernel(half, tiles, scale, len_ref, q_ref, k_ref, v_ref, g_ref, o_ref, lse_ref, dq_ref, dk_ref, dv_ref, acc_ref):
    t = pl.program_id(1)
    q2 = pair_stack(q_ref[...], half)
    g2 = pair_stack(g_ref[...], half)
    k, v = k_ref[...], v_ref[...]
    prod = pair_stack(g_ref[...].astype(jnp.float32) * o_ref[...], half)
    delta = jnp.sum(jnp.transpose(prod), axis=0, keepdims=True)
    s = nt(k, q2)
    row = lax.broadcasted_iota(jnp.int32, (s.shape[0], 1), 0) + t * s.shape[0]
    p = jnp.where(row < len_ref[0], jnp.exp(s - lse_ref[0]), 0.0)
    dp = nt(v, g2)
    ds = (p * (dp - delta)).astype(jnp.bfloat16)
    dk_ref[...] = nn(ds, q2).astype(jnp.bfloat16)
    dv_ref[...] = nn(p.astype(jnp.bfloat16), g2).astype(jnp.bfloat16)
    dq = tn(ds, k)
    if tiles > 1:
        dq = dq + jnp.where(t == 0, 0.0, acc_ref[...])
        acc_ref[...] = dq
    @pl.when(t == tiles - 1)
    def _():
        dq_ref[...] = (pair_join(dq, half) * scale).astype(jnp.bfloat16)

def attend_back(q, k, v, g, o, lse, length, heads, tile):
    rows, width = q.shape
    size = width // heads
    total, pairs = k.shape[0], heads // 2
    tiles = total // tile
    wide = 2 * size
    R = pl.BlockSpec((rows, wide), lambda p, t, n: (0, p))
    K = pl.BlockSpec((tile, wide), lambda p, t, n: (t, p))
    return pl.pallas_call(
        functools.partial(backward_kernel, size, tiles, size ** -0.5),
        grid_spec=pltpu.PrefetchScalarGridSpec(
            num_scalar_prefetch=1, grid=(pairs, tiles),
            in_specs=[R, K, K, R, R, pl.BlockSpec((1, 1, 2 * rows), lambda p, t, n: (p, 0, 0))],
            out_specs=[R, K, K],
            scratch_shapes=[pltpu.VMEM((2 * rows, wide), jnp.float32)]),
        out_shape=[jax.ShapeDtypeStruct((rows, width), jnp.bfloat16)] + [jax.ShapeDtypeStruct((total, width), jnp.bfloat16)] * 2,
        name="attend_back",
    )(length, q, k, v, g, o, lse)
HEADS = 12
EPSILON = 1e-12
ROOM = 52 * 2**20

def normalize(u):
    mean = jnp.mean(u, axis=-1, keepdims=True)
    centred = u - mean
    r = lax.rsqrt(jnp.mean(centred * centred, axis=-1, keepdims=True) + EPSILON)
    return centred * r, r

def normalize_back(e, n, r, gain):
    c = e * gain
    return r * (c - jnp.mean(c, axis=-1, keepdims=True) - n * jnp.mean(c * n, axis=-1, keepdims=True))

def gelu_parts(v):
    cdf = 0.5 * (1.0 + lax.erf(v * (0.5 ** 0.5)))
    slope = cdf + v * jnp.exp(-0.5 * v * v) * ((2 * jnp.pi) ** -0.5)
    return v * cdf, slope

def padded(shape, dtype):
    sub = 32 // jnp.dtype(dtype).itemsize // 1 if False else (8 if jnp.dtype(dtype).itemsize == 4 else 16)
    return math.prod(shape[:-2]) * (-(-shape[-2] // sub) * sub) * (-(-shape[-1] // 128) * 128) * jnp.dtype(dtype).itemsize

def reduce_blocks(grid, arrays, orders, name, cid_):
    need = sum(padded(a.shape, a.dtype) * 3 for a in arrays)
    if need <= ROOM + 20 * 2**20 and grid.depth <= 4:
        return scatter(grid, arrays, orders, name, cid_)
    out = []
    for a, order in zip(arrays, orders):
        axes = ("seq", "ctx") if "x" in order else "ctx"
        out.append(lax.psum_scatter(a.astype(jnp.float32), axes, scatter_dimension=0, tiled=True))
    return out

def per_device(grid, inputs, lengths, cotangent, w_qkv, w_out, w_in, w_back, vectors, ffn_bias):
    bf, f4 = jnp.bfloat16, jnp.float32
    rows_in = inputs[0]
    rows, width = rows_in.shape
    hidden_size = w_in.shape[1]
    devices = grid.seqs * grid.ctx
    part, part_ff = w_qkv.shape[0], w_back.shape[0]
    slots = grid.ctx * rows
    scale = (width // HEADS) ** -0.5

    small = jnp.concatenate((jnp.pad(vectors.T, ((0, 0), (0, 128 - part))), jnp.pad(ffn_bias[None], ((0, 7), (0, 128 - part_ff)))), axis=0)[None]
    half = 3 * width // 2
    qkv_all, small_all = gather(grid, [w_qkv[None], small], [(0, "zyx", pl.ds(0, half)), (0, "zxy", pl.ds(half, half)), (1, "zyx", None)], "gather_qkv", 0)
    qkv_full = qkv_all.reshape(width, 3 * width)
    vec = small_all[:, :8, :part].transpose(1, 0, 2).reshape(8, width).astype(f4)
    ffn_full = small_all[:, 8, :part_ff].reshape(1, hidden_size).astype(f4)

    projected = jnp.dot(rows_in, qkv_full, preferred_element_type=f4)
    query = (projected[:, :width] + vec[0]).astype(bf)
    key = projected[:, width:2 * width].astype(bf)
    value = (projected[:, 2 * width:] + vec[1]).astype(bf)
    key_all, value_all, out_all, in_all, back_all = gather(
        grid, [key[None], value[None], w_out[None], w_in[None], w_back[None]],
        [(0, "zy", None), (1, "zy", None), (2, "zyx", None), (3, "zyx", None), (4, "zxy", None)], "gather_rest", 1)
    key_all, value_all = key_all.reshape(slots, width), value_all.reshape(slots, width)
    out_full, in_full, back_full = out_all.reshape(width, width), in_all.reshape(width, hidden_size), back_all.reshape(hidden_size, width)

    tile = min(slots, 2048)
    query_scaled = query * jnp.asarray(scale, bf)
    attended_f, lse = attend(query_scaled, key_all, value_all, lengths, HEADS, tile)
    attended = attended_f.astype(bf)
    branch = jnp.dot(attended, out_full, preferred_element_type=f4) + vec[2]
    norm_one, r_one = normalize(rows_in.astype(f4) + branch)
    first = norm_one * vec[3] + vec[4]
    first_low = first.astype(bf)
    hidden = jnp.dot(first_low, in_full, preferred_element_type=f4) + ffn_full
    active_f, slope = gelu_parts(hidden)
    active = active_f.astype(bf)
    second = jnp.dot(active, back_full, preferred_element_type=f4) + vec[5]
    norm_two, r_two = normalize(first + second)
    result = (norm_two * vec[6] + vec[7]).astype(bf)
    start = lax.axis_index("ctx") * rows
    valid = (start + jnp.arange(rows, dtype=jnp.int32) < lengths[0]).astype(f4)[:, None]
    grad_result = cotangent[0].astype(f4) * valid
    grad_second = normalize_back(grad_result, norm_two, r_two, vec[6])
    grad_second_low = grad_second.astype(bf)
    grad_active = lax.dot_general(grad_second_low, back_full, (((1,), (1,)), ((), ())), preferred_element_type=f4)
    grad_hidden = (grad_active * slope).astype(bf)
    grad_first = grad_second + lax.dot_general(grad_hidden, in_full, (((1,), (1,)), ((), ())), preferred_element_type=f4)
    grad_branch_full = normalize_back(grad_first, norm_one, r_one, vec[3])
    grad_branch = grad_branch_full.astype(bf)
    grad_attended = lax.dot_general(grad_branch, out_full, (((1,), (1,)), ((), ())), preferred_element_type=f4).astype(bf)

    def outer(a, b):
        return lax.dot_general(a, b, (((0,), (0,)), ((), ())), preferred_element_type=f4).astype(bf)
    g_back = outer(active, grad_second_low).reshape(devices, part_ff, width)
    g_in = outer(first_low, grad_hidden).reshape(devices, part, hidden_size)
    g_out = outer(attended, grad_branch).reshape(devices, part, width)
    grad_query, g_key, g_value = attend_back(query_scaled, key_all, value_all, grad_attended, attended_f, lse, lengths, HEADS, tile)
    own_key, own_value, d_out, d_in, d_back = reduce_blocks(
        grid, [g_key.reshape(grid.ctx, rows, width), g_value.reshape(grid.ctx, rows, width), g_out, g_in, g_back],
        ["zy", "zy", "zyx", "zyx", "zxy"], "reduce_rest", 2)
    grad_projected = jnp.concatenate((grad_query, own_key[0].astype(bf), own_value[0].astype(bf)), axis=1)
    g_qkv = outer(rows_in, grad_projected).reshape(devices, part, 3 * width)
    grad_inputs = grad_branch_full + lax.dot_general(grad_projected, qkv_full, (((1,), (1,)), ((), ())), preferred_element_type=f4)
    sums = jnp.stack((
        jnp.sum(grad_query.astype(f4), axis=0), jnp.sum(own_value[0].astype(bf).astype(f4), axis=0),
        jnp.sum(grad_branch.astype(f4), axis=0), jnp.sum(grad_first * norm_one, axis=0), jnp.sum(grad_first, axis=0),
        jnp.sum(grad_second_low.astype(f4), axis=0), jnp.sum(grad_result * norm_two, axis=0), jnp.sum(grad_result, axis=0)))
    grad_ffn = jnp.sum(grad_hidden.astype(f4), axis=0)
    blocks = jnp.pad(sums.reshape(8, devices, part).transpose(1, 0, 2), ((0, 0), (0, 0), (0, 128 - part)))
    ffn_blocks = jnp.pad(grad_ffn.reshape(devices, 1, part_ff), ((0, 0), (0, 7), (0, 128 - part_ff)))
    g_small = jnp.concatenate((blocks, ffn_blocks), axis=1)
    d_qkv_a, d_qkv_b, d_small = reduce_blocks(grid, [g_qkv[:, :, :half], g_qkv[:, :, half:], g_small], ["zyx", "zxy", "zyx"], "reduce_qkv", 3)
    d_qkv = jnp.concatenate((d_qkv_a[0], d_qkv_b[0]), axis=1)
    return (result[None], grad_inputs[None], d_qkv, d_out[0], d_in[0], d_back[0], d_small[0, :8, :part].T, d_small[0, 8, :part_ff])

def solution(mesh):
    grid = Grid(mesh.shape["seq"], mesh.shape["ctx"])
    split, both = P("seq", "ctx", None), P(("seq", "ctx"), None)
    return jax.shard_map(
        functools.partial(per_device, grid), mesh=mesh,
        in_specs=(split, P("seq"), split, both, both, both, both, both, P(("seq", "ctx"))),
        out_specs=(split, split, both, both, both, both, both, P(("seq", "ctx"))),
        check_vma=False,
    )
```

```python
import functools, math
import jax, jax.numpy as jnp
from jax import lax
from jax.experimental import pallas as pl
from jax.experimental.pallas import tpu as pltpu

MESH = pl.DeviceIdType.MESH

class Grid:
    def __init__(self, seqs, ctx):
        self.seqs, self.ctx = seqs, ctx
        self.depth = ctx // 4
    def here(self):
        s, i = lax.axis_index("seq"), lax.axis_index("ctx")
        return s, i // 4, (i // 2) % 2, i % 2

def cid(z, y, c):
    return (z * 2 + y) * 2 + c

def greet(grid, with_seq):
    s, z, y, c = grid.here()
    bar = pltpu.get_barrier_semaphore()
    def hello(p):
        pl.semaphore_signal(bar, inc=1, device_id=p, device_id_type=MESH)
    peers = [(s, cid(z, 1 - y, c)), (s, cid(z, y, 1 - c))]
    if with_seq:
        peers += [(1 - s, cid(z, y, c))]
    for p in peers:
        hello(p)
    @pl.when(z > 0)
    def _():
        hello((s, cid(z - 1, y, c)))
    @pl.when(z < grid.depth - 1)
    def _():
        hello((s, cid(z + 1, y, c)))
    ends = jnp.where(z > 0, 1, 0) + jnp.where(z < grid.depth - 1, 1, 0)
    pl.semaphore_wait(bar, len(peers) + ends)

def each(n, body):
    if n <= 4:
        for k in range(n):
            body(k)
    else:
        lax.fori_loop(0, n, lambda k, _: (body(k), None)[1], None)

class Gather:
    def __init__(self, grid, src, dst, send, zsend, recv, local, order, cols=None):
        self.g, self.src, self.dst = grid, src, dst
        self.send, self.zsend, self.recv, self.local, self.order = send, zsend, recv, local, order
        self.cols = cols
        self.s, self.z, self.y, self.c = grid.here()
        self.rest = order[1:]
    def view(self, b):
        return self.dst.at[b] if self.cols is None else self.dst.at[b, :, self.cols]
    def own(self):
        return self.src.at[0] if self.cols is None else self.src.at[0, :, self.cols]
    def push(self, src, b, dev, sem):
        pltpu.make_async_remote_copy(src, self.view(b), sem, self.recv.at[b], device_id=dev, device_id_type=MESH).start()
    def wait(self, b, sem=None):
        v = self.view(b)
        pltpu.make_async_copy(v, v, self.recv.at[b] if sem is None else sem).wait()
    def dev(self, dim):
        if dim == 'x': return (1 - self.s, cid(self.z, self.y, self.c))
        if dim == 'y': return (self.s, cid(self.z, 1 - self.y, self.c))
        if dim == 'c': return (self.s, cid(self.z, self.y, 1 - self.c))
        return (self.s, cid(self.z + (1 if dim == '+' else -1), self.y, self.c))
    def at(self, flips, z):
        s = 1 - self.s if 'x' in flips else self.s
        y = 1 - self.y if 'y' in flips else self.y
        c = 1 - self.c if 'c' in flips else self.c
        return cid(z, y, c) + (s * self.g.ctx if 'x' in self.order else 0)
    def zpush(self, src, b, z, side):
        ok = self.z < self.g.depth - 1 if side == '+' else self.z > 0
        @pl.when(ok)
        def _():
            self.push(src, b, self.dev(side), self.zsend.at[0 if side == '+' else 1, z])
    def start(self):
        own = self.at('', self.z)
        for side in '+-':
            self.zpush(self.own(), own, self.z, side)
        for dim in self.rest + 'c':
            self.push(self.own(), own, self.dev(dim), self.send)
        pltpu.make_async_copy(self.own(), self.view(own), self.local).start()
    def sides(self, d, body):
        if isinstance(d, int) and d == 0:
            body(self.z, '')
            return
        @pl.when(self.z - d >= 0)
        def _():
            body(self.z - d, '-')
        @pl.when(self.z + d < self.g.depth)
        def _():
            body(self.z + d, '+')
    def line(self, d):
        def go(z, side):
            b = self.at('', z)
            self.wait(b)
            self.zpush(self.view(b), b, z, '+' if side == '-' else '-')
            for k in self.rest + 'c':
                self.push(self.view(b), b, self.dev(k), self.send)
        self.sides(d, go)
    def cross(self, flips, dims, d):
        def go(z, side):
            b = self.at(flips, z)
            self.wait(b)
            for k in dims:
                self.push(self.view(b), b, self.dev(k), self.send)
        self.sides(d, go)
    def step(self, t):
        r = self.rest
        if t < self.g.depth:
            self.line(t)
        if 1 <= t <= self.g.depth:
            self.cross(r[0], r[1:] + 'c', t - 1)
        if len(r) > 1:
            if 1 <= t <= self.g.depth:
                self.cross(r[1], 'c', t - 1)
            if 2 <= t <= self.g.depth + 1:
                self.cross(r, 'c', t - 2)
    def steps(self):
        return self.g.depth + len(self.rest)
    def finish(self):
        r = self.rest
        sets = ['', r[0]] + ([r[1], r] if len(r) > 1 else [])
        for f in sets:
            def go(k, f=f):
                self.wait(self.at(f + 'c', k))
            each(self.g.depth, go)
        self.wait(self.at('', self.z), self.local)
        def sent(k):
            for side in '+-':
                n = 0 if side == '+' else 1
                ok = (jnp.logical_and(self.z < self.g.depth - 1, k <= self.z) if side == '+'
                      else jnp.logical_and(self.z > 0, k >= self.z))
                @pl.when(ok)
                def _():
                    self.wait(self.at('', k), self.zsend.at[n, k])
        each(self.g.depth, sent)
        p = self.g.depth
        n = p + (2 * p if len(r) > 1 else 0) + (4 * p if len(r) > 1 else 2 * p)
        v = self.dst.at[pl.ds(0, n)] if self.cols is None else self.dst.at[pl.ds(0, n), :, self.cols]
        pltpu.make_async_copy(v, v, self.send).wait()

def run_gathers(jobs):
    for job in jobs: job.start()
    for t in range(1, max(j.steps() for j in jobs)):
        for job in jobs:
            job.step(t)
    for job in jobs: job.finish()

def gather_kernel(grid, plan, n_in, *refs):
    ins, outs = refs[:n_in], refs[n_in:2 * n_in]
    send, zsend, recv, local = refs[2 * n_in:]
    greet(grid, any('x' in p[1] for p in plan))
    jobs = [Gather(grid, ins[i], outs[i], send.at[j], zsend.at[j], recv.at[j], local.at[j], order, cols) for j, (i, order, cols) in enumerate(plan)]
    run_gathers(jobs)

def gather_sems(grid, plan):
    n = max(grid.ctx * (grid.seqs if 'x' in order else 1) for _, order, _ in plan)
    k = len(plan)
    return [pltpu.SemaphoreType.DMA((k,)), pltpu.SemaphoreType.DMA((k, 2, grid.depth)), pltpu.SemaphoreType.DMA((k, n)), pltpu.SemaphoreType.DMA((k,))]

def gather(grid, arrays, plan, name, cid_):
    full = {}
    for i, order, cols in plan:
        full[i] = grid.ctx * (grid.seqs if 'x' in order else 1)
    outs = [jax.ShapeDtypeStruct((full[i],) + a.shape[1:], a.dtype) for i, a in enumerate(arrays)]
    return pl.pallas_call(
        functools.partial(gather_kernel, grid, plan, len(arrays)),
        out_shape=outs,
        in_specs=[pl.BlockSpec(memory_space=pltpu.VMEM)] * len(arrays),
        out_specs=[pl.BlockSpec(memory_space=pl.ANY)] * len(arrays),
        scratch_shapes=gather_sems(grid, plan),
        compiler_params=pltpu.CompilerParams(collective_id=cid_, has_side_effects=True),
        name=name,
    )(*arrays)
from jax.sharding import PartitionSpec as P

def f32(x):
    return x.astype(jnp.float32)

class Scatter:
    def __init__(self, grid, src, out, bufs, send, zsend, recvs, order):
        self.g, self.src, self.out = grid, src, out
        self.bufc, self.buf1, self.buf2, self.bufz = bufs
        self.send, self.zsend, self.order = send, zsend, order
        self.rc, self.r1, self.r2, self.rz = recvs
        self.dims = order[:0:-1]
        self.two = len(self.dims) > 1
        self.s, self.z, self.y, self.c = grid.here()
    at = Gather.at
    dev = Gather.dev
    def flips(self, f):
        return ''.join(d for d, on in zip(self.dims, f) if on)
    def idx(self, f, z):
        k = 0
        for on in f:
            k = k * 2 + on
        return k * self.g.depth + z
    def push(self, src, dst, recv, dim):
        pltpu.make_async_remote_copy(src, dst, self.send, recv, device_id=self.dev(dim), device_id_type=MESH).start()
    def wait(self, ref, sem):
        pltpu.make_async_copy(ref, ref, sem).wait()
    def combos(self):
        return [(1, 1), (1, 0), (0, 1), (0, 0)] if self.two else [(1,), (0,)]
    def far(self, d, body):
        @pl.when(self.z + d < self.g.depth)
        def _():
            body(self.z + d, '+')
        @pl.when(self.z >= d)
        def _():
            body(self.z - d, '-')
    def start(self):
        for f in self.combos():
            def go(z, side, f=f):
                k = self.idx(f, z)
                self.push(self.src.at[self.at(self.flips(f) + 'c', z)], self.bufc.at[k], self.rc.at[k], 'c')
            def loop(k, _, go=go):
                self.far(self.g.depth - 1 - k, go)
                return _
            lax.fori_loop(0, self.g.depth - 1, loop, None)
            go(self.z, '')
    def stage1(self, f, d):
        def go(z, side):
            k = self.idx(f, z)
            buf = self.bufc.at[k]
            self.wait(buf, self.rc.at[k])
            buf[...] = (f32(self.src[self.at(self.flips(f), z)]) + f32(buf[...])).astype(buf.dtype)
            j = self.idx(f[1:], z)
            self.push(buf, self.buf1.at[j], self.r1.at[j], self.dims[0])
        self.far(d, go) if d is not None else go(self.z, '')
    def stage2(self, d):
        def go(z, side):
            k, j = self.idx((0, 1), z), self.idx((1,), z)
            bufc, buf = self.bufc.at[k], self.buf1.at[j]
            self.wait(bufc, self.rc.at[k])
            self.wait(buf, self.r1.at[j])
            buf[...] = (f32(self.src[self.at(self.dims[1], z)]) + f32(bufc[...]) + f32(buf[...])).astype(buf.dtype)
            self.push(buf, self.buf2.at[z], self.r2.at[z], self.dims[1])
        self.far(d, go) if d is not None else go(self.z, '')
    def merged(self, z):
        k = self.idx((0,) * len(self.dims), z)
        bufc, buf1 = self.bufc.at[k], self.buf1.at[z]
        self.wait(bufc, self.rc.at[k])
        self.wait(buf1, self.r1.at[z])
        acc = f32(self.src[self.at('', z)]) + f32(bufc[...]) + f32(buf1[...])
        if self.two:
            buf2 = self.buf2.at[z]
            self.wait(buf2, self.r2.at[z])
            acc = acc + f32(buf2[...])
        return acc, bufc
    def chain(self, d):
        top = self.g.depth - 1
        def go(zz, side):
            n = 0 if side == '+' else 1
            more = self.z > 0 if side == '+' else self.z < top
            acc, keep = self.merged(zz)
            keep[...] = acc.astype(keep.dtype)
            buf = self.bufz.at[n, zz]
            @pl.when(more)
            def _():
                self.wait(buf, self.rz.at[n, zz])
                keep[...] = (f32(keep[...]) + f32(buf[...])).astype(keep.dtype)
            pltpu.make_async_remote_copy(keep, buf, self.zsend.at[n, zz], self.rz.at[n, zz], device_id=self.dev(side), device_id_type=MESH).start()
        self.far(d, go)
    def total(self):
        top = self.g.depth - 1
        acc, _ = self.merged(self.z)
        self.out[0] = acc
        for n, ok in ((0, self.z > 0), (1, self.z < top)):
            @pl.when(ok)
            def _(n=n):
                buf = self.bufz.at[n, self.z]
                self.wait(buf, self.rz.at[n, self.z])
                self.out[0] += f32(buf[...])
    def finish(self):
        def sent(k):
            for n, ok in ((0, k > self.z), (1, k < self.z)):
                @pl.when(ok)
                def _(n=n):
                    self.wait(self.bufz.at[n, k], self.zsend.at[n, k])
        each(self.g.depth, sent)
        p = self.g.depth
        n = (4 + 2 + 1) * p if self.two else (2 + 1) * p
        v = self.src.at[pl.ds(0, n)]
        self.wait(v, self.send)

def run_scatters(jobs):
    depth = jobs[0].g.depth
    for job in jobs: job.start()
    def sweep(step, own):
        def loop(k, _):
            for job in jobs: step(job, depth - 1 - k)
            return _
        lax.fori_loop(0, depth - 1, loop, None)
        for job in jobs: own(job)
    def late(j, d):
        j.stage2(d) if j.two else j.chain(d)
    sweep(lambda j, d: j.stage1(j.combos()[0], d), lambda j: j.stage1(j.combos()[0], None))
    sweep(lambda j, d: j.stage1((1, 0), d) if j.two else None, lambda j: j.stage1((1, 0), None) if j.two else None)
    sweep(late, lambda j: j.stage2(None) if j.two else j.total())
    sweep(lambda j, d: j.chain(d) if j.two else None, lambda j: j.total() if j.two else None)
    for job in jobs: job.finish()

def scatter_scratch(grid, shape, dtype, order):
    p = grid.depth
    two = len(order) > 2
    n1, nc = (2 * p, 4 * p) if two else (p, 2 * p)
    D = pltpu.SemaphoreType.DMA
    return [pltpu.VMEM((nc,) + shape, dtype), pltpu.VMEM((n1,) + shape, dtype), pltpu.VMEM((p if two else 1,) + (shape if two else (8, 128)), dtype), pltpu.VMEM((2, p) + shape, dtype),
            D(()), D((2, p)), D((nc,)), D((n1,)), D((p,)), D((2, p))]

def scatter_kernel(grid, orders, *refs):
    m = len(orders)
    ins, outs, rest = refs[:m], refs[m:2 * m], refs[2 * m:]
    greet(grid, any('x' in o for o in orders))
    jobs = []
    for j, order in enumerate(orders):
        r = rest[10 * j:10 * j + 10]
        jobs.append(Scatter(grid, ins[j], outs[j], r[:4], r[4], r[5], r[6:10], order))
    run_scatters(jobs)

def scatter(grid, arrays, orders, name, cid_):
    scratch = []
    for a, o in zip(arrays, orders):
        scratch += scatter_scratch(grid, a.shape[1:], a.dtype, o)
    V = pl.BlockSpec(memory_space=pltpu.VMEM)
    return pl.pallas_call(
        functools.partial(scatter_kernel, grid, tuple(orders)),
        out_shape=[jax.ShapeDtypeStruct((1,) + a.shape[1:], jnp.float32) for a in arrays],
        in_specs=[V] * len(arrays), out_specs=[V] * len(arrays),
        scratch_shapes=scratch,
        compiler_params=pltpu.CompilerParams(collective_id=cid_, has_side_effects=True, vmem_limit_bytes=60 * 2**20),
        name=name,
    )(*arrays)

def pair_stack(x, half):
    lane = lax.broadcasted_iota(jnp.int32, x.shape, 1)
    zero = jnp.zeros_like(x)
    return jnp.concatenate((jnp.where(lane < half, x, zero), jnp.where(lane < half, zero, x)), axis=0)

def pair_join(x, half):
    r = x.shape[0] // 2
    lane = lax.broadcasted_iota(jnp.int32, (r, x.shape[1]), 1)
    return jnp.where(lane < half, x[:r], x[r:])

def nt(a, b):
    return lax.dot_general(a, b, (((1,), (1,)), ((), ())), preferred_element_type=jnp.float32)

def nn(a, b):
    return lax.dot_general(a, b, (((1,), (0,)), ((), ())), preferred_element_type=jnp.float32)

def tn(a, b):
    return lax.dot_general(a, b, (((0,), (0,)), ((), ())), preferred_element_type=jnp.float32)

def as_row(col):
    return jnp.transpose(jnp.broadcast_to(col, (col.shape[0], 128)))[0:1]

MASKED = -1e30

def forward_kernel(half, tiles, len_ref, q_ref, k_ref, v_ref, o_ref, lse_ref, top_ref, sum_ref, acc_ref):
    t = pl.program_id(1)
    q2 = pair_stack(q_ref[...], half)
    s = nt(q2, k_ref[...])
    wide = s.shape[1]
    col = lax.broadcasted_iota(jnp.int32, (1, wide), 1) + t * wide
    s = jnp.where(col < len_ref[0], s, MASKED)
    top = jnp.max(s, axis=1, keepdims=True)
    if tiles > 1:
        old = jnp.where(t == 0, MASKED, top_ref[...])
        top = jnp.maximum(old, top)
    p = jnp.exp(s - top)
    total = jnp.sum(p, axis=1, keepdims=True)
    acc = nn(p.astype(jnp.bfloat16), v_ref[...])
    if tiles > 1:
        factor = jnp.where(t == 0, 0.0, jnp.exp(old - top))
        total = total + jnp.where(t == 0, 0.0, sum_ref[...]) * factor
        acc = acc + jnp.where(t == 0, 0.0, acc_ref[...]) * factor
        top_ref[...], sum_ref[...], acc_ref[...] = top, total, acc
    @pl.when(t == tiles - 1)
    def _():
        o_ref[...] = pair_join(acc / total, half)
        lse_ref[0] = as_row(top + jnp.log(total))

def attend(q, k, v, length, heads, tile):
    rows, width = q.shape
    size = width // heads
    total, pairs = k.shape[0], heads // 2
    tiles = total // tile
    wide = 2 * size
    return pl.pallas_call(
        functools.partial(forward_kernel, size, tiles),
        grid_spec=pltpu.PrefetchScalarGridSpec(
            num_scalar_prefetch=1, grid=(pairs, tiles),
            in_specs=[pl.BlockSpec((rows, wide), lambda p, t, n: (0, p)),
                      pl.BlockSpec((tile, wide), lambda p, t, n: (t, p)),
                      pl.BlockSpec((tile, wide), lambda p, t, n: (t, p))],
            out_specs=[pl.BlockSpec((rows, wide), lambda p, t, n: (0, p)),
                       pl.BlockSpec((1, 1, 2 * rows), lambda p, t, n: (p, 0, 0))],
            scratch_shapes=[pltpu.VMEM((2 * rows, 1), jnp.float32), pltpu.VMEM((2 * rows, 1), jnp.float32), pltpu.VMEM((2 * rows, wide), jnp.float32)]),
        out_shape=[jax.ShapeDtypeStruct((rows, width), jnp.float32), jax.ShapeDtypeStruct((pairs, 1, 2 * rows), jnp.float32)],
        name="attend",
    )(length, q, k, v)

def backward_kernel(half, tiles, scale, len_ref, q_ref, k_ref, v_ref, g_ref, o_ref, lse_ref, dq_ref, dk_ref, dv_ref, acc_ref):
    t = pl.program_id(1)
    q2 = pair_stack(q_ref[...], half)
    g2 = pair_stack(g_ref[...], half)
    k, v = k_ref[...], v_ref[...]
    prod = pair_stack(g_ref[...].astype(jnp.float32) * o_ref[...], half)
    delta = jnp.sum(jnp.transpose(prod), axis=0, keepdims=True)
    s = nt(k, q2)
    row = lax.broadcasted_iota(jnp.int32, (s.shape[0], 1), 0) + t * s.shape[0]
    p = jnp.where(row < len_ref[0], jnp.exp(s - lse_ref[0]), 0.0)
    dp = nt(v, g2)
    ds = (p * (dp - delta)).astype(jnp.bfloat16)
    dk_ref[...] = nn(ds, q2).astype(jnp.bfloat16)
    dv_ref[...] = nn(p.astype(jnp.bfloat16), g2).astype(jnp.bfloat16)
    dq = tn(ds, k)
    if tiles > 1:
        dq = dq + jnp.where(t == 0, 0.0, acc_ref[...])
        acc_ref[...] = dq
    @pl.when(t == tiles - 1)
    def _():
        dq_ref[...] = (pair_join(dq, half) * scale).astype(jnp.bfloat16)

def attend_back(q, k, v, g, o, lse, length, heads, tile):
    rows, width = q.shape
    size = width // heads
    total, pairs = k.shape[0], heads // 2
    tiles = total // tile
    wide = 2 * size
    R = pl.BlockSpec((rows, wide), lambda p, t, n: (0, p))
    K = pl.BlockSpec((tile, wide), lambda p, t, n: (t, p))
    return pl.pallas_call(
        functools.partial(backward_kernel, size, tiles, size ** -0.5),
        grid_spec=pltpu.PrefetchScalarGridSpec(
            num_scalar_prefetch=1, grid=(pairs, tiles),
            in_specs=[R, K, K, R, R, pl.BlockSpec((1, 1, 2 * rows), lambda p, t, n: (p, 0, 0))],
            out_specs=[R, K, K],
            scratch_shapes=[pltpu.VMEM((2 * rows, wide), jnp.float32)]),
        out_shape=[jax.ShapeDtypeStruct((rows, width), jnp.bfloat16)] + [jax.ShapeDtypeStruct((total, width), jnp.bfloat16)] * 2,
        name="attend_back",
    )(length, q, k, v, g, o, lse)
HEADS = 12
EPSILON = 1e-12
ROOM = 52 * 2**20

def normalize(u):
    mean = jnp.mean(u, axis=-1, keepdims=True)
    centred = u - mean
    r = lax.rsqrt(jnp.mean(centred * centred, axis=-1, keepdims=True) + EPSILON)
    return centred * r, r

def normalize_back(e, n, r, gain):
    c = e * gain
    return r * (c - jnp.mean(c, axis=-1, keepdims=True) - n * jnp.mean(c * n, axis=-1, keepdims=True))

def gelu_parts(v):
    cdf = 0.5 * (1.0 + lax.erf(v * (0.5 ** 0.5)))
    slope = cdf + v * jnp.exp(-0.5 * v * v) * ((2 * jnp.pi) ** -0.5)
    return v * cdf, slope

def padded(shape, dtype):
    sub = 32 // jnp.dtype(dtype).itemsize // 1 if False else (8 if jnp.dtype(dtype).itemsize == 4 else 16)
    return math.prod(shape[:-2]) * (-(-shape[-2] // sub) * sub) * (-(-shape[-1] // 128) * 128) * jnp.dtype(dtype).itemsize

def reduce_blocks(grid, arrays, orders, name, cid_):
    need = sum(padded(a.shape, a.dtype) * 3 for a in arrays)
    if need <= ROOM + 20 * 2**20 and grid.depth <= 4:
        return scatter(grid, arrays, orders, name, cid_)
    out = []
    for a, order in zip(arrays, orders):
        axes = ("seq", "ctx") if "x" in order else "ctx"
        out.append(lax.psum_scatter(a.astype(jnp.float32), axes, scatter_dimension=0, tiled=True))
    return out

def per_device(grid, inputs, lengths, cotangent, w_qkv, w_out, w_in, w_back, vectors, ffn_bias):
    bf, f4 = jnp.bfloat16, jnp.float32
    rows_in = inputs[0]
    rows, width = rows_in.shape
    hidden_size = w_in.shape[1]
    devices = grid.seqs * grid.ctx
    part, part_ff = w_qkv.shape[0], w_back.shape[0]
    slots = grid.ctx * rows
    scale = (width // HEADS) ** -0.5

    small = jnp.concatenate((jnp.pad(vectors.T, ((0, 0), (0, 128 - part))), jnp.pad(ffn_bias[None], ((0, 7), (0, 128 - part_ff)))), axis=0)[None]
    half = 3 * width // 2
    qkv_all, small_all = gather(grid, [w_qkv[None], small], [(0, "zyx", pl.ds(0, half)), (0, "zxy", pl.ds(half, half)), (1, "zyx", None)], "gather_qkv", 0)
    qkv_full = qkv_all.reshape(width, 3 * width)
    vec = small_all[:, :8, :part].transpose(1, 0, 2).reshape(8, width).astype(f4)
    ffn_full = small_all[:, 8, :part_ff].reshape(1, hidden_size).astype(f4)

    projected = jnp.dot(rows_in, qkv_full, preferred_element_type=f4)
    query = (projected[:, :width] + vec[0]).astype(bf)
    key = projected[:, width:2 * width].astype(bf)
    value = (projected[:, 2 * width:] + vec[1]).astype(bf)
    key_all, value_all, out_all, in_all, back_all = gather(
        grid, [key[None], value[None], w_out[None], w_in[None], w_back[None]],
        [(0, "zy", None), (1, "zy", None), (2, "zyx", None), (3, "zyx", None), (4, "zyx", None)], "gather_rest", 1)
    key_all, value_all = key_all.reshape(slots, width), value_all.reshape(slots, width)
    out_full, in_full, back_full = out_all.reshape(width, width), in_all.reshape(width, hidden_size), back_all.reshape(hidden_size, width)

    tile = min(slots, 2048)
    query_scaled = query * jnp.asarray(scale, bf)
    attended_f, lse = attend(query_scaled, key_all, value_all, lengths, HEADS, tile)
    attended = attended_f.astype(bf)
    branch = jnp.dot(attended, out_full, preferred_element_type=f4) + vec[2]
    norm_one, r_one = normalize(rows_in.astype(f4) + branch)
    first = norm_one * vec[3] + vec[4]
    first_low = first.astype(bf)
    hidden = jnp.dot(first_low, in_full, preferred_element_type=f4) + ffn_full
    active_f, slope = gelu_parts(hidden)
    active = active_f.astype(bf)
    second = jnp.dot(active, back_full, preferred_element_type=f4) + vec[5]
    norm_two, r_two = normalize(first + second)
    result = (norm_two * vec[6] + vec[7]).astype(bf)
    start = lax.axis_index("ctx") * rows
    valid = (start + jnp.arange(rows, dtype=jnp.int32) < lengths[0]).astype(f4)[:, None]
    grad_result = cotangent[0].astype(f4) * valid
    grad_second = normalize_back(grad_result, norm_two, r_two, vec[6])
    grad_second_low = grad_second.astype(bf)
    grad_active = lax.dot_general(grad_second_low, back_full, (((1,), (1,)), ((), ())), preferred_element_type=f4)
    grad_hidden = (grad_active * slope).astype(bf)
    grad_first = grad_second + lax.dot_general(grad_hidden, in_full, (((1,), (1,)), ((), ())), preferred_element_type=f4)
    grad_branch_full = normalize_back(grad_first, norm_one, r_one, vec[3])
    grad_branch = grad_branch_full.astype(bf)
    grad_attended = lax.dot_general(grad_branch, out_full, (((1,), (1,)), ((), ())), preferred_element_type=f4).astype(bf)

    def outer(a, b):
        return lax.dot_general(a, b, (((0,), (0,)), ((), ())), preferred_element_type=f4).astype(bf)
    g_back = outer(active, grad_second_low).reshape(devices, part_ff, width)
    g_in = outer(first_low, grad_hidden).reshape(devices, part, hidden_size)
    g_out = outer(attended, grad_branch).reshape(devices, part, width)
    grad_query, g_key, g_value = attend_back(query_scaled, key_all, value_all, grad_attended, attended_f, lse, lengths, HEADS, tile)
    own_key, own_value, d_out, d_in, d_back = reduce_blocks(
        grid, [g_key.reshape(grid.ctx, rows, width), g_value.reshape(grid.ctx, rows, width), g_out, g_in, g_back],
        ["zy", "zy", "zyx", "zyx", "zyx"], "reduce_rest", 2)
    grad_projected = jnp.concatenate((grad_query, own_key[0].astype(bf), own_value[0].astype(bf)), axis=1)
    g_qkv = outer(rows_in, grad_projected).reshape(devices, part, 3 * width)
    grad_inputs = grad_branch_full + lax.dot_general(grad_projected, qkv_full, (((1,), (1,)), ((), ())), preferred_element_type=f4)
    sums = jnp.stack((
        jnp.sum(grad_query.astype(f4), axis=0), jnp.sum(own_value[0].astype(bf).astype(f4), axis=0),
        jnp.sum(grad_branch.astype(f4), axis=0), jnp.sum(grad_first * norm_one, axis=0), jnp.sum(grad_first, axis=0),
        jnp.sum(grad_second_low.astype(f4), axis=0), jnp.sum(grad_result * norm_two, axis=0), jnp.sum(grad_result, axis=0)))
    grad_ffn = jnp.sum(grad_hidden.astype(f4), axis=0)
    blocks = jnp.pad(sums.reshape(8, devices, part).transpose(1, 0, 2), ((0, 0), (0, 0), (0, 128 - part)))
    ffn_blocks = jnp.pad(grad_ffn.reshape(devices, 1, part_ff), ((0, 0), (0, 7), (0, 128 - part_ff)))
    g_small = jnp.concatenate((blocks, ffn_blocks), axis=1)
    d_qkv_a, d_qkv_b, d_small = reduce_blocks(grid, [g_qkv[:, :, :half], g_qkv[:, :, half:], g_small], ["zyx", "zxy", "zyx"], "reduce_qkv", 3)
    d_qkv = jnp.concatenate((d_qkv_a[0], d_qkv_b[0]), axis=1)
    return (result[None], grad_inputs[None], d_qkv, d_out[0], d_in[0], d_back[0], d_small[0, :8, :part].T, d_small[0, 8, :part_ff])

def solution(mesh):
    grid = Grid(mesh.shape["seq"], mesh.shape["ctx"])
    split, both = P("seq", "ctx", None), P(("seq", "ctx"), None)
    return jax.shard_map(
        functools.partial(per_device, grid), mesh=mesh,
        in_specs=(split, P("seq"), split, both, both, both, both, both, P(("seq", "ctx"))),
        out_specs=(split, split, both, both, both, both, both, P(("seq", "ctx"))),
        check_vma=False,
    )
```

```python
import functools, math
import jax, jax.numpy as jnp
from jax import lax
from jax.experimental import pallas as pl
from jax.experimental.pallas import tpu as pltpu

MESH = pl.DeviceIdType.MESH

class Grid:
    def __init__(self, seqs, ctx):
        self.seqs, self.ctx = seqs, ctx
        self.depth = ctx // 4
    def here(self):
        s, i = lax.axis_index("seq"), lax.axis_index("ctx")
        return s, i // 4, (i // 2) % 2, i % 2

def cid(z, y, c):
    return (z * 2 + y) * 2 + c

def greet(grid, with_seq):
    s, z, y, c = grid.here()
    bar = pltpu.get_barrier_semaphore()
    def hello(p):
        pl.semaphore_signal(bar, inc=1, device_id=p, device_id_type=MESH)
    peers = [(s, cid(z, 1 - y, c)), (s, cid(z, y, 1 - c))]
    if with_seq:
        peers += [(1 - s, cid(z, y, c))]
    for p in peers:
        hello(p)
    @pl.when(z > 0)
    def _():
        hello((s, cid(z - 1, y, c)))
    @pl.when(z < grid.depth - 1)
    def _():
        hello((s, cid(z + 1, y, c)))
    ends = jnp.where(z > 0, 1, 0) + jnp.where(z < grid.depth - 1, 1, 0)
    pl.semaphore_wait(bar, len(peers) + ends)

def each(n, body):
    if n <= 4:
        for k in range(n):
            body(k)
    else:
        lax.fori_loop(0, n, lambda k, _: (body(k), None)[1], None)

class Gather:
    def __init__(self, grid, src, dst, sems, order, cols=None):
        self.g, self.src, self.dst = grid, src, dst
        self.send, self.zsend, self.recv, self.local = sems
        self.order, self.cols = order, cols
        self.s, self.z, self.y, self.c = grid.here()
        self.rest = order[1:]
    def rows(self, start, n):
        if len(self.dst.shape) == 3:
            return self.dst.at[start] if n is None else self.dst.at[pl.ds(start, n)]
        size = self.src.shape[-2]
        span = pl.ds(pl.multiple_of(start * size, 8), size * (n or 1))
        return self.dst.at[span] if self.cols is None else self.dst.at[span, self.cols]
    def view(self, b):
        return self.rows(b, None)
    def own(self):
        src = self.src.at[0] if len(self.src.shape) == 3 else self.src
        return src if self.cols is None else src.at[:, self.cols]
    def push(self, src, b, dev, sem):
        pltpu.make_async_remote_copy(src, self.view(b), sem, self.recv.at[b], device_id=dev, device_id_type=MESH).start()
    def wait(self, b, sem=None):
        v = self.view(b)
        pltpu.make_async_copy(v, v, self.recv.at[b] if sem is None else sem).wait()
    def dev(self, dim):
        if dim == 'x': return (1 - self.s, cid(self.z, self.y, self.c))
        if dim == 'y': return (self.s, cid(self.z, 1 - self.y, self.c))
        if dim == 'c': return (self.s, cid(self.z, self.y, 1 - self.c))
        return (self.s, cid(self.z + (1 if dim == '+' else -1), self.y, self.c))
    def at(self, flips, z):
        s = 1 - self.s if 'x' in flips else self.s
        y = 1 - self.y if 'y' in flips else self.y
        c = 1 - self.c if 'c' in flips else self.c
        return cid(z, y, c) + (s * self.g.ctx if 'x' in self.order else 0)
    def zpush(self, src, b, z, side):
        ok = self.z < self.g.depth - 1 if side == '+' else self.z > 0
        @pl.when(ok)
        def _():
            self.push(src, b, self.dev(side), self.zsend.at[0 if side == '+' else 1, z])
    def start(self, dims=None):
        own = self.at('', self.z)
        for side in '+-':
            self.zpush(self.own(), own, self.z, side)
        for dim in dims or self.rest + 'c':
            self.push(self.own(), own, self.dev(dim), self.send)
        pltpu.make_async_copy(self.own(), self.view(own), self.local).start()
    def sides(self, d, body):
        if isinstance(d, int) and d == 0:
            body(self.z, '')
            return
        @pl.when(self.z - d >= 0)
        def _():
            body(self.z - d, '-')
        @pl.when(self.z + d < self.g.depth)
        def _():
            body(self.z + d, '+')
    def line(self, d, dims=None):
        def go(z, side):
            b = self.at('', z)
            self.wait(b)
            self.zpush(self.view(b), b, z, '+' if side == '-' else '-')
            for k in dims or self.rest + 'c':
                self.push(self.view(b), b, self.dev(k), self.send)
        self.sides(d, go)
    def late(self, dim, d):
        def go(z, side):
            b = self.at('', z)
            self.push(self.own() if side == '' else self.view(b), b, self.dev(dim), self.send)
        self.sides(d, go)
    def cross(self, flips, dims, d):
        def go(z, side):
            b = self.at(flips, z)
            self.wait(b)
            for k in dims:
                self.push(self.view(b), b, self.dev(k), self.send)
        self.sides(d, go)
    def step(self, t):
        r = self.rest
        if t < self.g.depth:
            self.line(t)
        if 1 <= t <= self.g.depth:
            self.cross(r[0], r[1:] + 'c', t - 1)
        if len(r) > 1:
            if 1 <= t <= self.g.depth:
                self.cross(r[1], 'c', t - 1)
            if 2 <= t <= self.g.depth + 1:
                self.cross(r, 'c', t - 2)
    def steps(self):
        return self.g.depth + len(self.rest)
    def arrive(self):
        r = self.rest
        sets = ['', r[0]] + ([r[1], r] if len(r) > 1 else [])
        for f in sets:
            def go(k, f=f):
                self.wait(self.at(f + 'c', k))
            each(self.g.depth, go)
        self.wait(self.at('', self.z), self.local)
    def leave(self):
        def sent(k):
            for side in '+-':
                n = 0 if side == '+' else 1
                ok = (jnp.logical_and(self.z < self.g.depth - 1, k <= self.z) if side == '+'
                      else jnp.logical_and(self.z > 0, k >= self.z))
                @pl.when(ok)
                def _():
                    self.wait(self.at('', k), self.zsend.at[n, k])
        each(self.g.depth, sent)
        p = self.g.depth
        n = p + (2 * p + 4 * p if len(self.rest) > 1 else 2 * p)
        v = self.rows(0, n)
        pltpu.make_async_copy(v, v, self.send).wait()

PLAN = ("q0", "q1", "q2", "q3", "w0", "q4", "w1", "q5", "qa", "k0", "k1", "w2", "k2", "w3", "k3", "w4", "k4", "w5")

def fetch_kernel(grid, scale, *refs):
    x, w_qkv, vec, w_bias, w_out, w_in, w_back = refs[:7]
    qkv_all, vec_all, bias_all, out_all, in_all, back_all, key_all, value_all, query = refs[7:16]
    key, value = refs[16:18]
    sems = refs[18:]
    greet(grid, True)
    def job(i, src, dst, order, cols=None):
        return Gather(grid, src, dst, [r.at[i] for r in sems], order, cols)
    width = x.shape[1]
    half = 3 * width // 2
    parts = {
        "q": [job(0, vec, vec_all, "zyx"), job(1, w_qkv, qkv_all, "zyx", pl.ds(0, half)), job(2, w_qkv, qkv_all, "zxy", pl.ds(half, half))],
        "w": [job(3, w_bias, bias_all, "zyx"), job(4, w_out, out_all, "zyx"), job(5, w_in, in_all, "zyx"), job(6, w_back, back_all, "zyx")],
        "k": [job(7, key, key_all, "zy"), job(8, value, value_all, "zy")]}
    for word in PLAN:
        jobs, t = parts[word[0]], word[1]
        for j in jobs:
            if t == "a": j.arrive()
            elif t == "s": j.start("xc")
            elif t == "l": j.line(int(word[2]), "xc")
            elif t == "y": j.late("y", int(word[2]))
            elif t == "b": j.cross("y", "xc", int(word[2]))
            elif t == "x": j.cross("x", "c", int(word[2]))
            elif t == "z": j.cross("yx", "c", int(word[2]))
            elif t == "0": j.start()
            else: j.step(int(t))
        if word == "qa":
            lane = lax.broadcasted_iota(jnp.int32, (16, 128), 1)
            pick = (lane == lax.broadcasted_iota(jnp.int32, (16, 128), 0)).astype(jnp.bfloat16)
            rows = nt(pick, vec_all[...])
            key[...] = nn(x[...], qkv_all[:, width:2 * width]).astype(jnp.bfloat16)
            value[...] = (nn(x[...], qkv_all[:, 2 * width:]) + rows[1:2]).astype(jnp.bfloat16)
    q = (nn(x[...], qkv_all[:, :width]) + rows[0:1]).astype(jnp.bfloat16)
    query[...] = q * jnp.asarray(scale, jnp.bfloat16)
    for j in parts["k"] + parts["w"]:
        j.arrive()
    for j in parts["q"] + parts["k"] + parts["w"]:
        j.leave()

def fetch(grid, x, w_qkv, vec, w_bias, w_out, w_in, w_back, scale):
    devices, bf = grid.seqs * grid.ctx, jnp.bfloat16
    rows, width = x.shape
    S = jax.ShapeDtypeStruct
    V, A = pl.BlockSpec(memory_space=pltpu.VMEM), pl.BlockSpec(memory_space=pl.ANY)
    D = pltpu.SemaphoreType.DMA
    flat = lambda a: S((devices * a.shape[-2], a.shape[-1]), bf)
    deep = lambda a: S((devices,) + a.shape[1:], bf)
    kv = S((grid.ctx * rows, width), bf)
    return pl.pallas_call(
        functools.partial(fetch_kernel, grid, scale),
        out_shape=[flat(w_qkv), flat(vec), deep(w_bias), deep(w_out), deep(w_in), deep(w_back), kv, kv, S((rows, width), bf)],
        in_specs=[V] * 7,
        out_specs=[V, V] + [A] * 6 + [V],
        scratch_shapes=[pltpu.VMEM((rows, width), bf)] * 2 + [D((9,)), D((9, 2, grid.depth)), D((9, devices)), D((9,))],
        compiler_params=pltpu.CompilerParams(collective_id=0, has_side_effects=True, vmem_limit_bytes=60 * 2**20),
        name="fetch",
    )(x, w_qkv, vec, w_bias, w_out, w_in, w_back)
from jax.sharding import PartitionSpec as P

def f32(x):
    return x.astype(jnp.float32)

class Scatter:
    def __init__(self, grid, src, out, bufs, send, zsend, recvs, order, mine=None, local=None):
        self.g, self.src, self.out, self.mine, self.local = grid, src, out, mine, local
        self.bufc, self.buf1, self.buf2, self.bufz = bufs
        self.send, self.zsend, self.order = send, zsend, order
        self.rc, self.r1, self.r2, self.rz = recvs
        self.dims = order[:0:-1]
        self.two = len(self.dims) > 1
        self.s, self.z, self.y, self.c = grid.here()
    at = Gather.at
    dev = Gather.dev
    def flips(self, f):
        return ''.join(d for d, on in zip(self.dims, f) if on)
    def idx(self, f, z):
        k = 0
        for on in f:
            k = k * 2 + on
        return k * self.g.depth + z
    def push(self, src, dst, recv, dim):
        pltpu.make_async_remote_copy(src, dst, self.send, recv, device_id=self.dev(dim), device_id_type=MESH).start()
    def wait(self, ref, sem):
        pltpu.make_async_copy(ref, ref, sem).wait()
    def combos(self):
        return [(1, 1), (1, 0), (0, 1), (0, 0)] if self.two else [(1,), (0,)]
    def far(self, d, body):
        @pl.when(self.z + d < self.g.depth)
        def _():
            body(self.z + d, '+')
        @pl.when(self.z >= d)
        def _():
            body(self.z - d, '-')
    def own(self, f, z):
        return self.src[self.at(self.flips(f), z)] if self.mine is None else self.mine[self.idx(f, z)]
    def load(self):
        for f in self.combos():
            def go(z, f=f):
                pltpu.make_async_copy(self.src.at[self.at(self.flips(f), z)], self.mine.at[self.idx(f, z)], self.local).start()
            each(self.g.depth, go)
    def loaded(self):
        pltpu.make_async_copy(self.mine, self.mine, self.local).wait()
    def start(self):
        for f in self.combos():
            def go(z, side, f=f):
                k = self.idx(f, z)
                self.push(self.src.at[self.at(self.flips(f) + 'c', z)], self.bufc.at[k], self.rc.at[k], 'c')
            def loop(k, _, go=go):
                self.far(self.g.depth - 1 - k, go)
                return _
            lax.fori_loop(0, self.g.depth - 1, loop, None)
            go(self.z, '')
    def stage1(self, f, d):
        def go(z, side):
            k = self.idx(f, z)
            buf = self.bufc.at[k]
            self.wait(buf, self.rc.at[k])
            buf[...] = (f32(self.own(f, z)) + f32(buf[...])).astype(buf.dtype)
            j = self.idx(f[1:], z)
            self.push(buf, self.buf1.at[j], self.r1.at[j], self.dims[0])
        self.far(d, go) if d is not None else go(self.z, '')
    def stage2(self, d):
        def go(z, side):
            k, j = self.idx((0, 1), z), self.idx((1,), z)
            bufc, buf = self.bufc.at[k], self.buf1.at[j]
            self.wait(bufc, self.rc.at[k])
            self.wait(buf, self.r1.at[j])
            buf[...] = (f32(self.own((0, 1), z)) + f32(bufc[...]) + f32(buf[...])).astype(buf.dtype)
            self.push(buf, self.buf2.at[z], self.r2.at[z], self.dims[1])
        self.far(d, go) if d is not None else go(self.z, '')
    def merged(self, z):
        k = self.idx((0,) * len(self.dims), z)
        bufc, buf1 = self.bufc.at[k], self.buf1.at[z]
        self.wait(bufc, self.rc.at[k])
        self.wait(buf1, self.r1.at[z])
        acc = f32(self.own((0,) * len(self.dims), z)) + f32(bufc[...]) + f32(buf1[...])
        if self.two:
            buf2 = self.buf2.at[z]
            self.wait(buf2, self.r2.at[z])
            acc = acc + f32(buf2[...])
        return acc, bufc
    def chain(self, d):
        top = self.g.depth - 1
        def go(zz, side):
            n = 0 if side == '+' else 1
            more = self.z > 0 if side == '+' else self.z < top
            acc, keep = self.merged(zz)
            keep[...] = acc.astype(keep.dtype)
            buf = self.bufz.at[n, zz]
            @pl.when(more)
            def _():
                self.wait(buf, self.rz.at[n, zz])
                keep[...] = (f32(keep[...]) + f32(buf[...])).astype(keep.dtype)
            pltpu.make_async_remote_copy(keep, buf, self.zsend.at[n, zz], self.rz.at[n, zz], device_id=self.dev(side), device_id_type=MESH).start()
        self.far(d, go)
    def total(self):
        top = self.g.depth - 1
        acc, _ = self.merged(self.z)
        self.out[0] = acc
        for n, ok in ((0, self.z > 0), (1, self.z < top)):
            @pl.when(ok)
            def _(n=n):
                buf = self.bufz.at[n, self.z]
                self.wait(buf, self.rz.at[n, self.z])
                self.out[0] += f32(buf[...])
    def finish(self):
        def sent(k):
            for n, ok in ((0, k > self.z), (1, k < self.z)):
                @pl.when(ok)
                def _(n=n):
                    self.wait(self.bufz.at[n, k], self.zsend.at[n, k])
        each(self.g.depth, sent)
        p = self.g.depth
        n = (4 + 2 + 1) * p if self.two else (2 + 1) * p
        v = self.src.at[pl.ds(0, n)]
        self.wait(v, self.send)

def scatter_scratch(grid, shape, dtype, order):
    p = grid.depth
    two = len(order) > 2
    n1, nc = (2 * p, 4 * p) if two else (p, 2 * p)
    D = pltpu.SemaphoreType.DMA
    return [pltpu.VMEM((nc,) + shape, dtype), pltpu.VMEM((n1,) + shape, dtype), pltpu.VMEM((p if two else 1,) + (shape if two else (8, 128)), dtype), pltpu.VMEM((2, p) + shape, dtype),
            D(()), D((2, p)), D((nc,)), D((n1,)), D((p,)), D((2, p))]

def pair_stack(x, half):
    lane = lax.broadcasted_iota(jnp.int32, x.shape, 1)
    zero = jnp.zeros_like(x)
    return jnp.concatenate((jnp.where(lane < half, x, zero), jnp.where(lane < half, zero, x)), axis=0)

def pair_join(x, half):
    r = x.shape[0] // 2
    lane = lax.broadcasted_iota(jnp.int32, (r, x.shape[1]), 1)
    return jnp.where(lane < half, x[:r], x[r:])

def nt(a, b):
    return lax.dot_general(a, b, (((1,), (1,)), ((), ())), preferred_element_type=jnp.float32)

def nn(a, b):
    return lax.dot_general(a, b, (((1,), (0,)), ((), ())), preferred_element_type=jnp.float32)

def tn(a, b):
    return lax.dot_general(a, b, (((0,), (0,)), ((), ())), preferred_element_type=jnp.float32)

def as_row(col):
    return jnp.transpose(jnp.broadcast_to(col, (col.shape[0], 128)))[0:1]

MASKED = -1e30

def forward_kernel(half, tiles, len_ref, q_ref, k_ref, v_ref, o_ref, lse_ref, top_ref, sum_ref, acc_ref):
    t = pl.program_id(1)
    q2 = pair_stack(q_ref[...], half)
    s = nt(q2, k_ref[...])
    wide = s.shape[1]
    col = lax.broadcasted_iota(jnp.int32, (1, wide), 1) + t * wide
    s = jnp.where(col < len_ref[0], s, MASKED)
    top = jnp.max(s, axis=1, keepdims=True)
    if tiles > 1:
        old = jnp.where(t == 0, MASKED, top_ref[...])
        top = jnp.maximum(old, top)
    p = jnp.exp(s - top)
    total = jnp.sum(p, axis=1, keepdims=True)
    acc = nn(p.astype(jnp.bfloat16), v_ref[...])
    if tiles > 1:
        factor = jnp.where(t == 0, 0.0, jnp.exp(old - top))
        total = total + jnp.where(t == 0, 0.0, sum_ref[...]) * factor
        acc = acc + jnp.where(t == 0, 0.0, acc_ref[...]) * factor
        top_ref[...], sum_ref[...], acc_ref[...] = top, total, acc
    @pl.when(t == tiles - 1)
    def _():
        o_ref[...] = pair_join(acc / total, half)
        lse_ref[0] = as_row(top + jnp.log(total))

def attend(q, k, v, length, heads, tile):
    rows, width = q.shape
    size = width // heads
    total, pairs = k.shape[0], heads // 2
    tiles = total // tile
    wide = 2 * size
    return pl.pallas_call(
        functools.partial(forward_kernel, size, tiles),
        grid_spec=pltpu.PrefetchScalarGridSpec(
            num_scalar_prefetch=1, grid=(pairs, tiles),
            in_specs=[pl.BlockSpec((rows, wide), lambda p, t, n: (0, p)),
                      pl.BlockSpec((tile, wide), lambda p, t, n: (t, p)),
                      pl.BlockSpec((tile, wide), lambda p, t, n: (t, p))],
            out_specs=[pl.BlockSpec((rows, wide), lambda p, t, n: (0, p)),
                       pl.BlockSpec((1, 1, 2 * rows), lambda p, t, n: (p, 0, 0))],
            scratch_shapes=[pltpu.VMEM((2 * rows, 1), jnp.float32), pltpu.VMEM((2 * rows, 1), jnp.float32), pltpu.VMEM((2 * rows, wide), jnp.float32)]),
        out_shape=[jax.ShapeDtypeStruct((rows, width), jnp.float32), jax.ShapeDtypeStruct((pairs, 1, 2 * rows), jnp.float32)],
        name="attend",
    )(length, q, k, v)

def backward_math(half, length, start, q, k, v, g, o, lse):
    q2, g2 = pair_stack(q, half), pair_stack(g, half)
    delta = jnp.sum(jnp.transpose(pair_stack(f32(g) * o, half)), axis=0, keepdims=True)
    s = nt(k, q2)
    row = lax.broadcasted_iota(jnp.int32, (s.shape[0], 1), 0) + start
    p = jnp.where(row < length, jnp.exp(s - lse), 0.0)
    ds = (p * (nt(v, g2) - delta)).astype(jnp.bfloat16)
    return tn(ds, k), nn(ds, q2), nn(p.astype(jnp.bfloat16), g2)

def backward_kernel(half, tiles, scale, len_ref, q_ref, k_ref, v_ref, g_ref, o_ref, lse_ref, dq_ref, dk_ref, dv_ref, sum_ref, acc_ref):
    t = pl.program_id(1)
    dq, dk, dv = backward_math(half, len_ref[0], t * k_ref.shape[0], q_ref[...], k_ref[...], v_ref[...], g_ref[...], o_ref[...], lse_ref[0])
    dk_ref[...] = dk.astype(jnp.bfloat16)
    dv_ref[...] = dv.astype(jnp.bfloat16)
    sums = jnp.sum(dv, axis=0, keepdims=True)
    sum_ref[0] = sums + jnp.where(t == 0, 0.0, sum_ref[0]) if tiles > 1 else sums
    if tiles > 1:
        dq = dq + jnp.where(t == 0, 0.0, acc_ref[...])
        acc_ref[...] = dq
    @pl.when(t == tiles - 1)
    def _():
        dq_ref[...] = (pair_join(dq, half) * scale).astype(jnp.bfloat16)

def attend_back(q, k, v, g, o, lse, length, heads, tile):
    rows, width = q.shape
    size = width // heads
    total, pairs = k.shape[0], heads // 2
    tiles = total // tile
    wide = 2 * size
    R = pl.BlockSpec((rows, wide), lambda p, t, n: (0, p))
    K = pl.BlockSpec((tile, wide), lambda p, t, n: (t, p))
    return pl.pallas_call(
        functools.partial(backward_kernel, size, tiles, size ** -0.5),
        grid_spec=pltpu.PrefetchScalarGridSpec(
            num_scalar_prefetch=1, grid=(pairs, tiles),
            in_specs=[R, K, K, R, R, pl.BlockSpec((1, 1, 2 * rows), lambda p, t, n: (p, 0, 0))],
            out_specs=[R, K, K, pl.BlockSpec((1, 1, wide), lambda p, t, n: (p, 0, 0))],
            scratch_shapes=[pltpu.VMEM((2 * rows, wide), jnp.float32)]),
        out_shape=[jax.ShapeDtypeStruct((rows, width), jnp.bfloat16)] + [jax.ShapeDtypeStruct((total, width), jnp.bfloat16)] * 2 + [jax.ShapeDtypeStruct((pairs, 1, wide), jnp.float32)],
        name="attend_back",
    )(length, q, k, v, g, o, lse)
ORDER = ("ds", "pA", "ld", "d1,*", "As", "A1,*", "pB", "Bs", "B1,*", "d2,*", "e", "A4,*", "B4,d3,*", "g", "qs", "q1,*", "q2,*", "d4,*", "i", "q3,*", "q4,*")

def settle_kernel(grid, size, *refs):
    length, key_all, value_all, g_out, g_in, g_back, w_qkv, q, g, o, lse, x, base, g_bias, g_vec = refs[:15]
    d_qkv, d_out, d_in, d_back, d_bias, d_vec, grad_inputs = refs[15:22]
    own_key, own_value, w_query, w_key, w_value, grads, k_slots, v_slots, wide_w, vec_cols, vec_src, kA, vA, kB, vB = refs[22:37]
    kv_sem, w_sem, local = refs[37:40]
    mine = refs[40:43]
    bufs = refs[43:]
    rows, width = x.shape
    third, pair, pairs = width // 2, 2 * size, width // (2 * size)
    def pull(p):
        at = pl.multiple_of(p * pair, pair)
        return [pltpu.make_async_copy(src.at[:, pl.ds(at, pair)], slots.at[lax.rem(p, 2)], kv_sem.at[n, lax.rem(p, 2)])
                for n, (src, slots) in enumerate(((key_all, k_slots), (value_all, v_slots)))]
    for copy in pull(0): copy.start()
    greet(grid, True)
    cut = lambda n: d_qkv.at[:, :, pl.ds(n * width, width)]
    part_of = lambda ref, n: ref.at[:, :, pl.ds(n * third, third)]
    specs = [("A", vA, part_of(own_value, 0), "zy"), ("A", kA, part_of(own_key, 0), "zy"), ("B", vB, part_of(own_value, 1), "zy"), ("B", kB, part_of(own_key, 1), "zy"),
             ("d", g_back, d_back, "zyx"), ("d", g_in, d_in, "zyx"), ("d", g_out, d_out, "zyx"), ("d", g_bias, d_bias, "zyx"),
             ("q", vec_src, d_vec, "zyx"), ("q", w_query, cut(0), "zyx"), ("q", w_key, cut(1), "zyx"), ("q", w_value, cut(2), "zxy")]
    jobs = {"A": [], "B": [], "d": [], "q": []}
    for n, (group, src, out, order) in enumerate(specs):
        r = bufs[10 * n:10 * n + 10]
        extra = (mine[n - 4], local.at[n - 4]) if 4 <= n < 7 else ()
        jobs[group].append(Scatter(grid, src, out, r[:4], r[4], r[5], r[6:10], order, *extra))
    big = jobs["d"][:3]
    def weigh(at, dst):
        part, wide = dst.shape[1], width // 2
        for n in range(2):
            full = tn(x[...], grads[:, at + n * wide:at + (n + 1) * wide])
            for k in range(dst.shape[0]):
                dst[k, :, n * wide:(n + 1) * wide] = full[k * part:(k + 1) * part].astype(dst.dtype)
    lane = lax.broadcasted_iota(jnp.int32, (pair, 128), 1)
    def attention(first, dk, dv):
        def one(j, _):
            p = first + j
            slot = lax.rem(p, 2)
            @pl.when(p + 1 < pairs)
            def _():
                for copy in pull(p + 1): copy.start()
            for copy in pull(p): copy.wait()
            at = pl.ds(pl.multiple_of(p * pair, pair), pair)
            to = pl.ds(pl.multiple_of(j * pair, pair), pair)
            dq, dk_part, dv_part = backward_math(size, length[0], 0, q[:, at], k_slots[slot], v_slots[slot], g[:, at], o[:, at], lse[p])
            dk[:, :, to] = dk_part.astype(dk.dtype).reshape(dk.shape[0], rows, pair)
            dv[:, :, to] = dv_part.astype(dv.dtype).reshape(dv.shape[0], rows, pair)
            dq = (pair_join(dq, size) * size ** -0.5).astype(grads.dtype)
            grads[:, at] = dq
            tall = lambda v: jnp.transpose(jnp.broadcast_to(jnp.sum(f32(v), axis=0, keepdims=True), (128, pair)))
            vec_cols[at, :] = jnp.where(lane == 0, tall(dq), jnp.where(lane == 1, tall(dv_part), g_vec[at, :]))
            return _
        lax.fori_loop(0, pairs // 2, one, None)
    def early():
        weigh(0, w_query)
        part = vec_src.shape[1]
        for k in range(vec_src.shape[0]):
            vec_src[k] = vec_cols[k * part:(k + 1) * part]
    def after():
        grads[:, width:2 * width] = own_key[0].astype(grads.dtype)
        grads[:, 2 * width:] = own_value[0].astype(grads.dtype)
        weigh(width, w_key)
        weigh(2 * width, w_value)
    def inward():
        total = base[...]
        for n in range(3):
            copy = pltpu.make_async_copy(w_qkv.at[:, pl.ds(n * width, width)], wide_w, w_sem)
            copy.start()
            copy.wait()
            total = total + nt(grads[:, n * width:(n + 1) * width], wide_w[...])
        grad_inputs[...] = total
    alone = {"pA": lambda: attention(0, kA, vA), "pB": lambda: attention(pairs // 2, kB, vB), "e": early, "g": after, "i": inward,
             "ld": lambda: [job.loaded() for job in big]}
    def step(word, d):
        for job in jobs[word[0]]:
            if word[1] == "s":
                if job.mine is not None: job.load()
                job.start()
            elif word[1] == "1": job.stage1(job.combos()[0], d)
            elif word[1] == "2": job.stage1((1, 0), d)
            elif word[1] == "3": job.stage2(d)
            elif d is None: job.total()
            else: job.chain(d)
    for phase in ORDER:
        words = phase.split(",")
        if phase in alone: alone[phase]()
        elif words[-1] == "*":
            def loop(k, _, words=words):
                for word in words[:-1]: step(word, grid.depth - 1 - k)
                return _
            lax.fori_loop(0, grid.depth - 1, loop, None)
            for word in words[:-1]: step(word, None)
        else:
            for word in words: step(word, None)
    for group in [n for n in "ABdq" if n + "s" in ORDER]:
        for job in jobs[group]: job.finish()

def settle(grid, size, length, key_all, value_all, g_out, g_in, g_back, w_qkv, q, g, o, lse, x, base, g_bias, g_vec):
    bf, f4 = jnp.bfloat16, jnp.float32
    rows, width = x.shape
    part, devices = g_out.shape[1], grid.seqs * grid.ctx
    slots, pair = key_all.shape[0], 2 * size
    S = jax.ShapeDtypeStruct
    V, A = pl.BlockSpec(memory_space=pltpu.VMEM), pl.BlockSpec(memory_space=pl.ANY)
    D, M = pltpu.SemaphoreType.DMA, pltpu.VMEM
    scratch = [M((1, rows, width), f4)] * 2 + [M((devices, part, width), bf)] * 3 + [M((rows, 3 * width), bf)] + [M((2, slots, pair), bf)] * 2
    scratch += [M((width, width), bf), M((width, 128), f4), M((devices, part, 128), f4)] + [M((grid.ctx, rows, width // 2), bf)] * 4
    scratch += [D((2, 2)), D(()), D((3,))] + [M((devices // 2,) + a.shape[1:], bf) for a in (g_back, g_in, g_out)]
    for shape, dtype, order in ([((rows, width // 2), bf, "zy")] * 4 + [(a.shape[1:], a.dtype, "zyx") for a in (g_back, g_in, g_out, g_bias)]
                                + [((part, 128), f4, "zyx"), ((part, width), bf, "zyx"), ((part, width), bf, "zyx"), ((part, width), bf, "zxy")]):
        scratch += scatter_scratch(grid, shape, dtype, order)
    one = lambda a: S((1,) + a.shape[1:], f4)
    return pl.pallas_call(
        functools.partial(settle_kernel, grid, size),
        out_shape=[S((1, part, 3 * width), f4), one(g_out), one(g_in), one(g_back), one(g_bias), S((1, part, 128), f4), S((rows, width), f4)],
        in_specs=[pl.BlockSpec(memory_space=pltpu.SMEM)] + [A] * 6 + [V] * 8, out_specs=[V] * 7, scratch_shapes=scratch,
        compiler_params=pltpu.CompilerParams(collective_id=1, has_side_effects=True, vmem_limit_bytes=63 * 2**20),
        name="settle",
    )(length, key_all, value_all, g_out, g_in, g_back, w_qkv, q, g, o, lse, x, base, g_bias, g_vec)

HEADS = 12
EPSILON = 1e-12

def normalize(u):
    mean = jnp.mean(u, axis=-1, keepdims=True)
    centred = u - mean
    r = lax.rsqrt(jnp.mean(centred * centred, axis=-1, keepdims=True) + EPSILON)
    return centred * r, r

def normalize_back(e, n, r, gain):
    c = e * gain
    return r * (c - jnp.mean(c, axis=-1, keepdims=True) - n * jnp.mean(c * n, axis=-1, keepdims=True))

def gelu_parts(v):
    cdf = 0.5 * (1.0 + lax.erf(v * (0.5 ** 0.5)))
    slope = cdf + v * jnp.exp(-0.5 * v * v) * ((2 * jnp.pi) ** -0.5)
    return v * cdf, slope

def per_device(grid, inputs, lengths, cotangent, w_qkv, w_out, w_in, w_back, vectors, ffn_bias):
    bf, f4 = jnp.bfloat16, jnp.float32
    rows_in = inputs[0]
    rows, width = rows_in.shape
    hidden_size = w_in.shape[1]
    devices = grid.seqs * grid.ctx
    part, part_ff = w_qkv.shape[0], w_back.shape[0]
    slots = grid.ctx * rows
    scale = (width // HEADS) ** -0.5

    half = 3 * width // 2
    whole = grid.depth <= 4 and part % 8 == 0 and part_ff <= 128
    if whole:
        vec_block = jnp.pad(vectors, ((0, 0), (0, 120)))
        bias_block = jnp.pad(ffn_bias[None], ((0, 7), (0, 128 - part_ff)))[None]
        qkv_full, vec_all, bias_all, out_all, in_all, back_all, key_all, value_all, query_scaled = fetch(
            grid, rows_in, w_qkv, vec_block, bias_block, w_out[None], w_in[None], w_back[None], scale)
        vec = vec_all[:, :8].T.astype(f4)
        ffn_full = bias_all[:, 0, :part_ff].reshape(1, hidden_size).astype(f4)
        out_full, in_full, back_full = out_all.reshape(width, width), in_all.reshape(width, hidden_size), back_all.reshape(hidden_size, width)
    else:
        everywhere = lambda a: lax.all_gather(a, ("seq", "ctx"), axis=0, tiled=True)
        qkv_full, out_full, in_full, back_full = everywhere(w_qkv), everywhere(w_out), everywhere(w_in), everywhere(w_back)
        vec = everywhere(vectors).T.astype(f4)
        ffn_full = everywhere(ffn_bias)[None].astype(f4)
        projected = jnp.dot(rows_in, qkv_full, preferred_element_type=f4)
        query_scaled = (projected[:, :width] + vec[0]).astype(bf) * jnp.asarray(scale, bf)
        key = projected[:, width:2 * width].astype(bf)
        value = (projected[:, 2 * width:] + vec[1]).astype(bf)
        key_all, value_all = (lax.all_gather(a, "ctx", axis=0, tiled=True) for a in (key, value))

    tile = min(slots, 2048)
    attended_f, lse = attend(query_scaled, key_all, value_all, lengths, HEADS, tile)
    attended = attended_f.astype(bf)
    branch = jnp.dot(attended, out_full, preferred_element_type=f4) + vec[2]
    norm_one, r_one = normalize(rows_in.astype(f4) + branch)
    first = norm_one * vec[3] + vec[4]
    first_low = first.astype(bf)
    hidden = jnp.dot(first_low, in_full, preferred_element_type=f4) + ffn_full
    active_f, slope = gelu_parts(hidden)
    active = active_f.astype(bf)
    second = jnp.dot(active, back_full, preferred_element_type=f4) + vec[5]
    norm_two, r_two = normalize(first + second)
    result = (norm_two * vec[6] + vec[7]).astype(bf)
    start = lax.axis_index("ctx") * rows
    valid = (start + jnp.arange(rows, dtype=jnp.int32) < lengths[0]).astype(f4)[:, None]
    grad_result = cotangent[0].astype(f4) * valid
    grad_second = normalize_back(grad_result, norm_two, r_two, vec[6])
    grad_second_low = grad_second.astype(bf)
    grad_active = lax.dot_general(grad_second_low, back_full, (((1,), (1,)), ((), ())), preferred_element_type=f4)
    grad_hidden = (grad_active * slope).astype(bf)
    grad_first = grad_second + lax.dot_general(grad_hidden, in_full, (((1,), (1,)), ((), ())), preferred_element_type=f4)
    grad_branch_full = normalize_back(grad_first, norm_one, r_one, vec[3])
    grad_branch = grad_branch_full.astype(bf)
    grad_attended = lax.dot_general(grad_branch, out_full, (((1,), (1,)), ((), ())), preferred_element_type=f4).astype(bf)

    def outer(a, b):
        return lax.dot_general(a, b, (((0,), (0,)), ((), ())), preferred_element_type=f4).astype(bf)
    g_back = outer(active, grad_second_low)
    g_in = outer(first_low, grad_hidden)
    g_out = outer(attended, grad_branch)
    grad_ffn = jnp.sum(grad_hidden.astype(f4), axis=0)
    sums = (jnp.sum(grad_branch.astype(f4), axis=0), jnp.sum(grad_first * norm_one, axis=0), jnp.sum(grad_first, axis=0),
            jnp.sum(grad_second_low.astype(f4), axis=0), jnp.sum(grad_result * norm_two, axis=0), jnp.sum(grad_result, axis=0))
    if whole:
        g_vec = jnp.pad(jnp.stack(sums).T, ((0, 0), (2, 120)))
        g_bias = jnp.pad(grad_ffn.reshape(devices, 1, part_ff), ((0, 0), (0, 7), (0, 128 - part_ff)))
        d_qkv, d_out, d_in, d_back, d_bias, d_vec, grad_inputs = settle(
            grid, width // HEADS, lengths, key_all, value_all, g_out.reshape(devices, part, width), g_in.reshape(devices, part, hidden_size),
            g_back.reshape(devices, part_ff, width), qkv_full, query_scaled, grad_attended, attended_f, lse, rows_in, grad_branch_full, g_bias, g_vec)
        return (result[None], grad_inputs[None], d_qkv[0], d_out[0], d_in[0], d_back[0], d_vec[0, :, :8], d_bias[0, 0, :part_ff])
    grad_query, g_key, g_value, sum_value = attend_back(query_scaled, key_all, value_all, grad_attended, attended_f, lse, lengths, HEADS, tile)
    sums = jnp.stack((jnp.sum(grad_query.astype(f4), axis=0), sum_value.reshape(width)) + sums)
    home = lambda a, axes: lax.psum_scatter(a.astype(f4), axes, scatter_dimension=0, tiled=True)
    own_key, own_value = (home(a, "ctx").astype(bf) for a in (g_key, g_value))
    grad_projected = jnp.concatenate((grad_query, own_key, own_value), axis=1)
    grad_inputs = grad_branch_full + lax.dot_general(grad_projected, qkv_full, (((1,), (1,)), ((), ())), preferred_element_type=f4)
    both = ("seq", "ctx")
    return (result[None], grad_inputs[None], home(outer(rows_in, grad_projected), both), home(g_out, both), home(g_in, both), home(g_back, both),
            home(sums.T, both), home(grad_ffn, both))

def solution(mesh):
    grid = Grid(mesh.shape["seq"], mesh.shape["ctx"])
    split, both = P("seq", "ctx", None), P(("seq", "ctx"), None)
    return jax.shard_map(
        functools.partial(per_device, grid), mesh=mesh,
        in_specs=(split, P("seq"), split, both, both, both, both, both, P(("seq", "ctx"))),
        out_specs=(split, split, both, both, both, both, both, P(("seq", "ctx"))),
        check_vma=False,
    )
```

```python
import functools, math
import jax, jax.numpy as jnp
from jax import lax
from jax.experimental import pallas as pl
from jax.experimental.pallas import tpu as pltpu

MESH = pl.DeviceIdType.MESH

class Grid:
    def __init__(self, seqs, ctx):
        self.seqs, self.ctx = seqs, ctx
        self.depth = ctx // 4
    def here(self):
        s, i = lax.axis_index("seq"), lax.axis_index("ctx")
        return s, i // 4, (i // 2) % 2, i % 2

def cid(z, y, c):
    return (z * 2 + y) * 2 + c

def greet(grid, with_seq):
    s, z, y, c = grid.here()
    bar = pltpu.get_barrier_semaphore()
    def hello(p):
        pl.semaphore_signal(bar, inc=1, device_id=p, device_id_type=MESH)
    peers = [(s, cid(z, 1 - y, c)), (s, cid(z, y, 1 - c))]
    if with_seq:
        peers += [(1 - s, cid(z, y, c))]
    for p in peers:
        hello(p)
    @pl.when(z > 0)
    def _():
        hello((s, cid(z - 1, y, c)))
    @pl.when(z < grid.depth - 1)
    def _():
        hello((s, cid(z + 1, y, c)))
    ends = jnp.where(z > 0, 1, 0) + jnp.where(z < grid.depth - 1, 1, 0)
    pl.semaphore_wait(bar, len(peers) + ends)

def each(n, body):
    if n <= 4:
        for k in range(n):
            body(k)
    else:
        lax.fori_loop(0, n, lambda k, _: (body(k), None)[1], None)

class Gather:
    def __init__(self, grid, src, dst, sems, order, cols=None):
        self.g, self.src, self.dst = grid, src, dst
        self.send, self.zsend, self.recv, self.local = sems
        self.order, self.cols = order, cols
        self.s, self.z, self.y, self.c = grid.here()
        self.rest = order[1:]
    def rows(self, start, n):
        if len(self.dst.shape) == 3:
            return self.dst.at[start] if n is None else self.dst.at[pl.ds(start, n)]
        size = self.src.shape[-2]
        span = pl.ds(pl.multiple_of(start * size, 8), size * (n or 1))
        return self.dst.at[span] if self.cols is None else self.dst.at[span, self.cols]
    def view(self, b):
        return self.rows(b, None)
    def own(self):
        src = self.src.at[0] if len(self.src.shape) == 3 else self.src
        return src if self.cols is None else src.at[:, self.cols]
    def push(self, src, b, dev, sem):
        pltpu.make_async_remote_copy(src, self.view(b), sem, self.recv.at[b], device_id=dev, device_id_type=MESH).start()
    def wait(self, b, sem=None):
        v = self.view(b)
        pltpu.make_async_copy(v, v, self.recv.at[b] if sem is None else sem).wait()
    def dev(self, dim):
        if dim == 'x': return (1 - self.s, cid(self.z, self.y, self.c))
        if dim == 'y': return (self.s, cid(self.z, 1 - self.y, self.c))
        if dim == 'c': return (self.s, cid(self.z, self.y, 1 - self.c))
        return (self.s, cid(self.z + (1 if dim == '+' else -1), self.y, self.c))
    def at(self, flips, z):
        s = 1 - self.s if 'x' in flips else self.s
        y = 1 - self.y if 'y' in flips else self.y
        c = 1 - self.c if 'c' in flips else self.c
        return cid(z, y, c) + (s * self.g.ctx if 'x' in self.order else 0)
    def zpush(self, src, b, z, side):
        ok = self.z < self.g.depth - 1 if side == '+' else self.z > 0
        @pl.when(ok)
        def _():
            self.push(src, b, self.dev(side), self.zsend.at[0 if side == '+' else 1, z])
    def start(self, dims=None):
        own = self.at('', self.z)
        for side in '+-':
            self.zpush(self.own(), own, self.z, side)
        for dim in dims or self.rest + 'c':
            self.push(self.own(), own, self.dev(dim), self.send)
        pltpu.make_async_copy(self.own(), self.view(own), self.local).start()
    def sides(self, d, body):
        if isinstance(d, int) and d == 0:
            body(self.z, '')
            return
        @pl.when(self.z - d >= 0)
        def _():
            body(self.z - d, '-')
        @pl.when(self.z + d < self.g.depth)
        def _():
            body(self.z + d, '+')
    def line(self, d, dims=None):
        def go(z, side):
            b = self.at('', z)
            self.wait(b)
            self.zpush(self.view(b), b, z, '+' if side == '-' else '-')
            for k in dims or self.rest + 'c':
                self.push(self.view(b), b, self.dev(k), self.send)
        self.sides(d, go)
    def late(self, dim, d):
        def go(z, side):
            b = self.at('', z)
            self.push(self.own() if side == '' else self.view(b), b, self.dev(dim), self.send)
        self.sides(d, go)
    def cross(self, flips, dims, d):
        def go(z, side):
            b = self.at(flips, z)
            self.wait(b)
            for k in dims:
                self.push(self.view(b), b, self.dev(k), self.send)
        self.sides(d, go)
    def step(self, t):
        r = self.rest
        if t < self.g.depth:
            self.line(t)
        if 1 <= t <= self.g.depth:
            self.cross(r[0], r[1:] + 'c', t - 1)
        if len(r) > 1:
            if 1 <= t <= self.g.depth:
                self.cross(r[1], 'c', t - 1)
            if 2 <= t <= self.g.depth + 1:
                self.cross(r, 'c', t - 2)
    def steps(self):
        return self.g.depth + len(self.rest)
    def arrive(self):
        r = self.rest
        sets = ['', r[0]] + ([r[1], r] if len(r) > 1 else [])
        for f in sets:
            def go(k, f=f):
                self.wait(self.at(f + 'c', k))
            each(self.g.depth, go)
        self.wait(self.at('', self.z), self.local)
    def leave(self):
        def sent(k):
            for side in '+-':
                n = 0 if side == '+' else 1
                ok = (jnp.logical_and(self.z < self.g.depth - 1, k <= self.z) if side == '+'
                      else jnp.logical_and(self.z > 0, k >= self.z))
                @pl.when(ok)
                def _():
                    self.wait(self.at('', k), self.zsend.at[n, k])
        each(self.g.depth, sent)
        p = self.g.depth
        n = p + (2 * p + 4 * p if len(self.rest) > 1 else 2 * p)
        v = self.rows(0, n)
        pltpu.make_async_copy(v, v, self.send).wait()

PLAN = ("q0", "q1", "q2", "q3", "w0", "q4", "w1", "q5", "qa", "k0", "k1", "w2", "k2", "w3", "k3", "w4", "k4", "w5")

def fetch_kernel(grid, scale, *refs):
    x, w_qkv, vec, w_bias, w_out, w_in, w_back = refs[:7]
    qkv_all, vec_all, bias_all, out_all, in_all, back_all, key_all, value_all, query = refs[7:16]
    key, value = refs[16:18]
    sems = refs[18:]
    greet(grid, True)
    def job(i, src, dst, order, cols=None):
        return Gather(grid, src, dst, [r.at[i] for r in sems], order, cols)
    width = x.shape[1]
    half = 3 * width // 2
    parts = {
        "q": [job(0, vec, vec_all, "zyx"), job(1, w_qkv, qkv_all, "zyx", pl.ds(0, half)), job(2, w_qkv, qkv_all, "zxy", pl.ds(half, half))],
        "w": [job(3, w_bias, bias_all, "zyx"), job(4, w_out, out_all, "zyx"), job(5, w_in, in_all, "zyx"), job(6, w_back, back_all, "zyx")],
        "k": [job(7, key, key_all, "zy"), job(8, value, value_all, "zy")]}
    for word in PLAN:
        jobs, t = parts[word[0]], word[1]
        for j in jobs:
            if t == "a": j.arrive()
            elif t == "s": j.start("xc")
            elif t == "l": j.line(int(word[2]), "xc")
            elif t == "y": j.late("y", int(word[2]))
            elif t == "b": j.cross("y", "xc", int(word[2]))
            elif t == "x": j.cross("x", "c", int(word[2]))
            elif t == "z": j.cross("yx", "c", int(word[2]))
            elif t == "0": j.start()
            else: j.step(int(t))
        if word == "qa":
            lane = lax.broadcasted_iota(jnp.int32, (16, 128), 1)
            pick = (lane == lax.broadcasted_iota(jnp.int32, (16, 128), 0)).astype(jnp.bfloat16)
            rows = nt(pick, vec_all[...])
            key[...] = nn(x[...], qkv_all[:, width:2 * width]).astype(jnp.bfloat16)
            value[...] = (nn(x[...], qkv_all[:, 2 * width:]) + rows[1:2]).astype(jnp.bfloat16)
    q = (nn(x[...], qkv_all[:, :width]) + rows[0:1]).astype(jnp.bfloat16)
    query[...] = q * jnp.asarray(scale, jnp.bfloat16)
    for j in parts["k"] + parts["w"]:
        j.arrive()
    for j in parts["q"] + parts["k"] + parts["w"]:
        j.leave()

def fetch(grid, x, w_qkv, vec, w_bias, w_out, w_in, w_back, scale):
    devices, bf = grid.seqs * grid.ctx, jnp.bfloat16
    rows, width = x.shape
    S = jax.ShapeDtypeStruct
    V, A = pl.BlockSpec(memory_space=pltpu.VMEM), pl.BlockSpec(memory_space=pl.ANY)
    D = pltpu.SemaphoreType.DMA
    flat = lambda a: S((devices * a.shape[-2], a.shape[-1]), bf)
    deep = lambda a: S((devices,) + a.shape[1:], bf)
    kv = S((grid.ctx * rows, width), bf)
    return pl.pallas_call(
        functools.partial(fetch_kernel, grid, scale),
        out_shape=[flat(w_qkv), flat(vec), deep(w_bias), deep(w_out), deep(w_in), deep(w_back), kv, kv, S((rows, width), bf)],
        in_specs=[V] * 7,
        out_specs=[V, V] + [A] * 6 + [V],
        scratch_shapes=[pltpu.VMEM((rows, width), bf)] * 2 + [D((9,)), D((9, 2, grid.depth)), D((9, devices)), D((9,))],
        compiler_params=pltpu.CompilerParams(collective_id=0, has_side_effects=True, vmem_limit_bytes=60 * 2**20),
        name="fetch",
    )(x, w_qkv, vec, w_bias, w_out, w_in, w_back)
from jax.sharding import PartitionSpec as P

def f32(x):
    return x.astype(jnp.float32)

class Scatter:
    def __init__(self, grid, src, out, bufs, send, zsend, recvs, order, mine=None, local=None):
        self.g, self.src, self.out, self.mine, self.local = grid, src, out, mine, local
        self.bufc, self.buf1, self.buf2, self.bufz = bufs
        self.send, self.zsend, self.order = send, zsend, order
        self.rc, self.r1, self.r2, self.rz = recvs
        self.dims = order[:0:-1]
        self.two = len(self.dims) > 1
        self.s, self.z, self.y, self.c = grid.here()
    at = Gather.at
    dev = Gather.dev
    def flips(self, f):
        return ''.join(d for d, on in zip(self.dims, f) if on)
    def idx(self, f, z):
        k = 0
        for on in f:
            k = k * 2 + on
        return k * self.g.depth + z
    def push(self, src, dst, recv, dim):
        pltpu.make_async_remote_copy(src, dst, self.send, recv, device_id=self.dev(dim), device_id_type=MESH).start()
    def wait(self, ref, sem):
        pltpu.make_async_copy(ref, ref, sem).wait()
    def combos(self):
        return [(1, 1), (1, 0), (0, 1), (0, 0)] if self.two else [(1,), (0,)]
    def far(self, d, body):
        @pl.when(self.z + d < self.g.depth)
        def _():
            body(self.z + d, '+')
        @pl.when(self.z >= d)
        def _():
            body(self.z - d, '-')
    def own(self, f, z):
        return self.src[self.at(self.flips(f), z)] if self.mine is None else self.mine[self.idx(f, z)]
    def load(self):
        for f in self.combos():
            def go(z, f=f):
                pltpu.make_async_copy(self.src.at[self.at(self.flips(f), z)], self.mine.at[self.idx(f, z)], self.local).start()
            each(self.g.depth, go)
    def loaded(self):
        pltpu.make_async_copy(self.mine, self.mine, self.local).wait()
    def start(self):
        for f in self.combos():
            def go(z, side, f=f):
                k = self.idx(f, z)
                self.push(self.src.at[self.at(self.flips(f) + 'c', z)], self.bufc.at[k], self.rc.at[k], 'c')
            def loop(k, _, go=go):
                self.far(self.g.depth - 1 - k, go)
                return _
            lax.fori_loop(0, self.g.depth - 1, loop, None)
            go(self.z, '')
    def stage1(self, f, d):
        def go(z, side):
            k = self.idx(f, z)
            buf = self.bufc.at[k]
            self.wait(buf, self.rc.at[k])
            buf[...] = (f32(self.own(f, z)) + f32(buf[...])).astype(buf.dtype)
            j = self.idx(f[1:], z)
            self.push(buf, self.buf1.at[j], self.r1.at[j], self.dims[0])
        self.far(d, go) if d is not None else go(self.z, '')
    def stage2(self, d):
        def go(z, side):
            k, j = self.idx((0, 1), z), self.idx((1,), z)
            bufc, buf = self.bufc.at[k], self.buf1.at[j]
            self.wait(bufc, self.rc.at[k])
            self.wait(buf, self.r1.at[j])
            buf[...] = (f32(self.own((0, 1), z)) + f32(bufc[...]) + f32(buf[...])).astype(buf.dtype)
            self.push(buf, self.buf2.at[z], self.r2.at[z], self.dims[1])
        self.far(d, go) if d is not None else go(self.z, '')
    def merged(self, z):
        k = self.idx((0,) * len(self.dims), z)
        bufc, buf1 = self.bufc.at[k], self.buf1.at[z]
        self.wait(bufc, self.rc.at[k])
        self.wait(buf1, self.r1.at[z])
        acc = f32(self.own((0,) * len(self.dims), z)) + f32(bufc[...]) + f32(buf1[...])
        if self.two:
            buf2 = self.buf2.at[z]
            self.wait(buf2, self.r2.at[z])
            acc = acc + f32(buf2[...])
        return acc, bufc
    def chain(self, d):
        top = self.g.depth - 1
        def go(zz, side):
            n = 0 if side == '+' else 1
            more = self.z > 0 if side == '+' else self.z < top
            acc, keep = self.merged(zz)
            keep[...] = acc.astype(keep.dtype)
            buf = self.bufz.at[n, zz]
            @pl.when(more)
            def _():
                self.wait(buf, self.rz.at[n, zz])
                keep[...] = (f32(keep[...]) + f32(buf[...])).astype(keep.dtype)
            pltpu.make_async_remote_copy(keep, buf, self.zsend.at[n, zz], self.rz.at[n, zz], device_id=self.dev(side), device_id_type=MESH).start()
        self.far(d, go)
    def total(self):
        top = self.g.depth - 1
        acc, _ = self.merged(self.z)
        self.out[0] = acc
        for n, ok in ((0, self.z > 0), (1, self.z < top)):
            @pl.when(ok)
            def _(n=n):
                buf = self.bufz.at[n, self.z]
                self.wait(buf, self.rz.at[n, self.z])
                self.out[0] += f32(buf[...])
    def finish(self):
        def sent(k):
            for n, ok in ((0, k > self.z), (1, k < self.z)):
                @pl.when(ok)
                def _(n=n):
                    self.wait(self.bufz.at[n, k], self.zsend.at[n, k])
        each(self.g.depth, sent)
        p = self.g.depth
        n = (4 + 2 + 1) * p if self.two else (2 + 1) * p
        v = self.src.at[pl.ds(0, n)]
        self.wait(v, self.send)

def scatter_scratch(grid, shape, dtype, order):
    p = grid.depth
    two = len(order) > 2
    n1, nc = (2 * p, 4 * p) if two else (p, 2 * p)
    D = pltpu.SemaphoreType.DMA
    return [pltpu.VMEM((nc,) + shape, dtype), pltpu.VMEM((n1,) + shape, dtype), pltpu.VMEM((p if two else 1,) + (shape if two else (8, 128)), dtype), pltpu.VMEM((2, p) + shape, dtype),
            D(()), D((2, p)), D((nc,)), D((n1,)), D((p,)), D((2, p))]

def pair_stack(x, half):
    lane = lax.broadcasted_iota(jnp.int32, x.shape, 1)
    zero = jnp.zeros_like(x)
    return jnp.concatenate((jnp.where(lane < half, x, zero), jnp.where(lane < half, zero, x)), axis=0)

def pair_join(x, half):
    r = x.shape[0] // 2
    lane = lax.broadcasted_iota(jnp.int32, (r, x.shape[1]), 1)
    return jnp.where(lane < half, x[:r], x[r:])

def nt(a, b):
    return lax.dot_general(a, b, (((1,), (1,)), ((), ())), preferred_element_type=jnp.float32)

def nn(a, b):
    return lax.dot_general(a, b, (((1,), (0,)), ((), ())), preferred_element_type=jnp.float32)

def tn(a, b):
    return lax.dot_general(a, b, (((0,), (0,)), ((), ())), preferred_element_type=jnp.float32)

def as_row(col):
    return jnp.transpose(jnp.broadcast_to(col, (col.shape[0], 128)))[0:1]

MASKED = -1e30

def forward_kernel(half, tiles, len_ref, q_ref, k_ref, v_ref, o_ref, lse_ref, top_ref, sum_ref, acc_ref):
    t = pl.program_id(1)
    q2 = pair_stack(q_ref[...], half)
    s = nt(q2, k_ref[...])
    wide = s.shape[1]
    col = lax.broadcasted_iota(jnp.int32, (1, wide), 1) + t * wide
    s = jnp.where(col < len_ref[0], s, MASKED)
    top = jnp.max(s, axis=1, keepdims=True)
    if tiles > 1:
        old = jnp.where(t == 0, MASKED, top_ref[...])
        top = jnp.maximum(old, top)
    p = jnp.exp(s - top)
    total = jnp.sum(p, axis=1, keepdims=True)
    acc = nn(p.astype(jnp.bfloat16), v_ref[...])
    if tiles > 1:
        factor = jnp.where(t == 0, 0.0, jnp.exp(old - top))
        total = total + jnp.where(t == 0, 0.0, sum_ref[...]) * factor
        acc = acc + jnp.where(t == 0, 0.0, acc_ref[...]) * factor
        top_ref[...], sum_ref[...], acc_ref[...] = top, total, acc
    @pl.when(t == tiles - 1)
    def _():
        o_ref[...] = pair_join(acc / total, half)
        lse_ref[0] = as_row(top + jnp.log(total))

def attend(q, k, v, length, heads, tile):
    rows, width = q.shape
    size = width // heads
    total, pairs = k.shape[0], heads // 2
    tiles = total // tile
    wide = 2 * size
    return pl.pallas_call(
        functools.partial(forward_kernel, size, tiles),
        grid_spec=pltpu.PrefetchScalarGridSpec(
            num_scalar_prefetch=1, grid=(pairs, tiles),
            in_specs=[pl.BlockSpec((rows, wide), lambda p, t, n: (0, p)),
                      pl.BlockSpec((tile, wide), lambda p, t, n: (t, p)),
                      pl.BlockSpec((tile, wide), lambda p, t, n: (t, p))],
            out_specs=[pl.BlockSpec((rows, wide), lambda p, t, n: (0, p)),
                       pl.BlockSpec((1, 1, 2 * rows), lambda p, t, n: (p, 0, 0))],
            scratch_shapes=[pltpu.VMEM((2 * rows, 1), jnp.float32), pltpu.VMEM((2 * rows, 1), jnp.float32), pltpu.VMEM((2 * rows, wide), jnp.float32)]),
        out_shape=[jax.ShapeDtypeStruct((rows, width), jnp.float32), jax.ShapeDtypeStruct((pairs, 1, 2 * rows), jnp.float32)],
        name="attend",
    )(length, q, k, v)

def backward_math(half, length, start, q, k, v, g, o, lse):
    q2, g2 = pair_stack(q, half), pair_stack(g, half)
    delta = jnp.sum(jnp.transpose(pair_stack(f32(g) * o, half)), axis=0, keepdims=True)
    s = nt(k, q2)
    row = lax.broadcasted_iota(jnp.int32, (s.shape[0], 1), 0) + start
    p = jnp.where(row < length, jnp.exp(s - lse), 0.0)
    ds = (p * (nt(v, g2) - delta)).astype(jnp.bfloat16)
    return tn(ds, k), nn(ds, q2), nn(p.astype(jnp.bfloat16), g2)

def backward_kernel(half, tiles, scale, len_ref, q_ref, k_ref, v_ref, g_ref, o_ref, lse_ref, dq_ref, dk_ref, dv_ref, sum_ref, acc_ref):
    t = pl.program_id(1)
    dq, dk, dv = backward_math(half, len_ref[0], t * k_ref.shape[0], q_ref[...], k_ref[...], v_ref[...], g_ref[...], o_ref[...], lse_ref[0])
    dk_ref[...] = dk.astype(jnp.bfloat16)
    dv_ref[...] = dv.astype(jnp.bfloat16)
    sums = jnp.sum(dv, axis=0, keepdims=True)
    sum_ref[0] = sums + jnp.where(t == 0, 0.0, sum_ref[0]) if tiles > 1 else sums
    if tiles > 1:
        dq = dq + jnp.where(t == 0, 0.0, acc_ref[...])
        acc_ref[...] = dq
    @pl.when(t == tiles - 1)
    def _():
        dq_ref[...] = (pair_join(dq, half) * scale).astype(jnp.bfloat16)

def attend_back(q, k, v, g, o, lse, length, heads, tile):
    rows, width = q.shape
    size = width // heads
    total, pairs = k.shape[0], heads // 2
    tiles = total // tile
    wide = 2 * size
    R = pl.BlockSpec((rows, wide), lambda p, t, n: (0, p))
    K = pl.BlockSpec((tile, wide), lambda p, t, n: (t, p))
    return pl.pallas_call(
        functools.partial(backward_kernel, size, tiles, size ** -0.5),
        grid_spec=pltpu.PrefetchScalarGridSpec(
            num_scalar_prefetch=1, grid=(pairs, tiles),
            in_specs=[R, K, K, R, R, pl.BlockSpec((1, 1, 2 * rows), lambda p, t, n: (p, 0, 0))],
            out_specs=[R, K, K, pl.BlockSpec((1, 1, wide), lambda p, t, n: (p, 0, 0))],
            scratch_shapes=[pltpu.VMEM((2 * rows, wide), jnp.float32)]),
        out_shape=[jax.ShapeDtypeStruct((rows, width), jnp.bfloat16)] + [jax.ShapeDtypeStruct((total, width), jnp.bfloat16)] * 2 + [jax.ShapeDtypeStruct((pairs, 1, wide), jnp.float32)],
        name="attend_back",
    )(length, q, k, v, g, o, lse)
ORDER = ("ds", "pA", "ld", "d1,*", "As", "A1,*", "pB", "Bs", "B1,*", "d2,*", "e", "A4,*", "B4,d3,*", "g", "qs", "q1,*", "q2,*", "d4,*", "i", "q3,*", "q4,*")

def settle_kernel(grid, size, *refs):
    length, key_all, value_all, g_out, g_in, g_back, w_qkv, q, g, o, lse, x, base, g_bias, g_vec = refs[:15]
    d_qkv, d_out, d_in, d_back, d_bias, d_vec, grad_inputs = refs[15:22]
    own_key, own_value, w_query, w_key, w_value, grads, k_slots, v_slots, wide_w, vec_cols, vec_src, kA, vA, kB, vB = refs[22:37]
    kv_sem, w_sem, local = refs[37:40]
    mine = refs[40:43]
    bufs = refs[43:]
    rows, width = x.shape
    third, pair, pairs = width // 2, 2 * size, width // (2 * size)
    def pull(p):
        at = pl.multiple_of(p * pair, pair)
        return [pltpu.make_async_copy(src.at[:, pl.ds(at, pair)], slots.at[lax.rem(p, 2)], kv_sem.at[n, lax.rem(p, 2)])
                for n, (src, slots) in enumerate(((key_all, k_slots), (value_all, v_slots)))]
    for copy in pull(0): copy.start()
    greet(grid, True)
    cut = lambda n: d_qkv.at[:, :, pl.ds(n * width, width)]
    part_of = lambda ref, n: ref.at[:, :, pl.ds(n * third, third)]
    specs = [("A", vA, part_of(own_value, 0), "zy"), ("A", kA, part_of(own_key, 0), "zy"), ("B", vB, part_of(own_value, 1), "zy"), ("B", kB, part_of(own_key, 1), "zy"),
             ("d", g_back, d_back, "zyx"), ("d", g_in, d_in, "zyx"), ("d", g_out, d_out, "zyx"), ("d", g_bias, d_bias, "zyx"),
             ("q", vec_src, d_vec, "zyx"), ("q", w_query, cut(0), "zyx"), ("q", w_key, cut(1), "zyx"), ("q", w_value, cut(2), "zxy")]
    jobs = {"A": [], "B": [], "d": [], "q": []}
    for n, (group, src, out, order) in enumerate(specs):
        r = bufs[10 * n:10 * n + 10]
        extra = (mine[n - 4], local.at[n - 4]) if 4 <= n < 7 else ()
        jobs[group].append(Scatter(grid, src, out, r[:4], r[4], r[5], r[6:10], order, *extra))
    big = jobs["d"][:3]
    def weigh(at, dst):
        part, wide = dst.shape[1], width // 2
        for n in range(2):
            full = tn(x[...], grads[:, at + n * wide:at + (n + 1) * wide])
            for k in range(dst.shape[0]):
                dst[k, :, n * wide:(n + 1) * wide] = full[k * part:(k + 1) * part].astype(dst.dtype)
    lane = lax.broadcasted_iota(jnp.int32, (pair, 128), 1)
    def attention(first, dk, dv):
        def one(j, _):
            p = first + j
            slot = lax.rem(p, 2)
            @pl.when(p + 1 < pairs)
            def _():
                for copy in pull(p + 1): copy.start()
            for copy in pull(p): copy.wait()
            at = pl.ds(pl.multiple_of(p * pair, pair), pair)
            to = pl.ds(pl.multiple_of(j * pair, pair), pair)
            dq, dk_part, dv_part = backward_math(size, length[0], 0, q[:, at], k_slots[slot], v_slots[slot], g[:, at], o[:, at], lse[p])
            dk[:, :, to] = dk_part.astype(dk.dtype).reshape(dk.shape[0], rows, pair)
            dv[:, :, to] = dv_part.astype(dv.dtype).reshape(dv.shape[0], rows, pair)
            dq = (pair_join(dq, size) * size ** -0.5).astype(grads.dtype)
            grads[:, at] = dq
            tall = lambda v: jnp.transpose(jnp.broadcast_to(jnp.sum(f32(v), axis=0, keepdims=True), (128, pair)))
            vec_cols[at, :] = jnp.where(lane == 0, tall(dq), jnp.where(lane == 1, tall(dv_part), g_vec[at, :]))
            return _
        lax.fori_loop(0, pairs // 2, one, None)
    def early():
        weigh(0, w_query)
        part = vec_src.shape[1]
        for k in range(vec_src.shape[0]):
            vec_src[k] = vec_cols[k * part:(k + 1) * part]
    def after():
        grads[:, width:2 * width] = own_key[0].astype(grads.dtype)
        grads[:, 2 * width:] = own_value[0].astype(grads.dtype)
        weigh(width, w_key)
        weigh(2 * width, w_value)
    def inward():
        total = base[...]
        for n in range(3):
            copy = pltpu.make_async_copy(w_qkv.at[:, pl.ds(n * width, width)], wide_w, w_sem)
            copy.start()
            copy.wait()
            total = total + nt(grads[:, n * width:(n + 1) * width], wide_w[...])
        grad_inputs[...] = total
    alone = {"pA": lambda: attention(0, kA, vA), "pB": lambda: attention(pairs // 2, kB, vB), "e": early, "g": after, "i": inward,
             "ld": lambda: [job.loaded() for job in big]}
    def step(word, d):
        for job in jobs[word[0]]:
            if word[1] == "s":
                if job.mine is not None: job.load()
                job.start()
            elif word[1] == "1": job.stage1(job.combos()[0], d)
            elif word[1] == "2": job.stage1((1, 0), d)
            elif word[1] == "3": job.stage2(d)
            elif d is None: job.total()
            else: job.chain(d)
    for phase in ORDER:
        words = phase.split(",")
        if phase in alone: alone[phase]()
        elif words[-1] == "*":
            def loop(k, _, words=words):
                for word in words[:-1]: step(word, grid.depth - 1 - k)
                return _
            lax.fori_loop(0, grid.depth - 1, loop, None)
            for word in words[:-1]: step(word, None)
        else:
            for word in words: step(word, None)
    for group in [n for n in "ABdq" if n + "s" in ORDER]:
        for job in jobs[group]: job.finish()

def settle(grid, size, length, key_all, value_all, g_out, g_in, g_back, w_qkv, q, g, o, lse, x, base, g_bias, g_vec):
    bf, f4 = jnp.bfloat16, jnp.float32
    rows, width = x.shape
    part, devices = g_out.shape[1], grid.seqs * grid.ctx
    slots, pair = key_all.shape[0], 2 * size
    S = jax.ShapeDtypeStruct
    V, A = pl.BlockSpec(memory_space=pltpu.VMEM), pl.BlockSpec(memory_space=pl.ANY)
    D, M = pltpu.SemaphoreType.DMA, pltpu.VMEM
    scratch = [M((1, rows, width), f4)] * 2 + [M((devices, part, width), bf)] * 3 + [M((rows, 3 * width), bf)] + [M((2, slots, pair), bf)] * 2
    scratch += [M((width, width), bf), M((width, 128), f4), M((devices, part, 128), f4)] + [M((grid.ctx, rows, width // 2), bf)] * 4
    scratch += [D((2, 2)), D(()), D((3,))] + [M((devices // 2,) + a.shape[1:], bf) for a in (g_back, g_in, g_out)]
    for shape, dtype, order in ([((rows, width // 2), bf, "zy")] * 4 + [(a.shape[1:], a.dtype, "zyx") for a in (g_back, g_in, g_out, g_bias)]
                                + [((part, 128), f4, "zyx"), ((part, width), bf, "zyx"), ((part, width), bf, "zyx"), ((part, width), bf, "zxy")]):
        scratch += scatter_scratch(grid, shape, dtype, order)
    one = lambda a: S((1,) + a.shape[1:], f4)
    return pl.pallas_call(
        functools.partial(settle_kernel, grid, size),
        out_shape=[S((1, part, 3 * width), f4), one(g_out), one(g_in), one(g_back), one(g_bias), S((1, part, 128), f4), S((rows, width), f4)],
        in_specs=[pl.BlockSpec(memory_space=pltpu.SMEM)] + [A] * 6 + [V] * 8, out_specs=[V] * 7, scratch_shapes=scratch,
        compiler_params=pltpu.CompilerParams(collective_id=1, has_side_effects=True, vmem_limit_bytes=63 * 2**20),
        name="settle",
    )(length, key_all, value_all, g_out, g_in, g_back, w_qkv, q, g, o, lse, x, base, g_bias, g_vec)

HEADS = 12
EPSILON = 1e-12

def normalize(u):
    mean = jnp.mean(u, axis=-1, keepdims=True)
    centred = u - mean
    r = lax.rsqrt(jnp.mean(centred * centred, axis=-1, keepdims=True) + EPSILON)
    return centred * r, r

def normalize_back(e, n, r, gain):
    c = e * gain
    return r * (c - jnp.mean(c, axis=-1, keepdims=True) - n * jnp.mean(c * n, axis=-1, keepdims=True))

def gelu_parts(v):
    cdf = 0.5 * (1.0 + lax.erf(v * (0.5 ** 0.5)))
    slope = cdf + v * jnp.exp(-0.5 * v * v) * ((2 * jnp.pi) ** -0.5)
    return v * cdf, slope

def layer_kernel(grid, length, w_out_hbm, w_in_hbm, w_back_hbm, attended_ref, x, cotangent, vec_all, bias_all,
                 g_out_hbm, g_in_hbm, g_back_hbm, result, grad_attended, base, g_bias, g_vec,
                 w_out, w_in, w_back, g_out, g_in, g_back, bias, in_sem, out_sem):
    bf = jnp.bfloat16
    loads = [pltpu.make_async_copy(src, dst, in_sem.at[n]) for n, (src, dst) in enumerate(((w_out_hbm, w_out), (w_in_hbm, w_in), (w_back_hbm, w_back)))]
    for copy in loads: copy.start()
    stores = [pltpu.make_async_copy(src, dst, out_sem.at[n]) for n, (src, dst) in enumerate(((g_out, g_out_hbm), (g_in, g_in_hbm), (g_back, g_back_hbm)))]
    rows, width = x.shape
    devices, part_ff = g_back.shape[:2]
    part = g_in.shape[1]
    lane = lax.broadcasted_iota(jnp.int32, (16, 128), 1)
    pick = (lane == lax.broadcasted_iota(jnp.int32, (16, 128), 0)).astype(bf)
    vec = nt(pick, vec_all[...])
    for k in range(devices):
        bias[0:1, k * part_ff:(k + 1) * part_ff] = f32(bias_all[k])[0:1, :part_ff]
    attended = attended_ref[...].astype(bf)
    loads[0].wait()
    branch = nn(attended, w_out[...]) + vec[2:3]
    norm_one, r_one = normalize(f32(x[...]) + branch)
    first = norm_one * vec[3:4] + vec[4:5]
    first_low = first.astype(bf)
    loads[1].wait()
    hidden = nn(first_low, w_in[...]) + bias[0:1]
    active_f, slope = gelu_parts(hidden)
    active = active_f.astype(bf)
    loads[2].wait()
    second = nn(active, w_back[...]) + vec[5:6]
    norm_two, r_two = normalize(first + second)
    result[...] = (norm_two * vec[6:7] + vec[7:8]).astype(bf)
    slot = lax.broadcasted_iota(jnp.int32, (rows, 1), 0) + lax.axis_index("ctx") * rows
    grad_result = jnp.where(slot < length[0], f32(cotangent[...]), 0.0)
    grad_second = normalize_back(grad_result, norm_two, r_two, vec[6:7])
    grad_second_low = grad_second.astype(bf)
    grad_hidden_f = nt(grad_second_low, w_back[...]) * slope
    grad_hidden = grad_hidden_f.astype(bf)
    for n in range(devices * part_ff // width):
        full = tn(active[:, n * width:(n + 1) * width], grad_second_low).astype(bf)
        for k in range(width // part_ff):
            g_back[n * (width // part_ff) + k] = full[k * part_ff:(k + 1) * part_ff]
    stores[2].start()
    for n in range(devices * part_ff // width):
        full = tn(first_low, grad_hidden[:, n * width:(n + 1) * width])
        for k in range(devices):
            g_in[k, :, n * width:(n + 1) * width] = full[k * part:(k + 1) * part].astype(bf)
    stores[1].start()
    grad_first = grad_second + nt(grad_hidden, w_in[...])
    grad_branch_full = normalize_back(grad_first, norm_one, r_one, vec[3:4])
    base[...] = grad_branch_full
    grad_branch = grad_branch_full.astype(bf)
    grad_attended[...] = nt(grad_branch, w_out[...]).astype(bf)
    full = tn(attended, grad_branch)
    for k in range(devices):
        g_out[k] = full[k * part:(k + 1) * part].astype(bf)
    stores[0].start()
    total = lambda a: jnp.sum(f32(a), axis=0, keepdims=True)
    sums = total(grad_hidden)
    g_bias[...] = jnp.zeros_like(g_bias)
    for k in range(devices):
        g_bias[k, 0:1, 0:part_ff] = sums[:, k * part_ff:(k + 1) * part_ff]
    stack = jnp.concatenate((jnp.zeros((2, width), jnp.float32), total(grad_branch), total(grad_first * norm_one), total(grad_first),
                             total(grad_second_low), total(grad_result * norm_two), total(grad_result), jnp.zeros((120, width), jnp.float32)), axis=0)
    for n in range(width // 128):
        g_vec[n * 128:(n + 1) * 128, :] = jnp.transpose(stack[:, n * 128:(n + 1) * 128])
    for copy in stores: copy.wait()

def layer(grid, length, w_out, w_in, w_back, attended, x, cotangent, vec_all, bias_all):
    bf, f4 = jnp.bfloat16, jnp.float32
    rows, width = x.shape
    hidden = w_in.shape[1]
    devices = grid.seqs * grid.ctx
    S, M, D = jax.ShapeDtypeStruct, pltpu.VMEM, pltpu.SemaphoreType.DMA
    V, A = pl.BlockSpec(memory_space=pltpu.VMEM), pl.BlockSpec(memory_space=pl.ANY)
    grads = [(devices, width // devices, width), (devices, width // devices, hidden), (devices, hidden // devices, width)]
    return pl.pallas_call(
        functools.partial(layer_kernel, grid),
        out_shape=[S(g, bf) for g in grads] + [S((rows, width), bf), S((rows, width), bf), S((rows, width), f4), S((devices, 8, 128), f4), S((width, 128), f4)],
        in_specs=[pl.BlockSpec(memory_space=pltpu.SMEM)] + [A] * 3 + [V] * 5, out_specs=[A] * 3 + [V] * 5,
        scratch_shapes=[M(w.shape, bf) for w in (w_out, w_in, w_back)] + [M(g, bf) for g in grads] + [M((8, hidden), f4), D((3,)), D((3,))],
        compiler_params=pltpu.CompilerParams(vmem_limit_bytes=60 * 2**20),
        name="layer",
    )(length, w_out, w_in, w_back, attended, x, cotangent, vec_all, bias_all)

def deliver_kernel(*refs):
    n = len(refs) // 2
    for src, dst in zip(refs[:n], refs[n:]):
        if len(dst.shape) == 3: dst[0] = src[...]
        else: dst[...] = src[0, :dst.shape[0], :dst.shape[1]]

def deliver(arrays, shapes):
    V = pl.BlockSpec(memory_space=pltpu.VMEM)
    return pl.pallas_call(
        deliver_kernel, out_shape=[jax.ShapeDtypeStruct(s, jnp.float32) for s in shapes],
        in_specs=[V] * len(arrays), out_specs=[V] * len(arrays), name="deliver",
    )(*arrays)

def per_device(grid, inputs, lengths, cotangent, w_qkv, w_out, w_in, w_back, vectors, ffn_bias):
    bf, f4 = jnp.bfloat16, jnp.float32
    rows_in = inputs[0]
    rows, width = rows_in.shape
    hidden_size = w_in.shape[1]
    devices = grid.seqs * grid.ctx
    part, part_ff = w_qkv.shape[0], w_back.shape[0]
    slots = grid.ctx * rows
    scale = (width // HEADS) ** -0.5

    half = 3 * width // 2
    whole = grid.depth <= 4 and part % 8 == 0 and part_ff <= 128
    if whole:
        vec_block = jnp.pad(vectors, ((0, 0), (0, 120)))
        bias_block = jnp.pad(ffn_bias[None], ((0, 7), (0, 128 - part_ff)))[None]
        qkv_full, vec_all, bias_all, out_all, in_all, back_all, key_all, value_all, query_scaled = fetch(
            grid, rows_in, w_qkv, vec_block, bias_block, w_out[None], w_in[None], w_back[None], scale)
        out_full, in_full, back_full = out_all.reshape(width, width), in_all.reshape(width, hidden_size), back_all.reshape(hidden_size, width)
    else:
        everywhere = lambda a: lax.all_gather(a, ("seq", "ctx"), axis=0, tiled=True)
        qkv_full, out_full, in_full, back_full = everywhere(w_qkv), everywhere(w_out), everywhere(w_in), everywhere(w_back)
        vec = everywhere(vectors).T.astype(f4)
        ffn_full = everywhere(ffn_bias)[None].astype(f4)
        projected = jnp.dot(rows_in, qkv_full, preferred_element_type=f4)
        query_scaled = (projected[:, :width] + vec[0]).astype(bf) * jnp.asarray(scale, bf)
        key = projected[:, width:2 * width].astype(bf)
        value = (projected[:, 2 * width:] + vec[1]).astype(bf)
        key_all, value_all = (lax.all_gather(a, "ctx", axis=0, tiled=True) for a in (key, value))

    tile = min(slots, 2048)
    attended_f, lse = attend(query_scaled, key_all, value_all, lengths, HEADS, tile)
    if whole:
        g_out, g_in, g_back, result, grad_attended, base, g_bias, g_vec = layer(
            grid, lengths, out_full, in_full, back_full, attended_f, rows_in, cotangent[0], vec_all, bias_all)
        d_qkv, d_out, d_in, d_back, d_bias, d_vec, grad_inputs = settle(
            grid, width // HEADS, lengths, key_all, value_all, g_out, g_in, g_back, qkv_full, query_scaled, grad_attended, attended_f, lse, rows_in, base, g_bias, g_vec)
        grad_inputs, d_qkv, d_out, d_in, d_back, d_vec, d_bias = deliver(
            (grad_inputs, d_qkv, d_out, d_in, d_back, d_vec, d_bias),
            ((1, rows, width), (part, 3 * width), (part, width), (part, hidden_size), (part_ff, width), (part, 8), (1, part_ff)))
        return (result[None], grad_inputs, d_qkv, d_out, d_in, d_back, d_vec, d_bias[0])
    attended = attended_f.astype(bf)
    branch = jnp.dot(attended, out_full, preferred_element_type=f4) + vec[2]
    norm_one, r_one = normalize(rows_in.astype(f4) + branch)
    first = norm_one * vec[3] + vec[4]
    first_low = first.astype(bf)
    hidden = jnp.dot(first_low, in_full, preferred_element_type=f4) + ffn_full
    active_f, slope = gelu_parts(hidden)
    active = active_f.astype(bf)
    second = jnp.dot(active, back_full, preferred_element_type=f4) + vec[5]
    norm_two, r_two = normalize(first + second)
    result = (norm_two * vec[6] + vec[7]).astype(bf)
    start = lax.axis_index("ctx") * rows
    valid = (start + jnp.arange(rows, dtype=jnp.int32) < lengths[0]).astype(f4)[:, None]
    grad_result = cotangent[0].astype(f4) * valid
    grad_second = normalize_back(grad_result, norm_two, r_two, vec[6])
    grad_second_low = grad_second.astype(bf)
    grad_active = lax.dot_general(grad_second_low, back_full, (((1,), (1,)), ((), ())), preferred_element_type=f4)
    grad_hidden = (grad_active * slope).astype(bf)
    grad_first = grad_second + lax.dot_general(grad_hidden, in_full, (((1,), (1,)), ((), ())), preferred_element_type=f4)
    grad_branch_full = normalize_back(grad_first, norm_one, r_one, vec[3])
    grad_branch = grad_branch_full.astype(bf)
    grad_attended = lax.dot_general(grad_branch, out_full, (((1,), (1,)), ((), ())), preferred_element_type=f4).astype(bf)

    def outer(a, b):
        return lax.dot_general(a, b, (((0,), (0,)), ((), ())), preferred_element_type=f4).astype(bf)
    g_back = outer(active, grad_second_low)
    g_in = outer(first_low, grad_hidden)
    g_out = outer(attended, grad_branch)
    grad_ffn = jnp.sum(grad_hidden.astype(f4), axis=0)
    sums = (jnp.sum(grad_branch.astype(f4), axis=0), jnp.sum(grad_first * norm_one, axis=0), jnp.sum(grad_first, axis=0),
            jnp.sum(grad_second_low.astype(f4), axis=0), jnp.sum(grad_result * norm_two, axis=0), jnp.sum(grad_result, axis=0))
    grad_query, g_key, g_value, sum_value = attend_back(query_scaled, key_all, value_all, grad_attended, attended_f, lse, lengths, HEADS, tile)
    sums = jnp.stack((jnp.sum(grad_query.astype(f4), axis=0), sum_value.reshape(width)) + sums)
    home = lambda a, axes: lax.psum_scatter(a.astype(f4), axes, scatter_dimension=0, tiled=True)
    own_key, own_value = (home(a, "ctx").astype(bf) for a in (g_key, g_value))
    grad_projected = jnp.concatenate((grad_query, own_key, own_value), axis=1)
    grad_inputs = grad_branch_full + lax.dot_general(grad_projected, qkv_full, (((1,), (1,)), ((), ())), preferred_element_type=f4)
    both = ("seq", "ctx")
    return (result[None], grad_inputs[None], home(outer(rows_in, grad_projected), both), home(g_out, both), home(g_in, both), home(g_back, both),
            home(sums.T, both), home(grad_ffn, both))

def solution(mesh):
    grid = Grid(mesh.shape["seq"], mesh.shape["ctx"])
    split, both = P("seq", "ctx", None), P(("seq", "ctx"), None)
    return jax.shard_map(
        functools.partial(per_device, grid), mesh=mesh,
        in_specs=(split, P("seq"), split, both, both, both, both, both, P(("seq", "ctx"))),
        out_specs=(split, split, both, both, both, both, both, P(("seq", "ctx"))),
        check_vma=False,
    )
```

```python
import functools, math
import jax, jax.numpy as jnp
from jax import lax
from jax.experimental import pallas as pl
from jax.experimental.pallas import tpu as pltpu

MESH = pl.DeviceIdType.MESH

class Grid:
    def __init__(self, seqs, ctx):
        self.seqs, self.ctx = seqs, ctx
        self.depth = ctx // 4
    def here(self):
        s, i = lax.axis_index("seq"), lax.axis_index("ctx")
        return s, i // 4, (i // 2) % 2, i % 2

def cid(z, y, c):
    return (z * 2 + y) * 2 + c

def greet(grid, with_seq):
    s, z, y, c = grid.here()
    bar = pltpu.get_barrier_semaphore()
    def hello(p):
        pl.semaphore_signal(bar, inc=1, device_id=p, device_id_type=MESH)
    peers = [(s, cid(z, 1 - y, c)), (s, cid(z, y, 1 - c))]
    if with_seq:
        peers += [(1 - s, cid(z, y, c))]
    for p in peers:
        hello(p)
    @pl.when(z > 0)
    def _():
        hello((s, cid(z - 1, y, c)))
    @pl.when(z < grid.depth - 1)
    def _():
        hello((s, cid(z + 1, y, c)))
    ends = jnp.where(z > 0, 1, 0) + jnp.where(z < grid.depth - 1, 1, 0)
    pl.semaphore_wait(bar, len(peers) + ends)

def each(n, body):
    if n <= 4:
        for k in range(n):
            body(k)
    else:
        lax.fori_loop(0, n, lambda k, _: (body(k), None)[1], None)

class Gather:
    def __init__(self, grid, src, dst, sems, order, cols=None):
        self.g, self.src, self.dst = grid, src, dst
        self.send, self.zsend, self.recv, self.local = sems
        self.order, self.cols = order, cols
        self.s, self.z, self.y, self.c = grid.here()
        self.early = order[0] == 'y'
        self.rest = 'x' if self.early else order[1:]
    def rows(self, start, n):
        if len(self.dst.shape) == 3:
            return self.dst.at[start] if n is None else self.dst.at[pl.ds(start, n)]
        size = self.src.shape[-2]
        span = pl.ds(pl.multiple_of(start * size, 8), size * (n or 1))
        return self.dst.at[span] if self.cols is None else self.dst.at[span, self.cols]
    def view(self, b):
        return self.rows(b, None)
    def own(self):
        src = self.src.at[0] if len(self.src.shape) == 3 else self.src
        return src if self.cols is None else src.at[:, self.cols]
    def push(self, src, b, dev, sem):
        pltpu.make_async_remote_copy(src, self.view(b), sem, self.recv.at[b], device_id=dev, device_id_type=MESH).start()
    def wait(self, b, sem=None):
        v = self.view(b)
        pltpu.make_async_copy(v, v, self.recv.at[b] if sem is None else sem).wait()
    def dev(self, dim):
        if dim == 'x': return (1 - self.s, cid(self.z, self.y, self.c))
        if dim == 'y': return (self.s, cid(self.z, 1 - self.y, self.c))
        if dim == 'c': return (self.s, cid(self.z, self.y, 1 - self.c))
        return (self.s, cid(self.z + (1 if dim == '+' else -1), self.y, self.c))
    def at(self, flips, z):
        s = 1 - self.s if 'x' in flips else self.s
        y = 1 - self.y if 'y' in flips else self.y
        c = 1 - self.c if 'c' in flips else self.c
        return cid(z, y, c) + (s * self.g.ctx if 'x' in self.order else 0)
    def zpush(self, src, b, z, side, f=''):
        ok = self.z < self.g.depth - 1 if side == '+' else self.z > 0
        @pl.when(ok)
        def _():
            self.push(src, b, self.dev(side), self.zsend.at[0 if side == '+' else 1, z + (self.g.depth if f else 0)])
    def start(self):
        own = self.at('', self.z)
        if self.early:
            self.push(self.own(), own, self.dev('y'), self.send)
        for side in '+-':
            self.zpush(self.own(), own, self.z, side)
        for dim in self.rest + 'c':
            self.push(self.own(), own, self.dev(dim), self.send)
        pltpu.make_async_copy(self.own(), self.view(own), self.local).start()
    def sides(self, d, body):
        if isinstance(d, int) and d == 0:
            body(self.z, '')
            return
        @pl.when(self.z - d >= 0)
        def _():
            body(self.z - d, '-')
        @pl.when(self.z + d < self.g.depth)
        def _():
            body(self.z + d, '+')
    def line(self, d, f=''):
        def go(z, side):
            b = self.at(f, z)
            self.wait(b)
            for way in '+-':
                if way != side:
                    self.zpush(self.view(b), b, z, way, f)
            for k in self.rest + 'c':
                self.push(self.view(b), b, self.dev(k), self.send)
        self.sides(d, go)
    def cross(self, flips, dims, d):
        def go(z, side):
            b = self.at(flips, z)
            self.wait(b)
            for k in dims:
                self.push(self.view(b), b, self.dev(k), self.send)
        self.sides(d, go)
    def step(self, t):
        r = self.rest
        if self.early:
            if t < self.g.depth:
                self.line(t)
            if t <= self.g.depth:
                self.line(t - 1, 'y')
                self.cross('x', 'c', t - 1)
            if 2 <= t <= self.g.depth + 1:
                self.cross('yx', 'c', t - 2)
            return
        if t < self.g.depth:
            self.line(t)
        if 1 <= t <= self.g.depth:
            self.cross(r[0], r[1:] + 'c', t - 1)
        if len(r) > 1:
            if 1 <= t <= self.g.depth:
                self.cross(r[1], 'c', t - 1)
            if 2 <= t <= self.g.depth + 1:
                self.cross(r, 'c', t - 2)
    def steps(self):
        return self.g.depth + len(self.order) - 1
    def arrive(self):
        r = 'yx' if self.early else self.rest
        sets = ['', r[0]] + ([r[1], r] if len(r) > 1 else [])
        for f in sets:
            def go(k, f=f):
                self.wait(self.at(f + 'c', k))
            each(self.g.depth, go)
        self.wait(self.at('', self.z), self.local)
    def leave(self):
        def sent(k):
            for side in '+-':
                n = 0 if side == '+' else 1
                ok = (jnp.logical_and(self.z < self.g.depth - 1, k <= self.z) if side == '+'
                      else jnp.logical_and(self.z > 0, k >= self.z))
                @pl.when(ok)
                def _():
                    for f in ('', 'y') if self.early else ('',):
                        self.wait(self.at(f, k), self.zsend.at[n, k + (self.g.depth if f else 0)])
        each(self.g.depth, sent)
        p = self.g.depth
        n = 6 * p + 1 if self.early else p + (2 * p + 4 * p if len(self.rest) > 1 else 2 * p)
        v = self.rows(0, n)
        pltpu.make_async_copy(v, v, self.send).wait()

WAYS = ("yzx", "zyx")
PLAN = ("q0", "q1", "q2", "q3", "w0", "q4", "w1", "q5", "qa", "k0", "qq", "k1", "w2", "k2", "w3", "k3", "w4", "k4", "ka", "p0", "p1", "w5", "wa")

def fetch_kernel(grid, size, *refs):
    length, x, w_qkv, vec, w_bias, w_out, w_in, w_back = refs[:8]
    qkv_all, vec_all, bias_all, out_all, in_all, back_all, key_all, value_all, query, attended, lse = refs[8:19]
    key, value, k_slots, v_slots, kv_sem = refs[19:24]
    sems = refs[24:]
    greet(grid, True)
    pair, pairs = 2 * size, x.shape[1] // (2 * size)
    def pull(p):
        at = pl.multiple_of(p * pair, pair)
        return [pltpu.make_async_copy(src.at[:, pl.ds(at, pair)], slots.at[lax.rem(p, 2)], kv_sem.at[n, lax.rem(p, 2)])
                for n, (src, slots) in enumerate(((key_all, k_slots), (value_all, v_slots)))]
    def attention(first):
        def one(j, _):
            p = first + j
            slot = lax.rem(p, 2)
            @pl.when(p + 1 < pairs)
            def _():
                for copy in pull(p + 1): copy.start()
            for copy in pull(p): copy.wait()
            at = pl.ds(pl.multiple_of(p * pair, pair), pair)
            attended[:, at], lse[p] = forward_math(size, length[0], query[:, at], k_slots[slot], v_slots[slot])
            return _
        lax.fori_loop(0, pairs // 2, one, None)
    def job(i, src, dst, order, cols=None):
        return Gather(grid, src, dst, [r.at[i] for r in sems], order, cols)
    width = x.shape[1]
    half = 3 * width // 2
    parts = {
        "q": [job(0, vec, vec_all, "zyx"), job(1, w_qkv, qkv_all, "zyx", pl.ds(0, half)), job(2, w_qkv, qkv_all, "zxy", pl.ds(half, half))],
        "w": [job(3, w_bias, bias_all, "zyx"), job(4, w_out, out_all, "zyx"), job(5, w_in, in_all, WAYS[0]), job(6, w_back, back_all, WAYS[1])],
        "k": [job(7, key, key_all, "zy"), job(8, value, value_all, "zy")]}
    for word in PLAN:
        if word == "p0":
            for copy in pull(0): copy.start()
        if word[0] == "p":
            attention(int(word[1]) * (pairs // 2))
            continue
        if word == "qq":
            q = (nn(x[...], qkv_all[:, :width]) + rows[0:1]).astype(jnp.bfloat16)
            query[...] = q * jnp.asarray(size ** -0.5, jnp.bfloat16)
            continue
        jobs, t = parts[word[0]], word[1]
        for j in jobs:
            if t == "a": j.arrive()
            elif t == "0": j.start()
            else: j.step(int(t))
        if word == "qa":
            lane = lax.broadcasted_iota(jnp.int32, (16, 128), 1)
            pick = (lane == lax.broadcasted_iota(jnp.int32, (16, 128), 0)).astype(jnp.bfloat16)
            rows = nt(pick, vec_all[...])
            key[...] = nn(x[...], qkv_all[:, width:2 * width]).astype(jnp.bfloat16)
            value[...] = (nn(x[...], qkv_all[:, 2 * width:]) + rows[1:2]).astype(jnp.bfloat16)
    for j in parts["q"] + parts["k"] + parts["w"]:
        j.leave()

def fetch(grid, size, length, x, w_qkv, vec, w_bias, w_out, w_in, w_back):
    devices, bf = grid.seqs * grid.ctx, jnp.bfloat16
    rows, width = x.shape
    S = jax.ShapeDtypeStruct
    V, A = pl.BlockSpec(memory_space=pltpu.VMEM), pl.BlockSpec(memory_space=pl.ANY)
    D = pltpu.SemaphoreType.DMA
    flat = lambda a: S((devices * a.shape[-2], a.shape[-1]), bf)
    deep = lambda a: S((devices,) + a.shape[1:], bf)
    kv = S((grid.ctx * rows, width), bf)
    return pl.pallas_call(
        functools.partial(fetch_kernel, grid, size),
        out_shape=[flat(w_qkv), flat(vec), deep(w_bias), deep(w_out), deep(w_in), deep(w_back), kv, kv, S((rows, width), bf),
                   S((rows, width), jnp.float32), S((width // (2 * size), 1, 2 * rows), jnp.float32)],
        in_specs=[pl.BlockSpec(memory_space=pltpu.SMEM)] + [V] * 7,
        out_specs=[V, V] + [A] * 6 + [V] * 3,
        scratch_shapes=[pltpu.VMEM((rows, width), bf)] * 2 + [pltpu.VMEM((2, grid.ctx * rows, 2 * size), bf)] * 2 + [D((2, 2)), D((9,)), D((9, 2, 2 * grid.depth)), D((9, devices)), D((9,))],
        compiler_params=pltpu.CompilerParams(collective_id=0, has_side_effects=True, vmem_limit_bytes=60 * 2**20),
        name="fetch",
    )(length, x, w_qkv, vec, w_bias, w_out, w_in, w_back)
from jax.sharding import PartitionSpec as P

def f32(x):
    return x.astype(jnp.float32)

class Scatter:
    def __init__(self, grid, src, out, bufs, send, zsend, recvs, order, mine=None, local=None):
        self.g, self.src, self.out, self.mine, self.local = grid, src, out, mine, local
        self.bufc, self.buf1, self.buf2, self.bufz = bufs
        self.send, self.zsend, self.order = send, zsend, order
        self.rc, self.r1, self.r2, self.rz = recvs
        self.dims = order[:0:-1]
        self.two = len(self.dims) > 1
        self.s, self.z, self.y, self.c = grid.here()
    at = Gather.at
    dev = Gather.dev
    def flips(self, f):
        return ''.join(d for d, on in zip(self.dims, f) if on)
    def idx(self, f, z):
        k = 0
        for on in f:
            k = k * 2 + on
        return k * self.g.depth + z
    def push(self, src, dst, recv, dim):
        pltpu.make_async_remote_copy(src, dst, self.send, recv, device_id=self.dev(dim), device_id_type=MESH).start()
    def wait(self, ref, sem):
        pltpu.make_async_copy(ref, ref, sem).wait()
    def combos(self):
        return [(1, 1), (1, 0), (0, 1), (0, 0)] if self.two else [(1,), (0,)]
    def far(self, d, body):
        @pl.when(self.z + d < self.g.depth)
        def _():
            body(self.z + d, '+')
        @pl.when(self.z >= d)
        def _():
            body(self.z - d, '-')
    def own(self, f, z):
        return self.src[self.at(self.flips(f), z)] if self.mine is None else self.mine[self.idx(f, z)]
    def load(self):
        for f in self.combos():
            def go(z, f=f):
                pltpu.make_async_copy(self.src.at[self.at(self.flips(f), z)], self.mine.at[self.idx(f, z)], self.local).start()
            each(self.g.depth, go)
    def loaded(self):
        pltpu.make_async_copy(self.mine, self.mine, self.local).wait()
    def start(self, which=slice(None)):
        for f in self.combos()[which]:
            def go(z, side, f=f):
                k = self.idx(f, z)
                self.push(self.src.at[self.at(self.flips(f) + 'c', z)], self.bufc.at[k], self.rc.at[k], 'c')
            def loop(k, _, go=go):
                self.far(self.g.depth - 1 - k, go)
                return _
            lax.fori_loop(0, self.g.depth - 1, loop, None)
            go(self.z, '')
    def stage1(self, f, d):
        def go(z, side):
            k = self.idx(f, z)
            buf = self.bufc.at[k]
            self.wait(buf, self.rc.at[k])
            buf[...] = (f32(self.own(f, z)) + f32(buf[...])).astype(buf.dtype)
            j = self.idx(f[1:], z)
            self.push(buf, self.buf1.at[j], self.r1.at[j], self.dims[0])
        self.far(d, go) if d is not None else go(self.z, '')
    def stage2(self, d):
        def go(z, side):
            k, j = self.idx((0, 1), z), self.idx((1,), z)
            bufc, buf = self.bufc.at[k], self.buf1.at[j]
            self.wait(bufc, self.rc.at[k])
            self.wait(buf, self.r1.at[j])
            buf[...] = (f32(self.own((0, 1), z)) + f32(bufc[...]) + f32(buf[...])).astype(buf.dtype)
            self.push(buf, self.buf2.at[z], self.r2.at[z], self.dims[1])
        self.far(d, go) if d is not None else go(self.z, '')
    def merged(self, z):
        k = self.idx((0,) * len(self.dims), z)
        bufc, buf1 = self.bufc.at[k], self.buf1.at[z]
        self.wait(bufc, self.rc.at[k])
        self.wait(buf1, self.r1.at[z])
        acc = f32(self.own((0,) * len(self.dims), z)) + f32(bufc[...]) + f32(buf1[...])
        if self.two:
            buf2 = self.buf2.at[z]
            self.wait(buf2, self.r2.at[z])
            acc = acc + f32(buf2[...])
        return acc, bufc
    def chain(self, d):
        top = self.g.depth - 1
        def go(zz, side):
            n = 0 if side == '+' else 1
            more = self.z > 0 if side == '+' else self.z < top
            acc, keep = self.merged(zz)
            keep[...] = acc.astype(keep.dtype)
            buf = self.bufz.at[n, zz]
            @pl.when(more)
            def _():
                self.wait(buf, self.rz.at[n, zz])
                keep[...] = (f32(keep[...]) + f32(buf[...])).astype(keep.dtype)
            pltpu.make_async_remote_copy(keep, buf, self.zsend.at[n, zz], self.rz.at[n, zz], device_id=self.dev(side), device_id_type=MESH).start()
        self.far(d, go)
    def total(self):
        top = self.g.depth - 1
        acc, _ = self.merged(self.z)
        self.out[0] = acc
        for n, ok in ((0, self.z > 0), (1, self.z < top)):
            @pl.when(ok)
            def _(n=n):
                buf = self.bufz.at[n, self.z]
                self.wait(buf, self.rz.at[n, self.z])
                self.out[0] += f32(buf[...])
    def finish(self):
        def sent(k):
            for n, ok in ((0, k > self.z), (1, k < self.z)):
                @pl.when(ok)
                def _(n=n):
                    self.wait(self.bufz.at[n, k], self.zsend.at[n, k])
        each(self.g.depth, sent)
        p = self.g.depth
        n = (4 + 2 + 1) * p if self.two else (2 + 1) * p
        v = self.src.at[pl.ds(0, n)]
        self.wait(v, self.send)

def scatter_scratch(grid, shape, dtype, order):
    p = grid.depth
    two = len(order) > 2
    n1, nc = (2 * p, 4 * p) if two else (p, 2 * p)
    D = pltpu.SemaphoreType.DMA
    return [pltpu.VMEM((nc,) + shape, dtype), pltpu.VMEM((n1,) + shape, dtype), pltpu.VMEM((p if two else 1,) + (shape if two else (8, 128)), dtype), pltpu.VMEM((2, p) + shape, dtype),
            D(()), D((2, p)), D((nc,)), D((n1,)), D((p,)), D((2, p))]

def pair_stack(x, half):
    lane = lax.broadcasted_iota(jnp.int32, x.shape, 1)
    zero = jnp.zeros_like(x)
    return jnp.concatenate((jnp.where(lane < half, x, zero), jnp.where(lane < half, zero, x)), axis=0)

def pair_join(x, half):
    r = x.shape[0] // 2
    lane = lax.broadcasted_iota(jnp.int32, (r, x.shape[1]), 1)
    return jnp.where(lane < half, x[:r], x[r:])

def nt(a, b):
    return lax.dot_general(a, b, (((1,), (1,)), ((), ())), preferred_element_type=jnp.float32)

def nn(a, b):
    return lax.dot_general(a, b, (((1,), (0,)), ((), ())), preferred_element_type=jnp.float32)

def tn(a, b):
    return lax.dot_general(a, b, (((0,), (0,)), ((), ())), preferred_element_type=jnp.float32)

def as_row(col):
    return jnp.transpose(jnp.broadcast_to(col, (col.shape[0], 128)))[0:1]

MASKED = -1e30

def forward_math(half, length, q, k, v):
    s = nt(pair_stack(q, half), k)
    s = jnp.where(lax.broadcasted_iota(jnp.int32, (1, s.shape[1]), 1) < length, s, MASKED)
    top = jnp.max(s, axis=1, keepdims=True)
    p = jnp.exp(s - top)
    total = jnp.sum(p, axis=1, keepdims=True)
    return pair_join(nn(p.astype(jnp.bfloat16), v) / total, half), as_row(top + jnp.log(total))

def forward_kernel(half, tiles, len_ref, q_ref, k_ref, v_ref, o_ref, lse_ref, top_ref, sum_ref, acc_ref):
    t = pl.program_id(1)
    q2 = pair_stack(q_ref[...], half)
    s = nt(q2, k_ref[...])
    wide = s.shape[1]
    col = lax.broadcasted_iota(jnp.int32, (1, wide), 1) + t * wide
    s = jnp.where(col < len_ref[0], s, MASKED)
    top = jnp.max(s, axis=1, keepdims=True)
    if tiles > 1:
        old = jnp.where(t == 0, MASKED, top_ref[...])
        top = jnp.maximum(old, top)
    p = jnp.exp(s - top)
    total = jnp.sum(p, axis=1, keepdims=True)
    acc = nn(p.astype(jnp.bfloat16), v_ref[...])
    if tiles > 1:
        factor = jnp.where(t == 0, 0.0, jnp.exp(old - top))
        total = total + jnp.where(t == 0, 0.0, sum_ref[...]) * factor
        acc = acc + jnp.where(t == 0, 0.0, acc_ref[...]) * factor
        top_ref[...], sum_ref[...], acc_ref[...] = top, total, acc
    @pl.when(t == tiles - 1)
    def _():
        o_ref[...] = pair_join(acc / total, half)
        lse_ref[0] = as_row(top + jnp.log(total))

def attend(q, k, v, length, heads, tile):
    rows, width = q.shape
    size = width // heads
    total, pairs = k.shape[0], heads // 2
    tiles = total // tile
    wide = 2 * size
    return pl.pallas_call(
        functools.partial(forward_kernel, size, tiles),
        grid_spec=pltpu.PrefetchScalarGridSpec(
            num_scalar_prefetch=1, grid=(pairs, tiles),
            in_specs=[pl.BlockSpec((rows, wide), lambda p, t, n: (0, p)),
                      pl.BlockSpec((tile, wide), lambda p, t, n: (t, p)),
                      pl.BlockSpec((tile, wide), lambda p, t, n: (t, p))],
            out_specs=[pl.BlockSpec((rows, wide), lambda p, t, n: (0, p)),
                       pl.BlockSpec((1, 1, 2 * rows), lambda p, t, n: (p, 0, 0))],
            scratch_shapes=[pltpu.VMEM((2 * rows, 1), jnp.float32), pltpu.VMEM((2 * rows, 1), jnp.float32), pltpu.VMEM((2 * rows, wide), jnp.float32)]),
        out_shape=[jax.ShapeDtypeStruct((rows, width), jnp.float32), jax.ShapeDtypeStruct((pairs, 1, 2 * rows), jnp.float32)],
        name="attend",
    )(length, q, k, v)

def backward_math(half, length, start, q, k, v, g, o, lse):
    q2, g2 = pair_stack(q, half), pair_stack(g, half)
    delta = jnp.sum(jnp.transpose(pair_stack(f32(g) * o, half)), axis=0, keepdims=True)
    s = nt(k, q2)
    row = lax.broadcasted_iota(jnp.int32, (s.shape[0], 1), 0) + start
    p = jnp.where(row < length, jnp.exp(s - lse), 0.0)
    ds = (p * (nt(v, g2) - delta)).astype(jnp.bfloat16)
    return tn(ds, k), nn(ds, q2), nn(p.astype(jnp.bfloat16), g2)

def backward_kernel(half, tiles, scale, len_ref, q_ref, k_ref, v_ref, g_ref, o_ref, lse_ref, dq_ref, dk_ref, dv_ref, sum_ref, acc_ref):
    t = pl.program_id(1)
    dq, dk, dv = backward_math(half, len_ref[0], t * k_ref.shape[0], q_ref[...], k_ref[...], v_ref[...], g_ref[...], o_ref[...], lse_ref[0])
    dk_ref[...] = dk.astype(jnp.bfloat16)
    dv_ref[...] = dv.astype(jnp.bfloat16)
    sums = jnp.sum(dv, axis=0, keepdims=True)
    sum_ref[0] = sums + jnp.where(t == 0, 0.0, sum_ref[0]) if tiles > 1 else sums
    if tiles > 1:
        dq = dq + jnp.where(t == 0, 0.0, acc_ref[...])
        acc_ref[...] = dq
    @pl.when(t == tiles - 1)
    def _():
        dq_ref[...] = (pair_join(dq, half) * scale).astype(jnp.bfloat16)

def attend_back(q, k, v, g, o, lse, length, heads, tile):
    rows, width = q.shape
    size = width // heads
    total, pairs = k.shape[0], heads // 2
    tiles = total // tile
    wide = 2 * size
    R = pl.BlockSpec((rows, wide), lambda p, t, n: (0, p))
    K = pl.BlockSpec((tile, wide), lambda p, t, n: (t, p))
    return pl.pallas_call(
        functools.partial(backward_kernel, size, tiles, size ** -0.5),
        grid_spec=pltpu.PrefetchScalarGridSpec(
            num_scalar_prefetch=1, grid=(pairs, tiles),
            in_specs=[R, K, K, R, R, pl.BlockSpec((1, 1, 2 * rows), lambda p, t, n: (p, 0, 0))],
            out_specs=[R, K, K, pl.BlockSpec((1, 1, wide), lambda p, t, n: (p, 0, 0))],
            scratch_shapes=[pltpu.VMEM((2 * rows, wide), jnp.float32)]),
        out_shape=[jax.ShapeDtypeStruct((rows, width), jnp.bfloat16)] + [jax.ShapeDtypeStruct((total, width), jnp.bfloat16)] * 2 + [jax.ShapeDtypeStruct((pairs, 1, wide), jnp.float32)],
        name="attend_back",
    )(length, q, k, v, g, o, lse)
ORDER = ("du", "pA", "ld", "d1,*", "As", "A1,*", "dv", "pB", "Bs", "B1,*", "d2,*", "e", "A4,*", "B4,d3,*", "g", "qs", "q1,*", "q2,*", "d4,*", "i", "q3,*", "q4,*")

def settle_kernel(grid, size, *refs):
    length, key_all, value_all, g_out, g_in, g_back, w_qkv, q, g, o, lse, x, base, g_bias, g_vec = refs[:15]
    d_qkv, d_out, d_in, d_back, d_bias, d_vec, grad_inputs = refs[15:22]
    own_key, own_value, w_query, w_key, w_value, grads, k_slots, v_slots, wide_w, vec_cols, vec_src, kA, vA, kB, vB = refs[22:37]
    kv_sem, w_sem, local = refs[37:40]
    mine = refs[40:43]
    bufs = refs[43:]
    rows, width = x.shape
    third, pair, pairs = width // 2, 2 * size, width // (2 * size)
    def pull(p):
        at = pl.multiple_of(p * pair, pair)
        return [pltpu.make_async_copy(src.at[:, pl.ds(at, pair)], slots.at[lax.rem(p, 2)], kv_sem.at[n, lax.rem(p, 2)])
                for n, (src, slots) in enumerate(((key_all, k_slots), (value_all, v_slots)))]
    for copy in pull(0): copy.start()
    greet(grid, True)
    cut = lambda n: d_qkv.at[:, :, pl.ds(n * width, width)]
    part_of = lambda ref, n: ref.at[:, :, pl.ds(n * third, third)]
    specs = [("A", vA, part_of(own_value, 0), "zy"), ("A", kA, part_of(own_key, 0), "zy"), ("B", vB, part_of(own_value, 1), "zy"), ("B", kB, part_of(own_key, 1), "zy"),
             ("d", g_back, d_back, "zyx"), ("d", g_in, d_in, "zyx"), ("d", g_out, d_out, "zyx"), ("d", g_bias, d_bias, "zyx"),
             ("q", vec_src, d_vec, "zyx"), ("q", w_query, cut(0), "zyx"), ("q", w_key, cut(1), "zyx"), ("q", w_value, cut(2), "zxy")]
    jobs = {"A": [], "B": [], "d": [], "q": []}
    for n, (group, src, out, order) in enumerate(specs):
        r = bufs[10 * n:10 * n + 10]
        extra = (mine[n - 4], local.at[n - 4]) if 4 <= n < 7 else ()
        jobs[group].append(Scatter(grid, src, out, r[:4], r[4], r[5], r[6:10], order, *extra))
    big = jobs["d"][:3]
    def weigh(at, dst):
        part, wide = dst.shape[1], width // 2
        for n in range(2):
            full = tn(x[...], grads[:, at + n * wide:at + (n + 1) * wide])
            for k in range(dst.shape[0]):
                dst[k, :, n * wide:(n + 1) * wide] = full[k * part:(k + 1) * part].astype(dst.dtype)
    lane = lax.broadcasted_iota(jnp.int32, (pair, 128), 1)
    def attention(first, dk, dv):
        def one(j, _):
            p = first + j
            slot = lax.rem(p, 2)
            @pl.when(p + 1 < pairs)
            def _():
                for copy in pull(p + 1): copy.start()
            for copy in pull(p): copy.wait()
            at = pl.ds(pl.multiple_of(p * pair, pair), pair)
            to = pl.ds(pl.multiple_of(j * pair, pair), pair)
            dq, dk_part, dv_part = backward_math(size, length[0], 0, q[:, at], k_slots[slot], v_slots[slot], g[:, at], o[:, at], lse[p])
            dk[:, :, to] = dk_part.astype(dk.dtype).reshape(dk.shape[0], rows, pair)
            dv[:, :, to] = dv_part.astype(dv.dtype).reshape(dv.shape[0], rows, pair)
            dq = (pair_join(dq, size) * size ** -0.5).astype(grads.dtype)
            grads[:, at] = dq
            tall = lambda v: jnp.transpose(jnp.broadcast_to(jnp.sum(f32(v), axis=0, keepdims=True), (128, pair)))
            vec_cols[at, :] = jnp.where(lane == 0, tall(dq), jnp.where(lane == 1, tall(dv_part), g_vec[at, :]))
            return _
        lax.fori_loop(0, pairs // 2, one, None)
    def early():
        weigh(0, w_query)
        part = vec_src.shape[1]
        for k in range(vec_src.shape[0]):
            vec_src[k] = vec_cols[k * part:(k + 1) * part]
    def after():
        grads[:, width:2 * width] = own_key[0].astype(grads.dtype)
        grads[:, 2 * width:] = own_value[0].astype(grads.dtype)
        weigh(width, w_key)
        weigh(2 * width, w_value)
    def inward():
        total = base[...]
        for n in range(3):
            copy = pltpu.make_async_copy(w_qkv.at[:, pl.ds(n * width, width)], wide_w, w_sem)
            copy.start()
            copy.wait()
            total = total + nt(grads[:, n * width:(n + 1) * width], wide_w[...])
        grad_inputs[...] = total
    alone = {"pA": lambda: attention(0, kA, vA), "pB": lambda: attention(pairs // 2, kB, vB), "e": early, "g": after, "i": inward,
             "ld": lambda: [job.loaded() for job in big]}
    def step(word, d):
        for job in jobs[word[0]]:
            if word[1] in "su":
                if job.mine is not None: job.load()
                job.start(slice(None, None if word[1] == "s" else 1))
            elif word[1] == "v": job.start(slice(1, None))
            elif word[1] == "1": job.stage1(job.combos()[0], d)
            elif word[1] == "2": job.stage1((1, 0), d)
            elif word[1] == "3": job.stage2(d)
            elif d is None: job.total()
            else: job.chain(d)
    for phase in ORDER:
        words = phase.split(",")
        if phase in alone: alone[phase]()
        elif words[-1] == "*":
            def loop(k, _, words=words):
                for word in words[:-1]: step(word, grid.depth - 1 - k)
                return _
            lax.fori_loop(0, grid.depth - 1, loop, None)
            for word in words[:-1]: step(word, None)
        else:
            for word in words: step(word, None)
    for group in "ABdq":
        for job in jobs[group]: job.finish()

def settle(grid, size, length, key_all, value_all, g_out, g_in, g_back, w_qkv, q, g, o, lse, x, base, g_bias, g_vec):
    bf, f4 = jnp.bfloat16, jnp.float32
    rows, width = x.shape
    part, devices = g_out.shape[1], grid.seqs * grid.ctx
    slots, pair = key_all.shape[0], 2 * size
    S = jax.ShapeDtypeStruct
    V, A = pl.BlockSpec(memory_space=pltpu.VMEM), pl.BlockSpec(memory_space=pl.ANY)
    D, M = pltpu.SemaphoreType.DMA, pltpu.VMEM
    scratch = [M((1, rows, width), f4)] * 2 + [M((devices, part, width), bf)] * 3 + [M((rows, 3 * width), bf)] + [M((2, slots, pair), bf)] * 2
    scratch += [M((width, width), bf), M((width, 128), f4), M((devices, part, 128), f4)] + [M((grid.ctx, rows, width // 2), bf)] * 4
    scratch += [D((2, 2)), D(()), D((3,))] + [M((devices // 2,) + a.shape[1:], bf) for a in (g_back, g_in, g_out)]
    for shape, dtype, order in ([((rows, width // 2), bf, "zy")] * 4 + [(a.shape[1:], a.dtype, "zyx") for a in (g_back, g_in, g_out, g_bias)]
                                + [((part, 128), f4, "zyx"), ((part, width), bf, "zyx"), ((part, width), bf, "zyx"), ((part, width), bf, "zxy")]):
        scratch += scatter_scratch(grid, shape, dtype, order)
    one = lambda a: S((1,) + a.shape[1:], f4)
    return pl.pallas_call(
        functools.partial(settle_kernel, grid, size),
        out_shape=[S((1, part, 3 * width), f4), one(g_out), one(g_in), one(g_back), one(g_bias), S((1, part, 128), f4), S((rows, width), f4)],
        in_specs=[pl.BlockSpec(memory_space=pltpu.SMEM)] + [A] * 6 + [V] * 8, out_specs=[V] * 7, scratch_shapes=scratch,
        compiler_params=pltpu.CompilerParams(collective_id=1, has_side_effects=True, vmem_limit_bytes=63 * 2**20),
        name="settle",
    )(length, key_all, value_all, g_out, g_in, g_back, w_qkv, q, g, o, lse, x, base, g_bias, g_vec)

HEADS = 12
EPSILON = 1e-12

def normalize(u):
    mean = jnp.mean(u, axis=-1, keepdims=True)
    centred = u - mean
    r = lax.rsqrt(jnp.mean(centred * centred, axis=-1, keepdims=True) + EPSILON)
    return centred * r, r

def normalize_back(e, n, r, gain):
    c = e * gain
    return r * (c - jnp.mean(c, axis=-1, keepdims=True) - n * jnp.mean(c * n, axis=-1, keepdims=True))

def gelu_parts(v):
    cdf = 0.5 * (1.0 + lax.erf(v * (0.5 ** 0.5)))
    slope = cdf + v * jnp.exp(-0.5 * v * v) * ((2 * jnp.pi) ** -0.5)
    return v * cdf, slope

def layer_kernel(grid, length, w_out_hbm, w_in_hbm, w_back_hbm, attended_ref, x, cotangent, vec_all, bias_all,
                 g_out_hbm, g_in_hbm, g_back_hbm, result, grad_attended, base, g_bias, g_vec,
                 w_out, w_in, w_back, g_out, g_in, g_back, bias, in_sem, out_sem):
    bf = jnp.bfloat16
    loads = [pltpu.make_async_copy(src, dst, in_sem.at[n]) for n, (src, dst) in enumerate(((w_out_hbm, w_out), (w_in_hbm, w_in), (w_back_hbm, w_back)))]
    for copy in loads: copy.start()
    stores = [pltpu.make_async_copy(src, dst, out_sem.at[n]) for n, (src, dst) in enumerate(((g_out, g_out_hbm), (g_in, g_in_hbm), (g_back, g_back_hbm)))]
    rows, width = x.shape
    devices, part_ff = g_back.shape[:2]
    part = g_in.shape[1]
    lane = lax.broadcasted_iota(jnp.int32, (16, 128), 1)
    pick = (lane == lax.broadcasted_iota(jnp.int32, (16, 128), 0)).astype(bf)
    vec = nt(pick, vec_all[...])
    for k in range(devices):
        bias[0:1, k * part_ff:(k + 1) * part_ff] = f32(bias_all[k])[0:1, :part_ff]
    attended = attended_ref[...].astype(bf)
    loads[0].wait()
    branch = nn(attended, w_out[...]) + vec[2:3]
    norm_one, r_one = normalize(f32(x[...]) + branch)
    first = norm_one * vec[3:4] + vec[4:5]
    first_low = first.astype(bf)
    loads[1].wait()
    hidden = nn(first_low, w_in[...]) + bias[0:1]
    active_f, slope = gelu_parts(hidden)
    active = active_f.astype(bf)
    loads[2].wait()
    second = nn(active, w_back[...]) + vec[5:6]
    norm_two, r_two = normalize(first + second)
    result[...] = (norm_two * vec[6:7] + vec[7:8]).astype(bf)
    slot = lax.broadcasted_iota(jnp.int32, (rows, 1), 0) + lax.axis_index("ctx") * rows
    grad_result = jnp.where(slot < length[0], f32(cotangent[...]), 0.0)
    grad_second = normalize_back(grad_result, norm_two, r_two, vec[6:7])
    grad_second_low = grad_second.astype(bf)
    grad_hidden_f = nt(grad_second_low, w_back[...]) * slope
    grad_hidden = grad_hidden_f.astype(bf)
    for n in range(devices * part_ff // width):
        full = tn(active[:, n * width:(n + 1) * width], grad_second_low).astype(bf)
        for k in range(width // part_ff):
            g_back[n * (width // part_ff) + k] = full[k * part_ff:(k + 1) * part_ff]
    stores[2].start()
    for n in range(devices * part_ff // width):
        full = tn(first_low, grad_hidden[:, n * width:(n + 1) * width])
        for k in range(devices):
            g_in[k, :, n * width:(n + 1) * width] = full[k * part:(k + 1) * part].astype(bf)
    stores[1].start()
    grad_first = grad_second + nt(grad_hidden, w_in[...])
    grad_branch_full = normalize_back(grad_first, norm_one, r_one, vec[3:4])
    base[...] = grad_branch_full
    grad_branch = grad_branch_full.astype(bf)
    grad_attended[...] = nt(grad_branch, w_out[...]).astype(bf)
    full = tn(attended, grad_branch)
    for k in range(devices):
        g_out[k] = full[k * part:(k + 1) * part].astype(bf)
    stores[0].start()
    total = lambda a: jnp.sum(f32(a), axis=0, keepdims=True)
    sums = total(grad_hidden)
    g_bias[...] = jnp.zeros_like(g_bias)
    for k in range(devices):
        g_bias[k, 0:1, 0:part_ff] = sums[:, k * part_ff:(k + 1) * part_ff]
    stack = jnp.concatenate((jnp.zeros((2, width), jnp.float32), total(grad_branch), total(grad_first * norm_one), total(grad_first),
                             total(grad_second_low), total(grad_result * norm_two), total(grad_result), jnp.zeros((120, width), jnp.float32)), axis=0)
    for n in range(width // 128):
        g_vec[n * 128:(n + 1) * 128, :] = jnp.transpose(stack[:, n * 128:(n + 1) * 128])
    for copy in stores: copy.wait()

def layer(grid, length, w_out, w_in, w_back, attended, x, cotangent, vec_all, bias_all):
    bf, f4 = jnp.bfloat16, jnp.float32
    rows, width = x.shape
    hidden = w_in.shape[1]
    devices = grid.seqs * grid.ctx
    S, M, D = jax.ShapeDtypeStruct, pltpu.VMEM, pltpu.SemaphoreType.DMA
    V, A = pl.BlockSpec(memory_space=pltpu.VMEM), pl.BlockSpec(memory_space=pl.ANY)
    grads = [(devices, width // devices, width), (devices, width // devices, hidden), (devices, hidden // devices, width)]
    return pl.pallas_call(
        functools.partial(layer_kernel, grid),
        out_shape=[S(g, bf) for g in grads] + [S((rows, width), bf), S((rows, width), bf), S((rows, width), f4), S((devices, 8, 128), f4), S((width, 128), f4)],
        in_specs=[pl.BlockSpec(memory_space=pltpu.SMEM)] + [A] * 3 + [V] * 5, out_specs=[A] * 3 + [V] * 5,
        scratch_shapes=[M(w.shape, bf) for w in (w_out, w_in, w_back)] + [M(g, bf) for g in grads] + [M((8, hidden), f4), D((3,)), D((3,))],
        compiler_params=pltpu.CompilerParams(vmem_limit_bytes=60 * 2**20),
        name="layer",
    )(length, w_out, w_in, w_back, attended, x, cotangent, vec_all, bias_all)

def deliver_kernel(*refs):
    n = len(refs) // 2
    for src, dst in zip(refs[:n], refs[n:]):
        if len(dst.shape) == 3: dst[0] = src[...]
        else: dst[...] = src[0, :dst.shape[0], :dst.shape[1]]

def deliver(arrays, shapes):
    V = pl.BlockSpec(memory_space=pltpu.VMEM)
    return pl.pallas_call(
        deliver_kernel, out_shape=[jax.ShapeDtypeStruct(s, jnp.float32) for s in shapes],
        in_specs=[V] * len(arrays), out_specs=[V] * len(arrays), name="deliver",
    )(*arrays)

def per_device(grid, inputs, lengths, cotangent, w_qkv, w_out, w_in, w_back, vectors, ffn_bias):
    bf, f4 = jnp.bfloat16, jnp.float32
    rows_in = inputs[0]
    rows, width = rows_in.shape
    hidden_size = w_in.shape[1]
    devices = grid.seqs * grid.ctx
    part, part_ff = w_qkv.shape[0], w_back.shape[0]
    slots = grid.ctx * rows
    scale = (width // HEADS) ** -0.5

    half = 3 * width // 2
    whole = grid.depth <= 4 and part % 8 == 0 and part_ff <= 128
    if whole:
        vec_block = jnp.pad(vectors, ((0, 0), (0, 120)))
        bias_block = jnp.pad(ffn_bias[None], ((0, 7), (0, 128 - part_ff)))[None]
        qkv_full, vec_all, bias_all, out_all, in_all, back_all, key_all, value_all, query_scaled, attended_f, lse = fetch(
            grid, width // HEADS, lengths, rows_in, w_qkv, vec_block, bias_block, w_out[None], w_in[None], w_back[None])
        out_full, in_full, back_full = out_all.reshape(width, width), in_all.reshape(width, hidden_size), back_all.reshape(hidden_size, width)
    else:
        everywhere = lambda a: lax.all_gather(a, ("seq", "ctx"), axis=0, tiled=True)
        qkv_full, out_full, in_full, back_full = everywhere(w_qkv), everywhere(w_out), everywhere(w_in), everywhere(w_back)
        vec = everywhere(vectors).T.astype(f4)
        ffn_full = everywhere(ffn_bias)[None].astype(f4)
        projected = jnp.dot(rows_in, qkv_full, preferred_element_type=f4)
        query_scaled = (projected[:, :width] + vec[0]).astype(bf) * jnp.asarray(scale, bf)
        key = projected[:, width:2 * width].astype(bf)
        value = (projected[:, 2 * width:] + vec[1]).astype(bf)
        key_all, value_all = (lax.all_gather(a, "ctx", axis=0, tiled=True) for a in (key, value))

    if whole:
        g_out, g_in, g_back, result, grad_attended, base, g_bias, g_vec = layer(
            grid, lengths, out_full, in_full, back_full, attended_f, rows_in, cotangent[0], vec_all, bias_all)
        d_qkv, d_out, d_in, d_back, d_bias, d_vec, grad_inputs = settle(
            grid, width // HEADS, lengths, key_all, value_all, g_out, g_in, g_back, qkv_full, query_scaled, grad_attended, attended_f, lse, rows_in, base, g_bias, g_vec)
        grad_inputs, d_qkv, d_out, d_in, d_back, d_vec, d_bias = deliver(
            (grad_inputs, d_qkv, d_out, d_in, d_back, d_vec, d_bias),
            ((1, rows, width), (part, 3 * width), (part, width), (part, hidden_size), (part_ff, width), (part, 8), (1, part_ff)))
        return (result[None], grad_inputs, d_qkv, d_out, d_in, d_back, d_vec, d_bias[0])
    tile = min(slots, 2048)
    attended_f, lse = attend(query_scaled, key_all, value_all, lengths, HEADS, tile)
    attended = attended_f.astype(bf)
    branch = jnp.dot(attended, out_full, preferred_element_type=f4) + vec[2]
    norm_one, r_one = normalize(rows_in.astype(f4) + branch)
    first = norm_one * vec[3] + vec[4]
    first_low = first.astype(bf)
    hidden = jnp.dot(first_low, in_full, preferred_element_type=f4) + ffn_full
    active_f, slope = gelu_parts(hidden)
    active = active_f.astype(bf)
    second = jnp.dot(active, back_full, preferred_element_type=f4) + vec[5]
    norm_two, r_two = normalize(first + second)
    result = (norm_two * vec[6] + vec[7]).astype(bf)
    start = lax.axis_index("ctx") * rows
    valid = (start + jnp.arange(rows, dtype=jnp.int32) < lengths[0]).astype(f4)[:, None]
    grad_result = cotangent[0].astype(f4) * valid
    grad_second = normalize_back(grad_result, norm_two, r_two, vec[6])
    grad_second_low = grad_second.astype(bf)
    grad_active = lax.dot_general(grad_second_low, back_full, (((1,), (1,)), ((), ())), preferred_element_type=f4)
    grad_hidden = (grad_active * slope).astype(bf)
    grad_first = grad_second + lax.dot_general(grad_hidden, in_full, (((1,), (1,)), ((), ())), preferred_element_type=f4)
    grad_branch_full = normalize_back(grad_first, norm_one, r_one, vec[3])
    grad_branch = grad_branch_full.astype(bf)
    grad_attended = lax.dot_general(grad_branch, out_full, (((1,), (1,)), ((), ())), preferred_element_type=f4).astype(bf)

    def outer(a, b):
        return lax.dot_general(a, b, (((0,), (0,)), ((), ())), preferred_element_type=f4).astype(bf)
    g_back = outer(active, grad_second_low)
    g_in = outer(first_low, grad_hidden)
    g_out = outer(attended, grad_branch)
    grad_ffn = jnp.sum(grad_hidden.astype(f4), axis=0)
    sums = (jnp.sum(grad_branch.astype(f4), axis=0), jnp.sum(grad_first * norm_one, axis=0), jnp.sum(grad_first, axis=0),
            jnp.sum(grad_second_low.astype(f4), axis=0), jnp.sum(grad_result * norm_two, axis=0), jnp.sum(grad_result, axis=0))
    grad_query, g_key, g_value, sum_value = attend_back(query_scaled, key_all, value_all, grad_attended, attended_f, lse, lengths, HEADS, tile)
    sums = jnp.stack((jnp.sum(grad_query.astype(f4), axis=0), sum_value.reshape(width)) + sums)
    home = lambda a, axes: lax.psum_scatter(a.astype(f4), axes, scatter_dimension=0, tiled=True)
    own_key, own_value = (home(a, "ctx").astype(bf) for a in (g_key, g_value))
    grad_projected = jnp.concatenate((grad_query, own_key, own_value), axis=1)
    grad_inputs = grad_branch_full + lax.dot_general(grad_projected, qkv_full, (((1,), (1,)), ((), ())), preferred_element_type=f4)
    both = ("seq", "ctx")
    return (result[None], grad_inputs[None], home(outer(rows_in, grad_projected), both), home(g_out, both), home(g_in, both), home(g_back, both),
            home(sums.T, both), home(grad_ffn, both))

def solution(mesh):
    grid = Grid(mesh.shape["seq"], mesh.shape["ctx"])
    split, both = P("seq", "ctx", None), P(("seq", "ctx"), None)
    return jax.shard_map(
        functools.partial(per_device, grid), mesh=mesh,
        in_specs=(split, P("seq"), split, both, both, both, both, both, P(("seq", "ctx"))),
        out_specs=(split, split, both, both, both, both, both, P(("seq", "ctx"))),
        check_vma=False,
    )
```

```python
import functools, math
import jax, jax.numpy as jnp
from jax import lax
from jax.experimental import pallas as pl
from jax.experimental.pallas import tpu as pltpu

MESH = pl.DeviceIdType.MESH

class Grid:
    def __init__(self, seqs, ctx):
        self.seqs, self.ctx = seqs, ctx
        self.depth = ctx // 4
    def here(self):
        s, i = lax.axis_index("seq"), lax.axis_index("ctx")
        return s, i // 4, (i // 2) % 2, i % 2

def cid(z, y, c):
    return (z * 2 + y) * 2 + c

def greet(grid, with_seq):
    s, z, y, c = grid.here()
    bar = pltpu.get_barrier_semaphore()
    def hello(p):
        pl.semaphore_signal(bar, inc=1, device_id=p, device_id_type=MESH)
    peers = [(s, cid(z, 1 - y, c)), (s, cid(z, y, 1 - c))]
    if with_seq:
        peers += [(1 - s, cid(z, y, c))]
    for p in peers:
        hello(p)
    @pl.when(z > 0)
    def _():
        hello((s, cid(z - 1, y, c)))
    @pl.when(z < grid.depth - 1)
    def _():
        hello((s, cid(z + 1, y, c)))
    ends = jnp.where(z > 0, 1, 0) + jnp.where(z < grid.depth - 1, 1, 0)
    pl.semaphore_wait(bar, len(peers) + ends)

def each(n, body):
    if n <= 4:
        for k in range(n):
            body(k)
    else:
        lax.fori_loop(0, n, lambda k, _: (body(k), None)[1], None)

class Gather:
    def __init__(self, grid, src, dst, sems, order, cols=None):
        self.g, self.src, self.dst = grid, src, dst
        self.send, self.zsend, self.recv, self.local = sems
        self.order, self.cols = order, cols
        self.s, self.z, self.y, self.c = grid.here()
        self.early = order[0] == 'y'
        self.rest = 'x' if self.early else order[1:]
    def rows(self, start, n):
        if len(self.dst.shape) == 3:
            return self.dst.at[start] if n is None else self.dst.at[pl.ds(start, n)]
        size = self.src.shape[-2]
        span = pl.ds(pl.multiple_of(start * size, 8), size * (n or 1))
        return self.dst.at[span] if self.cols is None else self.dst.at[span, self.cols]
    def view(self, b):
        return self.rows(b, None)
    def own(self):
        src = self.src.at[0] if len(self.src.shape) == 3 else self.src
        return src if self.cols is None else src.at[:, self.cols]
    def push(self, src, b, dev, sem):
        pltpu.make_async_remote_copy(src, self.view(b), sem, self.recv.at[b], device_id=dev, device_id_type=MESH).start()
    def wait(self, b, sem=None):
        v = self.view(b)
        pltpu.make_async_copy(v, v, self.recv.at[b] if sem is None else sem).wait()
    def dev(self, dim):
        if dim == 'x': return (1 - self.s, cid(self.z, self.y, self.c))
        if dim == 'y': return (self.s, cid(self.z, 1 - self.y, self.c))
        if dim == 'c': return (self.s, cid(self.z, self.y, 1 - self.c))
        return (self.s, cid(self.z + (1 if dim == '+' else -1), self.y, self.c))
    def at(self, flips, z):
        s = 1 - self.s if 'x' in flips else self.s
        y = 1 - self.y if 'y' in flips else self.y
        c = 1 - self.c if 'c' in flips else self.c
        return cid(z, y, c) + (s * self.g.ctx if 'x' in self.order else 0)
    def zpush(self, src, b, z, side, f=''):
        ok = self.z < self.g.depth - 1 if side == '+' else self.z > 0
        @pl.when(ok)
        def _():
            self.push(src, b, self.dev(side), self.zsend.at[0 if side == '+' else 1, z + (self.g.depth if f else 0)])
    def start(self):
        own = self.at('', self.z)
        if self.early:
            self.push(self.own(), own, self.dev('y'), self.send)
        for side in '+-':
            self.zpush(self.own(), own, self.z, side)
        for dim in self.rest + 'c':
            self.push(self.own(), own, self.dev(dim), self.send)
        pltpu.make_async_copy(self.own(), self.view(own), self.local).start()
    def sides(self, d, body):
        if isinstance(d, int) and d == 0:
            body(self.z, '')
            return
        @pl.when(self.z - d >= 0)
        def _():
            body(self.z - d, '-')
        @pl.when(self.z + d < self.g.depth)
        def _():
            body(self.z + d, '+')
    def line(self, d, f=''):
        def go(z, side):
            b = self.at(f, z)
            self.wait(b)
            for way in '+-':
                if way != side:
                    self.zpush(self.view(b), b, z, way, f)
            for k in self.rest + 'c':
                self.push(self.view(b), b, self.dev(k), self.send)
        self.sides(d, go)
    def cross(self, flips, dims, d):
        def go(z, side):
            b = self.at(flips, z)
            self.wait(b)
            for k in dims:
                self.push(self.view(b), b, self.dev(k), self.send)
        self.sides(d, go)
    def step(self, t):
        r = self.rest
        if self.early:
            if t < self.g.depth:
                self.line(t)
            if t <= self.g.depth:
                self.line(t - 1, 'y')
                self.cross('x', 'c', t - 1)
            if 2 <= t <= self.g.depth + 1:
                self.cross('yx', 'c', t - 2)
            return
        if t < self.g.depth:
            self.line(t)
        if 1 <= t <= self.g.depth:
            self.cross(r[0], r[1:] + 'c', t - 1)
        if len(r) > 1:
            if 1 <= t <= self.g.depth:
                self.cross(r[1], 'c', t - 1)
            if 2 <= t <= self.g.depth + 1:
                self.cross(r, 'c', t - 2)
    def steps(self):
        return self.g.depth + len(self.order) - 1
    def arrive(self):
        r = 'yx' if self.early else self.rest
        sets = ['', r[0]] + ([r[1], r] if len(r) > 1 else [])
        for f in sets:
            def go(k, f=f):
                self.wait(self.at(f + 'c', k))
            each(self.g.depth, go)
        self.wait(self.at('', self.z), self.local)
    def leave(self):
        def sent(k):
            for side in '+-':
                n = 0 if side == '+' else 1
                ok = (jnp.logical_and(self.z < self.g.depth - 1, k <= self.z) if side == '+'
                      else jnp.logical_and(self.z > 0, k >= self.z))
                @pl.when(ok)
                def _():
                    for f in ('', 'y') if self.early else ('',):
                        self.wait(self.at(f, k), self.zsend.at[n, k + (self.g.depth if f else 0)])
        each(self.g.depth, sent)
        p = self.g.depth
        n = 6 * p + 1 if self.early else p + (2 * p + 4 * p if len(self.rest) > 1 else 2 * p)
        v = self.rows(0, n)
        pltpu.make_async_copy(v, v, self.send).wait()

WAYS = ("yzx", "zyx")
PLAN = ("q0", "q1", "q2", "q3", "w0", "q4", "w1", "q5", "qa", "k0", "qq", "k1", "w2", "k2", "w3", "k3", "w4", "k4", "ka", "p0", "p1", "w5", "wa")

def fetch_kernel(grid, size, *refs):
    length, x, w_qkv, vec_rows, bias_row, w_out, w_in, w_back = refs[:8]
    qkv_all, vec_all, bias_all, out_all, in_all, back_all, key_all, value_all, query, attended, lse = refs[8:19]
    key, value, k_slots, v_slots, vec, w_bias, room, kv_sem = refs[19:27]
    sems = refs[27:]
    part, part_ff = vec.shape[0], bias_row.shape[1]
    room[...] = jnp.zeros_like(room)
    room[0:8, 0:part] = f32(vec_rows[...])
    vec[...] = jnp.transpose(room[...])[0:part].astype(vec.dtype)
    room[0:1, 0:part_ff] = f32(bias_row[...])
    w_bias[0] = room[0:8, :].astype(w_bias.dtype)
    greet(grid, True)
    pair, pairs = 2 * size, x.shape[1] // (2 * size)
    def pull(p):
        at = pl.multiple_of(p * pair, pair)
        return [pltpu.make_async_copy(src.at[:, pl.ds(at, pair)], slots.at[lax.rem(p, 2)], kv_sem.at[n, lax.rem(p, 2)])
                for n, (src, slots) in enumerate(((key_all, k_slots), (value_all, v_slots)))]
    def attention(first):
        def one(j, _):
            p = first + j
            slot = lax.rem(p, 2)
            @pl.when(p + 1 < pairs)
            def _():
                for copy in pull(p + 1): copy.start()
            for copy in pull(p): copy.wait()
            at = pl.ds(pl.multiple_of(p * pair, pair), pair)
            attended[:, at], lse[p] = forward_math(size, length[0], query[:, at], k_slots[slot], v_slots[slot])
            return _
        lax.fori_loop(0, pairs // 2, one, None)
    def job(i, src, dst, order, cols=None):
        return Gather(grid, src, dst, [r.at[i] for r in sems], order, cols)
    width = x.shape[1]
    half = 3 * width // 2
    parts = {
        "q": [job(0, vec, vec_all, "zyx"), job(1, w_qkv, qkv_all, "zyx", pl.ds(0, half)), job(2, w_qkv, qkv_all, "zxy", pl.ds(half, half))],
        "w": [job(3, w_bias, bias_all, "zyx"), job(4, w_out, out_all, "zyx"), job(5, w_in, in_all, WAYS[0]), job(6, w_back, back_all, WAYS[1])],
        "k": [job(7, key, key_all, "zy"), job(8, value, value_all, "zy")]}
    for word in PLAN:
        if word == "p0":
            for copy in pull(0): copy.start()
        if word[0] == "p":
            attention(int(word[1]) * (pairs // 2))
            continue
        if word == "qq":
            q = (nn(x[...], qkv_all[:, :width]) + rows[0:1]).astype(jnp.bfloat16)
            query[...] = q * jnp.asarray(size ** -0.5, jnp.bfloat16)
            continue
        jobs, t = parts[word[0]], word[1]
        for j in jobs:
            if t == "a": j.arrive()
            elif t == "0": j.start()
            else: j.step(int(t))
        if word == "qa":
            lane = lax.broadcasted_iota(jnp.int32, (16, 128), 1)
            pick = (lane == lax.broadcasted_iota(jnp.int32, (16, 128), 0)).astype(jnp.bfloat16)
            rows = nt(pick, vec_all[...])
            key[...] = nn(x[...], qkv_all[:, width:2 * width]).astype(jnp.bfloat16)
            value[...] = (nn(x[...], qkv_all[:, 2 * width:]) + rows[1:2]).astype(jnp.bfloat16)
    for j in parts["q"] + parts["k"] + parts["w"]:
        j.leave()

def fetch(grid, size, length, x, w_qkv, vec_rows, bias_row, w_out, w_in, w_back):
    devices, bf = grid.seqs * grid.ctx, jnp.bfloat16
    rows, width = x.shape
    S = jax.ShapeDtypeStruct
    V, A = pl.BlockSpec(memory_space=pltpu.VMEM), pl.BlockSpec(memory_space=pl.ANY)
    D = pltpu.SemaphoreType.DMA
    flat = lambda a: S((devices * a.shape[-2], a.shape[-1]), bf)
    deep = lambda a: S((devices,) + a.shape[1:], bf)
    kv = S((grid.ctx * rows, width), bf)
    return pl.pallas_call(
        functools.partial(fetch_kernel, grid, size),
        out_shape=[flat(w_qkv), S((width, 128), bf), S((devices, 8, 128), bf), deep(w_out), deep(w_in), deep(w_back), kv, kv, S((rows, width), bf),
                   S((rows, width), jnp.float32), S((width // (2 * size), 1, 2 * rows), jnp.float32)],
        in_specs=[pl.BlockSpec(memory_space=pltpu.SMEM)] + [V] * 7,
        out_specs=[V, V] + [A] * 6 + [V] * 3,
        scratch_shapes=[pltpu.VMEM((rows, width), bf)] * 2 + [pltpu.VMEM((2, grid.ctx * rows, 2 * size), bf)] * 2
                       + [pltpu.VMEM((width // devices, 128), bf), pltpu.VMEM((1, 8, 128), bf), pltpu.VMEM((128, 128), jnp.float32)] + [D((2, 2)), D((9,)), D((9, 2, 2 * grid.depth)), D((9, devices)), D((9,))],
        compiler_params=pltpu.CompilerParams(collective_id=0, has_side_effects=True, vmem_limit_bytes=60 * 2**20),
        name="fetch",
    )(length, x, w_qkv, vec_rows, bias_row, w_out, w_in, w_back)
from jax.sharding import PartitionSpec as P

def f32(x):
    return x.astype(jnp.float32)

class Scatter:
    def __init__(self, grid, src, out, bufs, send, zsend, recvs, order, mine=None, local=None):
        self.g, self.src, self.out, self.mine, self.local = grid, src, out, mine, local
        self.bufc, self.buf1, self.buf2, self.bufz = bufs
        self.send, self.zsend, self.order = send, zsend, order
        self.rc, self.r1, self.r2, self.rz = recvs
        self.dims = order[:0:-1]
        self.two = len(self.dims) > 1
        self.s, self.z, self.y, self.c = grid.here()
    at = Gather.at
    dev = Gather.dev
    def flips(self, f):
        return ''.join(d for d, on in zip(self.dims, f) if on)
    def idx(self, f, z):
        k = 0
        for on in f:
            k = k * 2 + on
        return k * self.g.depth + z
    def push(self, src, dst, recv, dim):
        pltpu.make_async_remote_copy(src, dst, self.send, recv, device_id=self.dev(dim), device_id_type=MESH).start()
    def wait(self, ref, sem):
        pltpu.make_async_copy(ref, ref, sem).wait()
    def combos(self):
        return [(1, 1), (1, 0), (0, 1), (0, 0)] if self.two else [(1,), (0,)]
    def far(self, d, body):
        @pl.when(self.z + d < self.g.depth)
        def _():
            body(self.z + d, '+')
        @pl.when(self.z >= d)
        def _():
            body(self.z - d, '-')
    def own(self, f, z):
        return self.src[self.at(self.flips(f), z)] if self.mine is None else self.mine[self.idx(f, z)]
    def load(self):
        for f in self.combos():
            def go(z, f=f):
                pltpu.make_async_copy(self.src.at[self.at(self.flips(f), z)], self.mine.at[self.idx(f, z)], self.local).start()
            each(self.g.depth, go)
    def loaded(self):
        pltpu.make_async_copy(self.mine, self.mine, self.local).wait()
    def start(self, which=slice(None)):
        for f in self.combos()[which]:
            def go(z, side, f=f):
                k = self.idx(f, z)
                self.push(self.src.at[self.at(self.flips(f) + 'c', z)], self.bufc.at[k], self.rc.at[k], 'c')
            def loop(k, _, go=go):
                self.far(self.g.depth - 1 - k, go)
                return _
            lax.fori_loop(0, self.g.depth - 1, loop, None)
            go(self.z, '')
    def stage1(self, f, d):
        def go(z, side):
            k = self.idx(f, z)
            buf = self.bufc.at[k]
            self.wait(buf, self.rc.at[k])
            buf[...] = (f32(self.own(f, z)) + f32(buf[...])).astype(buf.dtype)
            j = self.idx(f[1:], z)
            self.push(buf, self.buf1.at[j], self.r1.at[j], self.dims[0])
        self.far(d, go) if d is not None else go(self.z, '')
    def stage2(self, d):
        def go(z, side):
            k, j = self.idx((0, 1), z), self.idx((1,), z)
            bufc, buf = self.bufc.at[k], self.buf1.at[j]
            self.wait(bufc, self.rc.at[k])
            self.wait(buf, self.r1.at[j])
            buf[...] = (f32(self.own((0, 1), z)) + f32(bufc[...]) + f32(buf[...])).astype(buf.dtype)
            self.push(buf, self.buf2.at[z], self.r2.at[z], self.dims[1])
        self.far(d, go) if d is not None else go(self.z, '')
    def merged(self, z):
        k = self.idx((0,) * len(self.dims), z)
        bufc, buf1 = self.bufc.at[k], self.buf1.at[z]
        self.wait(bufc, self.rc.at[k])
        self.wait(buf1, self.r1.at[z])
        acc = f32(self.own((0,) * len(self.dims), z)) + f32(bufc[...]) + f32(buf1[...])
        if self.two:
            buf2 = self.buf2.at[z]
            self.wait(buf2, self.r2.at[z])
            acc = acc + f32(buf2[...])
        return acc, bufc
    def chain(self, d):
        top = self.g.depth - 1
        def go(zz, side):
            n = 0 if side == '+' else 1
            more = self.z > 0 if side == '+' else self.z < top
            acc, keep = self.merged(zz)
            keep[...] = acc.astype(keep.dtype)
            buf = self.bufz.at[n, zz]
            @pl.when(more)
            def _():
                self.wait(buf, self.rz.at[n, zz])
                keep[...] = (f32(keep[...]) + f32(buf[...])).astype(keep.dtype)
            pltpu.make_async_remote_copy(keep, buf, self.zsend.at[n, zz], self.rz.at[n, zz], device_id=self.dev(side), device_id_type=MESH).start()
        self.far(d, go)
    def total(self):
        top = self.g.depth - 1
        acc, _ = self.merged(self.z)
        self.out[0] = acc
        for n, ok in ((0, self.z > 0), (1, self.z < top)):
            @pl.when(ok)
            def _(n=n):
                buf = self.bufz.at[n, self.z]
                self.wait(buf, self.rz.at[n, self.z])
                self.out[0] += f32(buf[...])
    def finish(self):
        def sent(k):
            for n, ok in ((0, k > self.z), (1, k < self.z)):
                @pl.when(ok)
                def _(n=n):
                    self.wait(self.bufz.at[n, k], self.zsend.at[n, k])
        each(self.g.depth, sent)
        p = self.g.depth
        n = (4 + 2 + 1) * p if self.two else (2 + 1) * p
        v = self.src.at[pl.ds(0, n)]
        self.wait(v, self.send)

def scatter_scratch(grid, shape, dtype, order):
    p = grid.depth
    two = len(order) > 2
    n1, nc = (2 * p, 4 * p) if two else (p, 2 * p)
    D = pltpu.SemaphoreType.DMA
    return [pltpu.VMEM((nc,) + shape, dtype), pltpu.VMEM((n1,) + shape, dtype), pltpu.VMEM((p if two else 1,) + (shape if two else (8, 128)), dtype), pltpu.VMEM((2, p) + shape, dtype),
            D(()), D((2, p)), D((nc,)), D((n1,)), D((p,)), D((2, p))]

def pair_stack(x, half):
    lane = lax.broadcasted_iota(jnp.int32, x.shape, 1)
    zero = jnp.zeros_like(x)
    return jnp.concatenate((jnp.where(lane < half, x, zero), jnp.where(lane < half, zero, x)), axis=0)

def pair_join(x, half):
    r = x.shape[0] // 2
    lane = lax.broadcasted_iota(jnp.int32, (r, x.shape[1]), 1)
    return jnp.where(lane < half, x[:r], x[r:])

def nt(a, b):
    return lax.dot_general(a, b, (((1,), (1,)), ((), ())), preferred_element_type=jnp.float32)

def nn(a, b):
    return lax.dot_general(a, b, (((1,), (0,)), ((), ())), preferred_element_type=jnp.float32)

def tn(a, b):
    return lax.dot_general(a, b, (((0,), (0,)), ((), ())), preferred_element_type=jnp.float32)

def as_row(col):
    return jnp.transpose(jnp.broadcast_to(col, (col.shape[0], 128)))[0:1]

MASKED = -1e30

def forward_math(half, length, q, k, v):
    s = nt(pair_stack(q, half), k)
    s = jnp.where(lax.broadcasted_iota(jnp.int32, (1, s.shape[1]), 1) < length, s, MASKED)
    top = jnp.max(s, axis=1, keepdims=True)
    p = jnp.exp(s - top)
    total = jnp.sum(p, axis=1, keepdims=True)
    return pair_join(nn(p.astype(jnp.bfloat16), v) / total, half), as_row(top + jnp.log(total))

def forward_kernel(half, tiles, len_ref, q_ref, k_ref, v_ref, o_ref, lse_ref, top_ref, sum_ref, acc_ref):
    t = pl.program_id(1)
    q2 = pair_stack(q_ref[...], half)
    s = nt(q2, k_ref[...])
    wide = s.shape[1]
    col = lax.broadcasted_iota(jnp.int32, (1, wide), 1) + t * wide
    s = jnp.where(col < len_ref[0], s, MASKED)
    top = jnp.max(s, axis=1, keepdims=True)
    if tiles > 1:
        old = jnp.where(t == 0, MASKED, top_ref[...])
        top = jnp.maximum(old, top)
    p = jnp.exp(s - top)
    total = jnp.sum(p, axis=1, keepdims=True)
    acc = nn(p.astype(jnp.bfloat16), v_ref[...])
    if tiles > 1:
        factor = jnp.where(t == 0, 0.0, jnp.exp(old - top))
        total = total + jnp.where(t == 0, 0.0, sum_ref[...]) * factor
        acc = acc + jnp.where(t == 0, 0.0, acc_ref[...]) * factor
        top_ref[...], sum_ref[...], acc_ref[...] = top, total, acc
    @pl.when(t == tiles - 1)
    def _():
        o_ref[...] = pair_join(acc / total, half)
        lse_ref[0] = as_row(top + jnp.log(total))

def attend(q, k, v, length, heads, tile):
    rows, width = q.shape
    size = width // heads
    total, pairs = k.shape[0], heads // 2
    tiles = total // tile
    wide = 2 * size
    return pl.pallas_call(
        functools.partial(forward_kernel, size, tiles),
        grid_spec=pltpu.PrefetchScalarGridSpec(
            num_scalar_prefetch=1, grid=(pairs, tiles),
            in_specs=[pl.BlockSpec((rows, wide), lambda p, t, n: (0, p)),
                      pl.BlockSpec((tile, wide), lambda p, t, n: (t, p)),
                      pl.BlockSpec((tile, wide), lambda p, t, n: (t, p))],
            out_specs=[pl.BlockSpec((rows, wide), lambda p, t, n: (0, p)),
                       pl.BlockSpec((1, 1, 2 * rows), lambda p, t, n: (p, 0, 0))],
            scratch_shapes=[pltpu.VMEM((2 * rows, 1), jnp.float32), pltpu.VMEM((2 * rows, 1), jnp.float32), pltpu.VMEM((2 * rows, wide), jnp.float32)]),
        out_shape=[jax.ShapeDtypeStruct((rows, width), jnp.float32), jax.ShapeDtypeStruct((pairs, 1, 2 * rows), jnp.float32)],
        name="attend",
    )(length, q, k, v)

def backward_math(half, length, start, q, k, v, g, o, lse):
    q2, g2 = pair_stack(q, half), pair_stack(g, half)
    delta = jnp.sum(jnp.transpose(pair_stack(f32(g) * o, half)), axis=0, keepdims=True)
    s = nt(k, q2)
    row = lax.broadcasted_iota(jnp.int32, (s.shape[0], 1), 0) + start
    p = jnp.where(row < length, jnp.exp(s - lse), 0.0)
    ds = (p * (nt(v, g2) - delta)).astype(jnp.bfloat16)
    return tn(ds, k), nn(ds, q2), nn(p.astype(jnp.bfloat16), g2)

def backward_kernel(half, tiles, scale, len_ref, q_ref, k_ref, v_ref, g_ref, o_ref, lse_ref, dq_ref, dk_ref, dv_ref, sum_ref, acc_ref):
    t = pl.program_id(1)
    dq, dk, dv = backward_math(half, len_ref[0], t * k_ref.shape[0], q_ref[...], k_ref[...], v_ref[...], g_ref[...], o_ref[...], lse_ref[0])
    dk_ref[...] = dk.astype(jnp.bfloat16)
    dv_ref[...] = dv.astype(jnp.bfloat16)
    sums = jnp.sum(dv, axis=0, keepdims=True)
    sum_ref[0] = sums + jnp.where(t == 0, 0.0, sum_ref[0]) if tiles > 1 else sums
    if tiles > 1:
        dq = dq + jnp.where(t == 0, 0.0, acc_ref[...])
        acc_ref[...] = dq
    @pl.when(t == tiles - 1)
    def _():
        dq_ref[...] = (pair_join(dq, half) * scale).astype(jnp.bfloat16)

def attend_back(q, k, v, g, o, lse, length, heads, tile):
    rows, width = q.shape
    size = width // heads
    total, pairs = k.shape[0], heads // 2
    tiles = total // tile
    wide = 2 * size
    R = pl.BlockSpec((rows, wide), lambda p, t, n: (0, p))
    K = pl.BlockSpec((tile, wide), lambda p, t, n: (t, p))
    return pl.pallas_call(
        functools.partial(backward_kernel, size, tiles, size ** -0.5),
        grid_spec=pltpu.PrefetchScalarGridSpec(
            num_scalar_prefetch=1, grid=(pairs, tiles),
            in_specs=[R, K, K, R, R, pl.BlockSpec((1, 1, 2 * rows), lambda p, t, n: (p, 0, 0))],
            out_specs=[R, K, K, pl.BlockSpec((1, 1, wide), lambda p, t, n: (p, 0, 0))],
            scratch_shapes=[pltpu.VMEM((2 * rows, wide), jnp.float32)]),
        out_shape=[jax.ShapeDtypeStruct((rows, width), jnp.bfloat16)] + [jax.ShapeDtypeStruct((total, width), jnp.bfloat16)] * 2 + [jax.ShapeDtypeStruct((pairs, 1, wide), jnp.float32)],
        name="attend_back",
    )(length, q, k, v, g, o, lse)
ORDER = ("du", "pA", "ld", "d1,*", "As", "A1,*", "dv", "pB", "Bs", "B1,*", "d2,*", "e", "A4,*", "B4,d3,*", "g", "qs", "q1,*", "q2,*", "d4,*", "i", "q3,*", "q4,*")

def settle_kernel(grid, size, *refs):
    length, key_all, value_all, g_out, g_in, g_back, w_qkv, q, g, o, lse, x, base, g_bias, g_vec = refs[:15]
    d_qkv, d_out, d_in, d_back, d_bias, d_vec, grad_inputs = refs[15:22]
    own_key, own_value, w_query, w_key, w_value, grads, k_slots, v_slots, wide_w, vec_cols, vec_src, kA, vA, kB, vB = refs[22:37]
    kv_sem, w_sem, local = refs[37:40]
    mine = refs[40:43]
    bufs = refs[43:]
    rows, width = x.shape
    third, pair, pairs = width // 2, 2 * size, width // (2 * size)
    def pull(p):
        at = pl.multiple_of(p * pair, pair)
        return [pltpu.make_async_copy(src.at[:, pl.ds(at, pair)], slots.at[lax.rem(p, 2)], kv_sem.at[n, lax.rem(p, 2)])
                for n, (src, slots) in enumerate(((key_all, k_slots), (value_all, v_slots)))]
    for copy in pull(0): copy.start()
    greet(grid, True)
    cut = lambda n: d_qkv.at[:, :, pl.ds(n * width, width)]
    part_of = lambda ref, n: ref.at[:, :, pl.ds(n * third, third)]
    specs = [("A", vA, part_of(own_value, 0), "zy"), ("A", kA, part_of(own_key, 0), "zy"), ("B", vB, part_of(own_value, 1), "zy"), ("B", kB, part_of(own_key, 1), "zy"),
             ("d", g_back, d_back, "zyx"), ("d", g_in, d_in, "zyx"), ("d", g_out, d_out, "zyx"), ("d", g_bias, d_bias, "zyx"),
             ("q", vec_src, d_vec, "zyx"), ("q", w_query, cut(0), "zyx"), ("q", w_key, cut(1), "zyx"), ("q", w_value, cut(2), "zxy")]
    jobs = {"A": [], "B": [], "d": [], "q": []}
    for n, (group, src, out, order) in enumerate(specs):
        r = bufs[10 * n:10 * n + 10]
        extra = (mine[n - 4], local.at[n - 4]) if 4 <= n < 7 else ()
        jobs[group].append(Scatter(grid, src, out, r[:4], r[4], r[5], r[6:10], order, *extra))
    big = jobs["d"][:3]
    def weigh(at, dst):
        part, wide = dst.shape[1], width // 2
        for n in range(2):
            full = tn(x[...], grads[:, at + n * wide:at + (n + 1) * wide])
            for k in range(dst.shape[0]):
                dst[k, :, n * wide:(n + 1) * wide] = full[k * part:(k + 1) * part].astype(dst.dtype)
    lane = lax.broadcasted_iota(jnp.int32, (pair, 128), 1)
    def attention(first, dk, dv):
        def one(j, _):
            p = first + j
            slot = lax.rem(p, 2)
            @pl.when(p + 1 < pairs)
            def _():
                for copy in pull(p + 1): copy.start()
            for copy in pull(p): copy.wait()
            at = pl.ds(pl.multiple_of(p * pair, pair), pair)
            to = pl.ds(pl.multiple_of(j * pair, pair), pair)
            dq, dk_part, dv_part = backward_math(size, length[0], 0, q[:, at], k_slots[slot], v_slots[slot], g[:, at], o[:, at], lse[p])
            dk[:, :, to] = dk_part.astype(dk.dtype).reshape(dk.shape[0], rows, pair)
            dv[:, :, to] = dv_part.astype(dv.dtype).reshape(dv.shape[0], rows, pair)
            dq = (pair_join(dq, size) * size ** -0.5).astype(grads.dtype)
            grads[:, at] = dq
            tall = lambda v: jnp.transpose(jnp.broadcast_to(jnp.sum(f32(v), axis=0, keepdims=True), (128, pair)))
            vec_cols[at, :] = jnp.where(lane == 0, tall(dq), jnp.where(lane == 1, tall(dv_part), g_vec[at, :]))
            return _
        lax.fori_loop(0, pairs // 2, one, None)
    def early():
        weigh(0, w_query)
        part = vec_src.shape[1]
        for k in range(vec_src.shape[0]):
            vec_src[k] = vec_cols[k * part:(k + 1) * part]
    def after():
        grads[:, width:2 * width] = own_key[0].astype(grads.dtype)
        grads[:, 2 * width:] = own_value[0].astype(grads.dtype)
        weigh(width, w_key)
        weigh(2 * width, w_value)
    def inward():
        total = base[...]
        for n in range(3):
            copy = pltpu.make_async_copy(w_qkv.at[:, pl.ds(n * width, width)], wide_w, w_sem)
            copy.start()
            copy.wait()
            total = total + nt(grads[:, n * width:(n + 1) * width], wide_w[...])
        grad_inputs[...] = total
    alone = {"pA": lambda: attention(0, kA, vA), "pB": lambda: attention(pairs // 2, kB, vB), "e": early, "g": after, "i": inward,
             "ld": lambda: [job.loaded() for job in big]}
    def step(word, d):
        for job in jobs[word[0]]:
            if word[1] in "su":
                if job.mine is not None: job.load()
                job.start(slice(None, None if word[1] == "s" else 1))
            elif word[1] == "v": job.start(slice(1, None))
            elif word[1] == "1": job.stage1(job.combos()[0], d)
            elif word[1] == "2": job.stage1((1, 0), d)
            elif word[1] == "3": job.stage2(d)
            elif d is None: job.total()
            else: job.chain(d)
    for phase in ORDER:
        words = phase.split(",")
        if phase in alone: alone[phase]()
        elif words[-1] == "*":
            def loop(k, _, words=words):
                for word in words[:-1]: step(word, grid.depth - 1 - k)
                return _
            lax.fori_loop(0, grid.depth - 1, loop, None)
            for word in words[:-1]: step(word, None)
        else:
            for word in words: step(word, None)
    for group in "ABdq":
        for job in jobs[group]: job.finish()

def settle(grid, size, length, key_all, value_all, g_out, g_in, g_back, w_qkv, q, g, o, lse, x, base, g_bias, g_vec):
    bf, f4 = jnp.bfloat16, jnp.float32
    rows, width = x.shape
    part, devices = g_out.shape[1], grid.seqs * grid.ctx
    slots, pair = key_all.shape[0], 2 * size
    S = jax.ShapeDtypeStruct
    V, A = pl.BlockSpec(memory_space=pltpu.VMEM), pl.BlockSpec(memory_space=pl.ANY)
    D, M = pltpu.SemaphoreType.DMA, pltpu.VMEM
    scratch = [M((1, rows, width), f4)] * 2 + [M((devices, part, width), bf)] * 3 + [M((rows, 3 * width), bf)] + [M((2, slots, pair), bf)] * 2
    scratch += [M((width, width), bf), M((width, 128), f4), M((devices, part, 128), f4)] + [M((grid.ctx, rows, width // 2), bf)] * 4
    scratch += [D((2, 2)), D(()), D((3,))] + [M((devices // 2,) + a.shape[1:], bf) for a in (g_back, g_in, g_out)]
    for shape, dtype, order in ([((rows, width // 2), bf, "zy")] * 4 + [(a.shape[1:], a.dtype, "zyx") for a in (g_back, g_in, g_out, g_bias)]
                                + [((part, 128), f4, "zyx"), ((part, width), bf, "zyx"), ((part, width), bf, "zyx"), ((part, width), bf, "zxy")]):
        scratch += scatter_scratch(grid, shape, dtype, order)
    one = lambda a: S((1,) + a.shape[1:], f4)
    return pl.pallas_call(
        functools.partial(settle_kernel, grid, size),
        out_shape=[S((1, part, 3 * width), f4), one(g_out), one(g_in), one(g_back), one(g_bias), S((1, part, 128), f4), S((rows, width), f4)],
        in_specs=[pl.BlockSpec(memory_space=pltpu.SMEM)] + [A] * 6 + [V] * 8, out_specs=[V] * 7, scratch_shapes=scratch,
        compiler_params=pltpu.CompilerParams(collective_id=1, has_side_effects=True, vmem_limit_bytes=63 * 2**20),
        name="settle",
    )(length, key_all, value_all, g_out, g_in, g_back, w_qkv, q, g, o, lse, x, base, g_bias, g_vec)

HEADS = 12
EPSILON = 1e-12

def normalize(u):
    mean = jnp.mean(u, axis=-1, keepdims=True)
    centred = u - mean
    r = lax.rsqrt(jnp.mean(centred * centred, axis=-1, keepdims=True) + EPSILON)
    return centred * r, r

def normalize_back(e, n, r, gain):
    c = e * gain
    return r * (c - jnp.mean(c, axis=-1, keepdims=True) - n * jnp.mean(c * n, axis=-1, keepdims=True))

def gelu_parts(v):
    cdf = 0.5 * (1.0 + lax.erf(v * (0.5 ** 0.5)))
    slope = cdf + v * jnp.exp(-0.5 * v * v) * ((2 * jnp.pi) ** -0.5)
    return v * cdf, slope

def layer_kernel(grid, length, w_out_hbm, w_in_hbm, w_back_hbm, attended_ref, x, cotangent, vec_all, bias_all,
                 g_out_hbm, g_in_hbm, g_back_hbm, result, grad_attended, base, g_bias, g_vec,
                 w_out, w_in, w_back, g_out, g_in, g_back, bias, in_sem, out_sem):
    bf = jnp.bfloat16
    loads = [pltpu.make_async_copy(src, dst, in_sem.at[n]) for n, (src, dst) in enumerate(((w_out_hbm, w_out), (w_in_hbm, w_in), (w_back_hbm, w_back)))]
    for copy in loads: copy.start()
    stores = [pltpu.make_async_copy(src, dst, out_sem.at[n]) for n, (src, dst) in enumerate(((g_out, g_out_hbm), (g_in, g_in_hbm), (g_back, g_back_hbm)))]
    rows, width = x.shape
    devices, part_ff = g_back.shape[:2]
    part = g_in.shape[1]
    lane = lax.broadcasted_iota(jnp.int32, (16, 128), 1)
    pick = (lane == lax.broadcasted_iota(jnp.int32, (16, 128), 0)).astype(bf)
    vec = nt(pick, vec_all[...])
    for k in range(devices):
        bias[0:1, k * part_ff:(k + 1) * part_ff] = f32(bias_all[k])[0:1, :part_ff]
    attended = attended_ref[...].astype(bf)
    loads[0].wait()
    branch = nn(attended, w_out[...]) + vec[2:3]
    norm_one, r_one = normalize(f32(x[...]) + branch)
    first = norm_one * vec[3:4] + vec[4:5]
    first_low = first.astype(bf)
    loads[1].wait()
    hidden = nn(first_low, w_in[...]) + bias[0:1]
    active_f, slope = gelu_parts(hidden)
    active = active_f.astype(bf)
    loads[2].wait()
    second = nn(active, w_back[...]) + vec[5:6]
    norm_two, r_two = normalize(first + second)
    result[...] = (norm_two * vec[6:7] + vec[7:8]).astype(bf)
    slot = lax.broadcasted_iota(jnp.int32, (rows, 1), 0) + lax.axis_index("ctx") * rows
    grad_result = jnp.where(slot < length[0], f32(cotangent[...]), 0.0)
    grad_second = normalize_back(grad_result, norm_two, r_two, vec[6:7])
    grad_second_low = grad_second.astype(bf)
    grad_hidden_f = nt(grad_second_low, w_back[...]) * slope
    grad_hidden = grad_hidden_f.astype(bf)
    for n in range(devices * part_ff // width):
        full = tn(active[:, n * width:(n + 1) * width], grad_second_low).astype(bf)
        for k in range(width // part_ff):
            g_back[n * (width // part_ff) + k] = full[k * part_ff:(k + 1) * part_ff]
    stores[2].start()
    for n in range(devices * part_ff // width):
        full = tn(first_low, grad_hidden[:, n * width:(n + 1) * width])
        for k in range(devices):
            g_in[k, :, n * width:(n + 1) * width] = full[k * part:(k + 1) * part].astype(bf)
    stores[1].start()
    grad_first = grad_second + nt(grad_hidden, w_in[...])
    grad_branch_full = normalize_back(grad_first, norm_one, r_one, vec[3:4])
    base[...] = grad_branch_full
    grad_branch = grad_branch_full.astype(bf)
    grad_attended[...] = nt(grad_branch, w_out[...]).astype(bf)
    full = tn(attended, grad_branch)
    for k in range(devices):
        g_out[k] = full[k * part:(k + 1) * part].astype(bf)
    stores[0].start()
    total = lambda a: jnp.sum(f32(a), axis=0, keepdims=True)
    sums = total(grad_hidden)
    g_bias[...] = jnp.zeros_like(g_bias)
    for k in range(devices):
        g_bias[k, 0:1, 0:part_ff] = sums[:, k * part_ff:(k + 1) * part_ff]
    stack = jnp.concatenate((jnp.zeros((2, width), jnp.float32), total(grad_branch), total(grad_first * norm_one), total(grad_first),
                             total(grad_second_low), total(grad_result * norm_two), total(grad_result), jnp.zeros((120, width), jnp.float32)), axis=0)
    for n in range(width // 128):
        g_vec[n * 128:(n + 1) * 128, :] = jnp.transpose(stack[:, n * 128:(n + 1) * 128])
    for copy in stores: copy.wait()

def layer(grid, length, w_out, w_in, w_back, attended, x, cotangent, vec_all, bias_all):
    bf, f4 = jnp.bfloat16, jnp.float32
    rows, width = x.shape
    hidden = w_in.shape[1]
    devices = grid.seqs * grid.ctx
    S, M, D = jax.ShapeDtypeStruct, pltpu.VMEM, pltpu.SemaphoreType.DMA
    V, A = pl.BlockSpec(memory_space=pltpu.VMEM), pl.BlockSpec(memory_space=pl.ANY)
    grads = [(devices, width // devices, width), (devices, width // devices, hidden), (devices, hidden // devices, width)]
    return pl.pallas_call(
        functools.partial(layer_kernel, grid),
        out_shape=[S(g, bf) for g in grads] + [S((rows, width), bf), S((rows, width), bf), S((rows, width), f4), S((devices, 8, 128), f4), S((width, 128), f4)],
        in_specs=[pl.BlockSpec(memory_space=pltpu.SMEM)] + [A] * 3 + [V] * 5, out_specs=[A] * 3 + [V] * 5,
        scratch_shapes=[M(w.shape, bf) for w in (w_out, w_in, w_back)] + [M(g, bf) for g in grads] + [M((8, hidden), f4), D((3,)), D((3,))],
        compiler_params=pltpu.CompilerParams(vmem_limit_bytes=60 * 2**20),
        name="layer",
    )(length, w_out, w_in, w_back, attended, x, cotangent, vec_all, bias_all)

def deliver_kernel(*refs):
    n = len(refs) // 2
    for k, (src, dst) in enumerate(zip(refs[:n], refs[n:])):
        if k == 0:
            tall = jnp.concatenate((src[0], jnp.zeros((128 - src.shape[1], 128), jnp.float32)), axis=0)
            dst[...] = jnp.transpose(tall)[:dst.shape[0], :dst.shape[1]]
        elif len(dst.shape) == 3: dst[0] = src[...]
        else: dst[...] = src[0, :dst.shape[0], :dst.shape[1]]

def deliver(arrays, shapes):
    V = pl.BlockSpec(memory_space=pltpu.VMEM)
    return pl.pallas_call(
        deliver_kernel, out_shape=[jax.ShapeDtypeStruct(s, jnp.float32) for s in shapes],
        in_specs=[V] * len(arrays), out_specs=[V] * len(arrays), name="deliver",
    )(*arrays)

def per_device(grid, inputs, lengths, cotangent, w_qkv, w_out, w_in, w_back, vectors, ffn_bias):
    bf, f4 = jnp.bfloat16, jnp.float32
    rows_in = inputs[0]
    rows, width = rows_in.shape
    hidden_size = w_in.shape[1]
    devices = grid.seqs * grid.ctx
    part, part_ff = w_qkv.shape[0], w_back.shape[0]
    slots = grid.ctx * rows
    scale = (width // HEADS) ** -0.5

    half = 3 * width // 2
    whole = grid.depth <= 4 and part % 8 == 0 and part_ff <= 128
    if whole:
        qkv_full, vec_all, bias_all, out_all, in_all, back_all, key_all, value_all, query_scaled, attended_f, lse = fetch(
            grid, width // HEADS, lengths, rows_in, w_qkv, vectors.T, ffn_bias[None], w_out[None], w_in[None], w_back[None])
        out_full, in_full, back_full = out_all.reshape(width, width), in_all.reshape(width, hidden_size), back_all.reshape(hidden_size, width)
    else:
        everywhere = lambda a: lax.all_gather(a, ("seq", "ctx"), axis=0, tiled=True)
        qkv_full, out_full, in_full, back_full = everywhere(w_qkv), everywhere(w_out), everywhere(w_in), everywhere(w_back)
        vec = everywhere(vectors).T.astype(f4)
        ffn_full = everywhere(ffn_bias)[None].astype(f4)
        projected = jnp.dot(rows_in, qkv_full, preferred_element_type=f4)
        query_scaled = (projected[:, :width] + vec[0]).astype(bf) * jnp.asarray(scale, bf)
        key = projected[:, width:2 * width].astype(bf)
        value = (projected[:, 2 * width:] + vec[1]).astype(bf)
        key_all, value_all = (lax.all_gather(a, "ctx", axis=0, tiled=True) for a in (key, value))

    if whole:
        g_out, g_in, g_back, result, grad_attended, base, g_bias, g_vec = layer(
            grid, lengths, out_full, in_full, back_full, attended_f, rows_in, cotangent[0], vec_all, bias_all)
        d_qkv, d_out, d_in, d_back, d_bias, d_vec, grad_inputs = settle(
            grid, width // HEADS, lengths, key_all, value_all, g_out, g_in, g_back, qkv_full, query_scaled, grad_attended, attended_f, lse, rows_in, base, g_bias, g_vec)
        d_vec, grad_inputs, d_qkv, d_out, d_in, d_back, d_bias = deliver(
            (d_vec, grad_inputs, d_qkv, d_out, d_in, d_back, d_bias),
            ((8, part), (1, rows, width), (part, 3 * width), (part, width), (part, hidden_size), (part_ff, width), (1, part_ff)))
        return (result[None], grad_inputs, d_qkv, d_out, d_in, d_back, d_vec.T, d_bias[0])
    tile = min(slots, 2048)
    attended_f, lse = attend(query_scaled, key_all, value_all, lengths, HEADS, tile)
    attended = attended_f.astype(bf)
    branch = jnp.dot(attended, out_full, preferred_element_type=f4) + vec[2]
    norm_one, r_one = normalize(rows_in.astype(f4) + branch)
    first = norm_one * vec[3] + vec[4]
    first_low = first.astype(bf)
    hidden = jnp.dot(first_low, in_full, preferred_element_type=f4) + ffn_full
    active_f, slope = gelu_parts(hidden)
    active = active_f.astype(bf)
    second = jnp.dot(active, back_full, preferred_element_type=f4) + vec[5]
    norm_two, r_two = normalize(first + second)
    result = (norm_two * vec[6] + vec[7]).astype(bf)
    start = lax.axis_index("ctx") * rows
    valid = (start + jnp.arange(rows, dtype=jnp.int32) < lengths[0]).astype(f4)[:, None]
    grad_result = cotangent[0].astype(f4) * valid
    grad_second = normalize_back(grad_result, norm_two, r_two, vec[6])
    grad_second_low = grad_second.astype(bf)
    grad_active = lax.dot_general(grad_second_low, back_full, (((1,), (1,)), ((), ())), preferred_element_type=f4)
    grad_hidden = (grad_active * slope).astype(bf)
    grad_first = grad_second + lax.dot_general(grad_hidden, in_full, (((1,), (1,)), ((), ())), preferred_element_type=f4)
    grad_branch_full = normalize_back(grad_first, norm_one, r_one, vec[3])
    grad_branch = grad_branch_full.astype(bf)
    grad_attended = lax.dot_general(grad_branch, out_full, (((1,), (1,)), ((), ())), preferred_element_type=f4).astype(bf)

    def outer(a, b):
        return lax.dot_general(a, b, (((0,), (0,)), ((), ())), preferred_element_type=f4).astype(bf)
    g_back = outer(active, grad_second_low)
    g_in = outer(first_low, grad_hidden)
    g_out = outer(attended, grad_branch)
    grad_ffn = jnp.sum(grad_hidden.astype(f4), axis=0)
    sums = (jnp.sum(grad_branch.astype(f4), axis=0), jnp.sum(grad_first * norm_one, axis=0), jnp.sum(grad_first, axis=0),
            jnp.sum(grad_second_low.astype(f4), axis=0), jnp.sum(grad_result * norm_two, axis=0), jnp.sum(grad_result, axis=0))
    grad_query, g_key, g_value, sum_value = attend_back(query_scaled, key_all, value_all, grad_attended, attended_f, lse, lengths, HEADS, tile)
    sums = jnp.stack((jnp.sum(grad_query.astype(f4), axis=0), sum_value.reshape(width)) + sums)
    home = lambda a, axes: lax.psum_scatter(a.astype(f4), axes, scatter_dimension=0, tiled=True)
    own_key, own_value = (home(a, "ctx").astype(bf) for a in (g_key, g_value))
    grad_projected = jnp.concatenate((grad_query, own_key, own_value), axis=1)
    grad_inputs = grad_branch_full + lax.dot_general(grad_projected, qkv_full, (((1,), (1,)), ((), ())), preferred_element_type=f4)
    both = ("seq", "ctx")
    return (result[None], grad_inputs[None], home(outer(rows_in, grad_projected), both), home(g_out, both), home(g_in, both), home(g_back, both),
            home(sums.T, both), home(grad_ffn, both))

def solution(mesh):
    grid = Grid(mesh.shape["seq"], mesh.shape["ctx"])
    split, both = P("seq", "ctx", None), P(("seq", "ctx"), None)
    return jax.shard_map(
        functools.partial(per_device, grid), mesh=mesh,
        in_specs=(split, P("seq"), split, both, both, both, both, both, P(("seq", "ctx"))),
        out_specs=(split, split, both, both, both, both, both, P(("seq", "ctx"))),
        check_vma=False,
    )
```

```python
import functools, math
import jax, jax.numpy as jnp
from jax import lax
from jax.experimental import pallas as pl
from jax.experimental.pallas import tpu as pltpu

MESH = pl.DeviceIdType.MESH

class Grid:
    def __init__(self, seqs, ctx):
        self.seqs, self.ctx = seqs, ctx
        self.depth = ctx // 4
    def here(self):
        s, i = lax.axis_index("seq"), lax.axis_index("ctx")
        return s, i // 4, (i // 2) % 2, i % 2

def cid(z, y, c):
    return (z * 2 + y) * 2 + c

def greet(grid, with_seq):
    s, z, y, c = grid.here()
    bar = pltpu.get_barrier_semaphore()
    def hello(p):
        pl.semaphore_signal(bar, inc=1, device_id=p, device_id_type=MESH)
    peers = [(s, cid(z, 1 - y, c)), (s, cid(z, y, 1 - c))]
    if with_seq:
        peers += [(1 - s, cid(z, y, c))]
    for p in peers:
        hello(p)
    @pl.when(z > 0)
    def _():
        hello((s, cid(z - 1, y, c)))
    @pl.when(z < grid.depth - 1)
    def _():
        hello((s, cid(z + 1, y, c)))
    ends = jnp.where(z > 0, 1, 0) + jnp.where(z < grid.depth - 1, 1, 0)
    pl.semaphore_wait(bar, len(peers) + ends)

def each(n, body):
    if n <= 4:
        for k in range(n):
            body(k)
    else:
        lax.fori_loop(0, n, lambda k, _: (body(k), None)[1], None)

class Gather:
    def __init__(self, grid, src, dst, sems, order, cols=None):
        self.g, self.src, self.dst = grid, src, dst
        self.send, self.zsend, self.recv, self.local = sems
        self.order, self.cols = order, cols
        self.s, self.z, self.y, self.c = grid.here()
        self.early = order[0] == 'y'
        self.rest = 'x' if self.early else order[1:]
    def rows(self, start, n):
        if len(self.dst.shape) == 3:
            return self.dst.at[start] if n is None else self.dst.at[pl.ds(start, n)]
        size = self.src.shape[-2]
        span = pl.ds(pl.multiple_of(start * size, 8), size * (n or 1))
        return self.dst.at[span] if self.cols is None else self.dst.at[span, self.cols]
    def view(self, b):
        return self.rows(b, None)
    def own(self):
        src = self.src.at[0] if len(self.src.shape) == 3 else self.src
        return src if self.cols is None else src.at[:, self.cols]
    def push(self, src, b, dev, sem):
        pltpu.make_async_remote_copy(src, self.view(b), sem, self.recv.at[b], device_id=dev, device_id_type=MESH).start()
    def wait(self, b, sem=None):
        v = self.view(b)
        pltpu.make_async_copy(v, v, self.recv.at[b] if sem is None else sem).wait()
    def dev(self, dim):
        if dim == 'x': return (1 - self.s, cid(self.z, self.y, self.c))
        if dim == 'y': return (self.s, cid(self.z, 1 - self.y, self.c))
        if dim == 'c': return (self.s, cid(self.z, self.y, 1 - self.c))
        return (self.s, cid(self.z + (1 if dim == '+' else -1), self.y, self.c))
    def at(self, flips, z):
        s = 1 - self.s if 'x' in flips else self.s
        y = 1 - self.y if 'y' in flips else self.y
        c = 1 - self.c if 'c' in flips else self.c
        return cid(z, y, c) + (s * self.g.ctx if 'x' in self.order else 0)
    def zpush(self, src, b, z, side, f=''):
        ok = self.z < self.g.depth - 1 if side == '+' else self.z > 0
        @pl.when(ok)
        def _():
            self.push(src, b, self.dev(side), self.zsend.at[0 if side == '+' else 1, z + (self.g.depth if f else 0)])
    def start(self):
        own = self.at('', self.z)
        if self.early:
            self.push(self.own(), own, self.dev('y'), self.send)
        for side in '+-':
            self.zpush(self.own(), own, self.z, side)
        for dim in self.rest + 'c':
            self.push(self.own(), own, self.dev(dim), self.send)
        pltpu.make_async_copy(self.own(), self.view(own), self.local).start()
    def sides(self, d, body):
        if isinstance(d, int) and d == 0:
            body(self.z, '')
            return
        @pl.when(self.z - d >= 0)
        def _():
            body(self.z - d, '-')
        @pl.when(self.z + d < self.g.depth)
        def _():
            body(self.z + d, '+')
    def line(self, d, f=''):
        def go(z, side):
            b = self.at(f, z)
            self.wait(b)
            for way in '+-':
                if way != side:
                    self.zpush(self.view(b), b, z, way, f)
            for k in self.rest + 'c':
                self.push(self.view(b), b, self.dev(k), self.send)
        self.sides(d, go)
    def cross(self, flips, dims, d):
        def go(z, side):
            b = self.at(flips, z)
            self.wait(b)
            for k in dims:
                self.push(self.view(b), b, self.dev(k), self.send)
        self.sides(d, go)
    def step(self, t):
        r = self.rest
        if self.early:
            if t < self.g.depth:
                self.line(t)
            if t <= self.g.depth:
                self.line(t - 1, 'y')
                self.cross('x', 'c', t - 1)
            if 2 <= t <= self.g.depth + 1:
                self.cross('yx', 'c', t - 2)
            return
        if t < self.g.depth:
            self.line(t)
        if 1 <= t <= self.g.depth:
            self.cross(r[0], r[1:] + 'c', t - 1)
        if len(r) > 1:
            if 1 <= t <= self.g.depth:
                self.cross(r[1], 'c', t - 1)
            if 2 <= t <= self.g.depth + 1:
                self.cross(r, 'c', t - 2)
    def steps(self):
        return self.g.depth + len(self.order) - 1
    def arrive(self):
        r = 'yx' if self.early else self.rest
        sets = ['', r[0]] + ([r[1], r] if len(r) > 1 else [])
        for f in sets:
            def go(k, f=f):
                self.wait(self.at(f + 'c', k))
            each(self.g.depth, go)
        self.wait(self.at('', self.z), self.local)
    def leave(self):
        def sent(k):
            for side in '+-':
                n = 0 if side == '+' else 1
                ok = (jnp.logical_and(self.z < self.g.depth - 1, k <= self.z) if side == '+'
                      else jnp.logical_and(self.z > 0, k >= self.z))
                @pl.when(ok)
                def _():
                    for f in ('', 'y') if self.early else ('',):
                        self.wait(self.at(f, k), self.zsend.at[n, k + (self.g.depth if f else 0)])
        each(self.g.depth, sent)
        p = self.g.depth
        n = 6 * p + 1 if self.early else p + (2 * p + 4 * p if len(self.rest) > 1 else 2 * p)
        v = self.rows(0, n)
        pltpu.make_async_copy(v, v, self.send).wait()

WAYS = ("yzx", "zyx")
PLAN = ("q0", "q1", "q2", "q3", "w0", "q4", "w1", "q5", "qa", "k0", "qq", "k1", "l0", "w2", "k2", "l1", "w3", "k3", "l2", "k4", "w4", "ka", "l3", "p0", "l4", "la", "p1", "w5", "wa")

def fetch_kernel(grid, size, *refs):
    length, x, w_qkv, vec_rows, bias_row, w_out, w_in, w_back = refs[:8]
    qkv_all, vec_all, bias_all, out_all, in_all, back_all, key_all, value_all, query, attended, lse = refs[8:19]
    key, value, k_slots, v_slots, vec, w_bias, room, kv_sem = refs[19:27]
    sems = refs[27:]
    part, part_ff = vec.shape[0], bias_row.shape[1]
    room[...] = jnp.zeros_like(room)
    room[0:8, 0:part] = f32(vec_rows[...])
    vec[...] = jnp.transpose(room[...])[0:part].astype(vec.dtype)
    room[0:1, 0:part_ff] = f32(bias_row[...])
    w_bias[0] = room[0:8, :].astype(w_bias.dtype)
    greet(grid, True)
    pair, pairs = 2 * size, x.shape[1] // (2 * size)
    def pull(p):
        at = pl.multiple_of(p * pair, pair)
        return [pltpu.make_async_copy(src.at[:, pl.ds(at, pair)], slots.at[lax.rem(p, 2)], kv_sem.at[n, lax.rem(p, 2)])
                for n, (src, slots) in enumerate(((key_all, k_slots), (value_all, v_slots)))]
    def attention(first):
        def one(j, _):
            p = first + j
            slot = lax.rem(p, 2)
            @pl.when(j + 1 < pairs // 2)
            def _():
                for copy in pull(p + 1): copy.start()
            for copy in pull(p): copy.wait()
            at = pl.ds(pl.multiple_of(p * pair, pair), pair)
            attended[:, at], lse[p] = forward_math(size, length[0], query[:, at], k_slots[slot], v_slots[slot])
            return _
        lax.fori_loop(0, pairs // 2, one, None)
    def job(i, src, dst, order, cols=None):
        return Gather(grid, src, dst, [r.at[i] for r in sems], order, cols)
    width = x.shape[1]
    half = 3 * width // 2
    parts = {
        "q": [job(0, vec, vec_all, "zyx"), job(1, w_qkv, qkv_all, "zyx", pl.ds(0, half)), job(2, w_qkv, qkv_all, "zxy", pl.ds(half, half))],
        "w": [job(3, w_bias, bias_all, "zyx"), job(4, w_out, out_all, "zyx"), job(5, w_in, in_all, WAYS[0]), job(6, w_back, back_all, WAYS[1])],
        "k": [job(7, key, key_all, "zy", pl.ds(0, width // 2)), job(8, value, value_all, "zy", pl.ds(0, width // 2))],
        "l": [job(9, key, key_all, "zy", pl.ds(width // 2, width // 2)), job(10, value, value_all, "zy", pl.ds(width // 2, width // 2))]}
    for word in PLAN:
        if word[0] == "p":
            first = int(word[1]) * (pairs // 2)
            for copy in pull(first): copy.start()
            attention(first)
            continue
        if word == "qq":
            q = (nn(x[...], qkv_all[:, :width]) + rows[0:1]).astype(jnp.bfloat16)
            query[...] = q * jnp.asarray(size ** -0.5, jnp.bfloat16)
            continue
        jobs, t = parts[word[0]], word[1]
        for j in jobs:
            if t == "a": j.arrive()
            elif t == "0": j.start()
            else: j.step(int(t))
        if word == "qa":
            lane = lax.broadcasted_iota(jnp.int32, (16, 128), 1)
            pick = (lane == lax.broadcasted_iota(jnp.int32, (16, 128), 0)).astype(jnp.bfloat16)
            rows = nt(pick, vec_all[...])
            key[...] = nn(x[...], qkv_all[:, width:2 * width]).astype(jnp.bfloat16)
            value[...] = (nn(x[...], qkv_all[:, 2 * width:]) + rows[1:2]).astype(jnp.bfloat16)
    for j in parts["q"] + parts["k"] + parts["l"] + parts["w"]:
        j.leave()

def fetch(grid, size, length, x, w_qkv, vec_rows, bias_row, w_out, w_in, w_back):
    devices, bf = grid.seqs * grid.ctx, jnp.bfloat16
    rows, width = x.shape
    S = jax.ShapeDtypeStruct
    V, A = pl.BlockSpec(memory_space=pltpu.VMEM), pl.BlockSpec(memory_space=pl.ANY)
    D = pltpu.SemaphoreType.DMA
    flat = lambda a: S((devices * a.shape[-2], a.shape[-1]), bf)
    deep = lambda a: S((devices,) + a.shape[1:], bf)
    kv = S((grid.ctx * rows, width), bf)
    return pl.pallas_call(
        functools.partial(fetch_kernel, grid, size),
        out_shape=[flat(w_qkv), S((width, 128), bf), S((devices, 8, 128), bf), deep(w_out), deep(w_in), deep(w_back), kv, kv, S((rows, width), bf),
                   S((rows, width), jnp.float32), S((width // (2 * size), 1, 2 * rows), jnp.float32)],
        in_specs=[pl.BlockSpec(memory_space=pltpu.SMEM)] + [V] * 7,
        out_specs=[V, V] + [A] * 6 + [V] * 3,
        scratch_shapes=[pltpu.VMEM((rows, width), bf)] * 2 + [pltpu.VMEM((2, grid.ctx * rows, 2 * size), bf)] * 2
                       + [pltpu.VMEM((width // devices, 128), bf), pltpu.VMEM((1, 8, 128), bf), pltpu.VMEM((128, 128), jnp.float32)] + [D((2, 2)), D((11,)), D((11, 2, 2 * grid.depth)), D((11, devices)), D((11,))],
        compiler_params=pltpu.CompilerParams(collective_id=0, has_side_effects=True, vmem_limit_bytes=60 * 2**20),
        name="fetch",
    )(length, x, w_qkv, vec_rows, bias_row, w_out, w_in, w_back)
from jax.sharding import PartitionSpec as P

def f32(x):
    return x.astype(jnp.float32)

class Scatter:
    def __init__(self, grid, src, out, bufs, send, zsend, recvs, order, mine=None, local=None):
        self.g, self.src, self.out, self.mine, self.local = grid, src, out, mine, local
        self.bufc, self.buf1, self.buf2, self.bufz = bufs
        self.send, self.zsend, self.order = send, zsend, order
        self.rc, self.r1, self.r2, self.rz = recvs
        self.dims = order[:0:-1]
        self.two = len(self.dims) > 1
        self.s, self.z, self.y, self.c = grid.here()
    at = Gather.at
    dev = Gather.dev
    def flips(self, f):
        return ''.join(d for d, on in zip(self.dims, f) if on)
    def idx(self, f, z):
        k = 0
        for on in f:
            k = k * 2 + on
        return k * self.g.depth + z
    def push(self, src, dst, recv, dim):
        pltpu.make_async_remote_copy(src, dst, self.send, recv, device_id=self.dev(dim), device_id_type=MESH).start()
    def wait(self, ref, sem):
        pltpu.make_async_copy(ref, ref, sem).wait()
    def combos(self):
        return [(1, 1), (1, 0), (0, 1), (0, 0)] if self.two else [(1,), (0,)]
    def far(self, d, body):
        @pl.when(self.z + d < self.g.depth)
        def _():
            body(self.z + d, '+')
        @pl.when(self.z >= d)
        def _():
            body(self.z - d, '-')
    def own(self, f, z):
        return self.src[self.at(self.flips(f), z)] if self.mine is None else self.mine[self.idx(f, z)]
    def load(self):
        for f in self.combos():
            def go(z, f=f):
                pltpu.make_async_copy(self.src.at[self.at(self.flips(f), z)], self.mine.at[self.idx(f, z)], self.local).start()
            each(self.g.depth, go)
    def loaded(self):
        pltpu.make_async_copy(self.mine, self.mine, self.local).wait()
    def start(self, which=slice(None)):
        for f in self.combos()[which]:
            def go(z, side, f=f):
                k = self.idx(f, z)
                self.push(self.src.at[self.at(self.flips(f) + 'c', z)], self.bufc.at[k], self.rc.at[k], 'c')
            def loop(k, _, go=go):
                self.far(self.g.depth - 1 - k, go)
                return _
            lax.fori_loop(0, self.g.depth - 1, loop, None)
            go(self.z, '')
    def stage1(self, f, d):
        def go(z, side):
            k = self.idx(f, z)
            buf = self.bufc.at[k]
            self.wait(buf, self.rc.at[k])
            buf[...] = (f32(self.own(f, z)) + f32(buf[...])).astype(buf.dtype)
            j = self.idx(f[1:], z)
            self.push(buf, self.buf1.at[j], self.r1.at[j], self.dims[0])
        self.far(d, go) if d is not None else go(self.z, '')
    def stage2(self, d):
        def go(z, side):
            k, j = self.idx((0, 1), z), self.idx((1,), z)
            bufc, buf = self.bufc.at[k], self.buf1.at[j]
            self.wait(bufc, self.rc.at[k])
            self.wait(buf, self.r1.at[j])
            buf[...] = (f32(self.own((0, 1), z)) + f32(bufc[...]) + f32(buf[...])).astype(buf.dtype)
            self.push(buf, self.buf2.at[z], self.r2.at[z], self.dims[1])
        self.far(d, go) if d is not None else go(self.z, '')
    def merged(self, z):
        k = self.idx((0,) * len(self.dims), z)
        bufc, buf1 = self.bufc.at[k], self.buf1.at[z]
        self.wait(bufc, self.rc.at[k])
        self.wait(buf1, self.r1.at[z])
        acc = f32(self.own((0,) * len(self.dims), z)) + f32(bufc[...]) + f32(buf1[...])
        if self.two:
            buf2 = self.buf2.at[z]
            self.wait(buf2, self.r2.at[z])
            acc = acc + f32(buf2[...])
        return acc, bufc
    def chain(self, d):
        top = self.g.depth - 1
        def go(zz, side):
            n = 0 if side == '+' else 1
            more = self.z > 0 if side == '+' else self.z < top
            acc, keep = self.merged(zz)
            keep[...] = acc.astype(keep.dtype)
            buf = self.bufz.at[n, zz]
            @pl.when(more)
            def _():
                self.wait(buf, self.rz.at[n, zz])
                keep[...] = (f32(keep[...]) + f32(buf[...])).astype(keep.dtype)
            pltpu.make_async_remote_copy(keep, buf, self.zsend.at[n, zz], self.rz.at[n, zz], device_id=self.dev(side), device_id_type=MESH).start()
        self.far(d, go)
    def total(self):
        top = self.g.depth - 1
        acc, _ = self.merged(self.z)
        self.out[0] = acc
        for n, ok in ((0, self.z > 0), (1, self.z < top)):
            @pl.when(ok)
            def _(n=n):
                buf = self.bufz.at[n, self.z]
                self.wait(buf, self.rz.at[n, self.z])
                self.out[0] += f32(buf[...])
    def finish(self):
        def sent(k):
            for n, ok in ((0, k > self.z), (1, k < self.z)):
                @pl.when(ok)
                def _(n=n):
                    self.wait(self.bufz.at[n, k], self.zsend.at[n, k])
        each(self.g.depth, sent)
        p = self.g.depth
        n = (4 + 2 + 1) * p if self.two else (2 + 1) * p
        v = self.src.at[pl.ds(0, n)]
        self.wait(v, self.send)

def scatter_scratch(grid, shape, dtype, order):
    p = grid.depth
    two = len(order) > 2
    n1, nc = (2 * p, 4 * p) if two else (p, 2 * p)
    D = pltpu.SemaphoreType.DMA
    return [pltpu.VMEM((nc,) + shape, dtype), pltpu.VMEM((n1,) + shape, dtype), pltpu.VMEM((p if two else 1,) + (shape if two else (8, 128)), dtype), pltpu.VMEM((2, p) + shape, dtype),
            D(()), D((2, p)), D((nc,)), D((n1,)), D((p,)), D((2, p))]

def pair_stack(x, half):
    lane = lax.broadcasted_iota(jnp.int32, x.shape, 1)
    zero = jnp.zeros_like(x)
    return jnp.concatenate((jnp.where(lane < half, x, zero), jnp.where(lane < half, zero, x)), axis=0)

def pair_join(x, half):
    r = x.shape[0] // 2
    lane = lax.broadcasted_iota(jnp.int32, (r, x.shape[1]), 1)
    return jnp.where(lane < half, x[:r], x[r:])

def nt(a, b):
    return lax.dot_general(a, b, (((1,), (1,)), ((), ())), preferred_element_type=jnp.float32)

def nn(a, b):
    return lax.dot_general(a, b, (((1,), (0,)), ((), ())), preferred_element_type=jnp.float32)

def tn(a, b):
    return lax.dot_general(a, b, (((0,), (0,)), ((), ())), preferred_element_type=jnp.float32)

def as_row(col):
    return jnp.transpose(jnp.broadcast_to(col, (col.shape[0], 128)))[0:1]

MASKED = -1e30

def forward_math(half, length, q, k, v):
    s = nt(pair_stack(q, half), k)
    s = jnp.where(lax.broadcasted_iota(jnp.int32, (1, s.shape[1]), 1) < length, s, MASKED)
    top = jnp.max(s, axis=1, keepdims=True)
    p = jnp.exp(s - top)
    total = jnp.sum(p, axis=1, keepdims=True)
    return pair_join(nn(p.astype(jnp.bfloat16), v) / total, half), as_row(top + jnp.log(total))

def forward_kernel(half, tiles, len_ref, q_ref, k_ref, v_ref, o_ref, lse_ref, top_ref, sum_ref, acc_ref):
    t = pl.program_id(1)
    q2 = pair_stack(q_ref[...], half)
    s = nt(q2, k_ref[...])
    wide = s.shape[1]
    col = lax.broadcasted_iota(jnp.int32, (1, wide), 1) + t * wide
    s = jnp.where(col < len_ref[0], s, MASKED)
    top = jnp.max(s, axis=1, keepdims=True)
    if tiles > 1:
        old = jnp.where(t == 0, MASKED, top_ref[...])
        top = jnp.maximum(old, top)
    p = jnp.exp(s - top)
    total = jnp.sum(p, axis=1, keepdims=True)
    acc = nn(p.astype(jnp.bfloat16), v_ref[...])
    if tiles > 1:
        factor = jnp.where(t == 0, 0.0, jnp.exp(old - top))
        total = total + jnp.where(t == 0, 0.0, sum_ref[...]) * factor
        acc = acc + jnp.where(t == 0, 0.0, acc_ref[...]) * factor
        top_ref[...], sum_ref[...], acc_ref[...] = top, total, acc
    @pl.when(t == tiles - 1)
    def _():
        o_ref[...] = pair_join(acc / total, half)
        lse_ref[0] = as_row(top + jnp.log(total))

def attend(q, k, v, length, heads, tile):
    rows, width = q.shape
    size = width // heads
    total, pairs = k.shape[0], heads // 2
    tiles = total // tile
    wide = 2 * size
    return pl.pallas_call(
        functools.partial(forward_kernel, size, tiles),
        grid_spec=pltpu.PrefetchScalarGridSpec(
            num_scalar_prefetch=1, grid=(pairs, tiles),
            in_specs=[pl.BlockSpec((rows, wide), lambda p, t, n: (0, p)),
                      pl.BlockSpec((tile, wide), lambda p, t, n: (t, p)),
                      pl.BlockSpec((tile, wide), lambda p, t, n: (t, p))],
            out_specs=[pl.BlockSpec((rows, wide), lambda p, t, n: (0, p)),
                       pl.BlockSpec((1, 1, 2 * rows), lambda p, t, n: (p, 0, 0))],
            scratch_shapes=[pltpu.VMEM((2 * rows, 1), jnp.float32), pltpu.VMEM((2 * rows, 1), jnp.float32), pltpu.VMEM((2 * rows, wide), jnp.float32)]),
        out_shape=[jax.ShapeDtypeStruct((rows, width), jnp.float32), jax.ShapeDtypeStruct((pairs, 1, 2 * rows), jnp.float32)],
        name="attend",
    )(length, q, k, v)

def backward_math(half, length, start, q, k, v, g, o, lse):
    q2, g2 = pair_stack(q, half), pair_stack(g, half)
    delta = jnp.sum(jnp.transpose(pair_stack(f32(g) * o, half)), axis=0, keepdims=True)
    s = nt(k, q2)
    row = lax.broadcasted_iota(jnp.int32, (s.shape[0], 1), 0) + start
    p = jnp.where(row < length, jnp.exp(s - lse), 0.0)
    ds = (p * (nt(v, g2) - delta)).astype(jnp.bfloat16)
    return tn(ds, k), nn(ds, q2), nn(p.astype(jnp.bfloat16), g2)

def backward_kernel(half, tiles, scale, len_ref, q_ref, k_ref, v_ref, g_ref, o_ref, lse_ref, dq_ref, dk_ref, dv_ref, sum_ref, acc_ref):
    t = pl.program_id(1)
    dq, dk, dv = backward_math(half, len_ref[0], t * k_ref.shape[0], q_ref[...], k_ref[...], v_ref[...], g_ref[...], o_ref[...], lse_ref[0])
    dk_ref[...] = dk.astype(jnp.bfloat16)
    dv_ref[...] = dv.astype(jnp.bfloat16)
    sums = jnp.sum(dv, axis=0, keepdims=True)
    sum_ref[0] = sums + jnp.where(t == 0, 0.0, sum_ref[0]) if tiles > 1 else sums
    if tiles > 1:
        dq = dq + jnp.where(t == 0, 0.0, acc_ref[...])
        acc_ref[...] = dq
    @pl.when(t == tiles - 1)
    def _():
        dq_ref[...] = (pair_join(dq, half) * scale).astype(jnp.bfloat16)

def attend_back(q, k, v, g, o, lse, length, heads, tile):
    rows, width = q.shape
    size = width // heads
    total, pairs = k.shape[0], heads // 2
    tiles = total // tile
    wide = 2 * size
    R = pl.BlockSpec((rows, wide), lambda p, t, n: (0, p))
    K = pl.BlockSpec((tile, wide), lambda p, t, n: (t, p))
    return pl.pallas_call(
        functools.partial(backward_kernel, size, tiles, size ** -0.5),
        grid_spec=pltpu.PrefetchScalarGridSpec(
            num_scalar_prefetch=1, grid=(pairs, tiles),
            in_specs=[R, K, K, R, R, pl.BlockSpec((1, 1, 2 * rows), lambda p, t, n: (p, 0, 0))],
            out_specs=[R, K, K, pl.BlockSpec((1, 1, wide), lambda p, t, n: (p, 0, 0))],
            scratch_shapes=[pltpu.VMEM((2 * rows, wide), jnp.float32)]),
        out_shape=[jax.ShapeDtypeStruct((rows, width), jnp.bfloat16)] + [jax.ShapeDtypeStruct((total, width), jnp.bfloat16)] * 2 + [jax.ShapeDtypeStruct((pairs, 1, wide), jnp.float32)],
        name="attend_back",
    )(length, q, k, v, g, o, lse)
ORDER = ("du", "pA", "ld", "d1,*", "As", "A1,*", "dv", "pB", "Bs", "B1,*", "d2,*", "e", "A4,*", "B4,d3,*", "g", "qs", "q1,*", "q2,*", "d4,*", "i", "q3,*", "q4,*")

def settle_kernel(grid, size, *refs):
    length, key_all, value_all, g_out, g_in, g_back, w_qkv, q, g, o, lse, x, base, g_bias, g_vec = refs[:15]
    d_qkv, d_out, d_in, d_back, d_bias, d_vec, grad_inputs = refs[15:22]
    own_key, own_value, w_query, w_key, w_value, grads, k_slots, v_slots, wide_w, vec_cols, vec_src, kA, vA, kB, vB = refs[22:37]
    kv_sem, w_sem, local = refs[37:40]
    mine = refs[40:43]
    bufs = refs[43:]
    rows, width = x.shape
    third, pair, pairs = width // 2, 2 * size, width // (2 * size)
    def pull(p):
        at = pl.multiple_of(p * pair, pair)
        return [pltpu.make_async_copy(src.at[:, pl.ds(at, pair)], slots.at[lax.rem(p, 2)], kv_sem.at[n, lax.rem(p, 2)])
                for n, (src, slots) in enumerate(((key_all, k_slots), (value_all, v_slots)))]
    for copy in pull(0): copy.start()
    greet(grid, True)
    cut = lambda n: d_qkv.at[:, :, pl.ds(n * width, width)]
    part_of = lambda ref, n: ref.at[:, :, pl.ds(n * third, third)]
    specs = [("A", vA, part_of(own_value, 0), "zy"), ("A", kA, part_of(own_key, 0), "zy"), ("B", vB, part_of(own_value, 1), "zy"), ("B", kB, part_of(own_key, 1), "zy"),
             ("d", g_back, d_back, "zyx"), ("d", g_in, d_in, "zyx"), ("d", g_out, d_out, "zyx"), ("d", g_bias, d_bias, "zyx"),
             ("q", vec_src, d_vec, "zyx"), ("q", w_query, cut(0), "zyx"), ("q", w_key, cut(1), "zyx"), ("q", w_value, cut(2), "zyx")]
    jobs = {"A": [], "B": [], "d": [], "q": []}
    for n, (group, src, out, order) in enumerate(specs):
        r = bufs[10 * n:10 * n + 10]
        extra = (mine[n - 4], local.at[n - 4]) if 4 <= n < 7 else ()
        jobs[group].append(Scatter(grid, src, out, r[:4], r[4], r[5], r[6:10], order, *extra))
    big = jobs["d"][:3]
    def weigh(at, dst):
        part, wide = dst.shape[1], width // 2
        for n in range(2):
            full = tn(x[...], grads[:, at + n * wide:at + (n + 1) * wide])
            for k in range(dst.shape[0]):
                dst[k, :, n * wide:(n + 1) * wide] = full[k * part:(k + 1) * part].astype(dst.dtype)
    lane = lax.broadcasted_iota(jnp.int32, (pair, 128), 1)
    def attention(first, dk, dv):
        def one(j, _):
            p = first + j
            slot = lax.rem(p, 2)
            @pl.when(p + 1 < pairs)
            def _():
                for copy in pull(p + 1): copy.start()
            for copy in pull(p): copy.wait()
            at = pl.ds(pl.multiple_of(p * pair, pair), pair)
            to = pl.ds(pl.multiple_of(j * pair, pair), pair)
            dq, dk_part, dv_part = backward_math(size, length[0], 0, q[:, at], k_slots[slot], v_slots[slot], g[:, at], o[:, at], lse[p])
            dk[:, :, to] = dk_part.astype(dk.dtype).reshape(dk.shape[0], rows, pair)
            dv[:, :, to] = dv_part.astype(dv.dtype).reshape(dv.shape[0], rows, pair)
            dq = (pair_join(dq, size) * size ** -0.5).astype(grads.dtype)
            grads[:, at] = dq
            tall = lambda v: jnp.transpose(jnp.broadcast_to(jnp.sum(f32(v), axis=0, keepdims=True), (128, pair)))
            vec_cols[at, :] = jnp.where(lane == 0, tall(dq), jnp.where(lane == 1, tall(dv_part), g_vec[at, :]))
            return _
        lax.fori_loop(0, pairs // 2, one, None)
    def early():
        weigh(0, w_query)
        part = vec_src.shape[1]
        for k in range(vec_src.shape[0]):
            vec_src[k] = vec_cols[k * part:(k + 1) * part]
    def after():
        grads[:, width:2 * width] = own_key[0].astype(grads.dtype)
        grads[:, 2 * width:] = own_value[0].astype(grads.dtype)
        weigh(width, w_key)
        weigh(2 * width, w_value)
    def inward():
        total = base[...]
        for n in range(3):
            copy = pltpu.make_async_copy(w_qkv.at[:, pl.ds(n * width, width)], wide_w, w_sem)
            copy.start()
            copy.wait()
            total = total + nt(grads[:, n * width:(n + 1) * width], wide_w[...])
        grad_inputs[...] = total
    alone = {"pA": lambda: attention(0, kA, vA), "pB": lambda: attention(pairs // 2, kB, vB), "e": early, "g": after, "i": inward,
             "ld": lambda: [job.loaded() for job in big]}
    def step(word, d):
        for job in jobs[word[0]]:
            if word[1] in "su":
                if job.mine is not None: job.load()
                job.start(slice(None, None if word[1] == "s" else 1))
            elif word[1] == "v": job.start(slice(1, None))
            elif word[1] == "1": job.stage1(job.combos()[0], d)
            elif word[1] == "2": job.stage1((1, 0), d)
            elif word[1] == "3": job.stage2(d)
            elif d is None: job.total()
            else: job.chain(d)
    for phase in ORDER:
        words = phase.split(",")
        if phase in alone: alone[phase]()
        elif words[-1] == "*":
            def loop(k, _, words=words):
                for word in words[:-1]: step(word, grid.depth - 1 - k)
                return _
            lax.fori_loop(0, grid.depth - 1, loop, None)
            for word in words[:-1]: step(word, None)
        else:
            for word in words: step(word, None)
    for group in "ABdq":
        for job in jobs[group]: job.finish()

def settle(grid, size, length, key_all, value_all, g_out, g_in, g_back, w_qkv, q, g, o, lse, x, base, g_bias, g_vec):
    bf, f4 = jnp.bfloat16, jnp.float32
    rows, width = x.shape
    part, devices = g_out.shape[1], grid.seqs * grid.ctx
    slots, pair = key_all.shape[0], 2 * size
    S = jax.ShapeDtypeStruct
    V, A = pl.BlockSpec(memory_space=pltpu.VMEM), pl.BlockSpec(memory_space=pl.ANY)
    D, M = pltpu.SemaphoreType.DMA, pltpu.VMEM
    scratch = [M((1, rows, width), f4)] * 2 + [M((devices, part, width), bf)] * 3 + [M((rows, 3 * width), bf)] + [M((2, slots, pair), bf)] * 2
    scratch += [M((width, width), bf), M((width, 128), f4), M((devices, part, 128), f4)] + [M((grid.ctx, rows, width // 2), bf)] * 4
    scratch += [D((2, 2)), D(()), D((3,))] + [M((devices // 2,) + a.shape[1:], bf) for a in (g_back, g_in, g_out)]
    for shape, dtype, order in ([((rows, width // 2), bf, "zy")] * 4 + [(a.shape[1:], a.dtype, "zyx") for a in (g_back, g_in, g_out, g_bias)]
                                + [((part, 128), f4, "zyx"), ((part, width), bf, "zyx"), ((part, width), bf, "zyx"), ((part, width), bf, "zxy")]):
        scratch += scatter_scratch(grid, shape, dtype, order)
    one = lambda a: S((1,) + a.shape[1:], f4)
    return pl.pallas_call(
        functools.partial(settle_kernel, grid, size),
        out_shape=[S((1, part, 3 * width), f4), one(g_out), one(g_in), one(g_back), one(g_bias), S((1, part, 128), f4), S((rows, width), f4)],
        in_specs=[pl.BlockSpec(memory_space=pltpu.SMEM)] + [A] * 6 + [V] * 8, out_specs=[V] * 7, scratch_shapes=scratch,
        compiler_params=pltpu.CompilerParams(collective_id=1, has_side_effects=True, vmem_limit_bytes=63 * 2**20),
        name="settle",
    )(length, key_all, value_all, g_out, g_in, g_back, w_qkv, q, g, o, lse, x, base, g_bias, g_vec)

HEADS = 12
EPSILON = 1e-12

def normalize(u):
    mean = jnp.mean(u, axis=-1, keepdims=True)
    centred = u - mean
    r = lax.rsqrt(jnp.mean(centred * centred, axis=-1, keepdims=True) + EPSILON)
    return centred * r, r

def normalize_back(e, n, r, gain):
    c = e * gain
    return r * (c - jnp.mean(c, axis=-1, keepdims=True) - n * jnp.mean(c * n, axis=-1, keepdims=True))

def gelu_parts(v):
    cdf = 0.5 * (1.0 + lax.erf(v * (0.5 ** 0.5)))
    slope = cdf + v * jnp.exp(-0.5 * v * v) * ((2 * jnp.pi) ** -0.5)
    return v * cdf, slope

def layer_kernel(grid, length, w_out_hbm, w_in_hbm, w_back_hbm, attended_ref, x, cotangent, vec_all, bias_all,
                 g_out_hbm, g_in_hbm, g_back_hbm, result, grad_attended, base, g_bias, g_vec,
                 w_out, w_in, w_back, g_out, g_in, g_back, bias, in_sem, out_sem):
    bf = jnp.bfloat16
    loads = [pltpu.make_async_copy(src, dst, in_sem.at[n]) for n, (src, dst) in enumerate(((w_out_hbm, w_out), (w_in_hbm, w_in), (w_back_hbm, w_back)))]
    for copy in loads: copy.start()
    stores = [pltpu.make_async_copy(src, dst, out_sem.at[n]) for n, (src, dst) in enumerate(((g_out, g_out_hbm), (g_in, g_in_hbm), (g_back, g_back_hbm)))]
    rows, width = x.shape
    devices, part_ff = g_back.shape[:2]
    part = g_in.shape[1]
    lane = lax.broadcasted_iota(jnp.int32, (16, 128), 1)
    pick = (lane == lax.broadcasted_iota(jnp.int32, (16, 128), 0)).astype(bf)
    vec = nt(pick, vec_all[...])
    for k in range(devices):
        bias[0:1, k * part_ff:(k + 1) * part_ff] = f32(bias_all[k])[0:1, :part_ff]
    attended = attended_ref[...].astype(bf)
    loads[0].wait()
    branch = nn(attended, w_out[...]) + vec[2:3]
    norm_one, r_one = normalize(f32(x[...]) + branch)
    first = norm_one * vec[3:4] + vec[4:5]
    first_low = first.astype(bf)
    loads[1].wait()
    hidden = nn(first_low, w_in[...]) + bias[0:1]
    active_f, slope = gelu_parts(hidden)
    active = active_f.astype(bf)
    loads[2].wait()
    second = nn(active, w_back[...]) + vec[5:6]
    norm_two, r_two = normalize(first + second)
    result[...] = (norm_two * vec[6:7] + vec[7:8]).astype(bf)
    slot = lax.broadcasted_iota(jnp.int32, (rows, 1), 0) + lax.axis_index("ctx") * rows
    grad_result = jnp.where(slot < length[0], f32(cotangent[...]), 0.0)
    grad_second = normalize_back(grad_result, norm_two, r_two, vec[6:7])
    grad_second_low = grad_second.astype(bf)
    grad_hidden_f = nt(grad_second_low, w_back[...]) * slope
    grad_hidden = grad_hidden_f.astype(bf)
    for n in range(devices * part_ff // width):
        full = tn(active[:, n * width:(n + 1) * width], grad_second_low).astype(bf)
        for k in range(width // part_ff):
            g_back[n * (width // part_ff) + k] = full[k * part_ff:(k + 1) * part_ff]
    stores[2].start()
    for n in range(devices * part_ff // width):
        full = tn(first_low, grad_hidden[:, n * width:(n + 1) * width])
        for k in range(devices):
            g_in[k, :, n * width:(n + 1) * width] = full[k * part:(k + 1) * part].astype(bf)
    stores[1].start()
    grad_first = grad_second + nt(grad_hidden, w_in[...])
    grad_branch_full = normalize_back(grad_first, norm_one, r_one, vec[3:4])
    base[...] = grad_branch_full
    grad_branch = grad_branch_full.astype(bf)
    grad_attended[...] = nt(grad_branch, w_out[...]).astype(bf)
    full = tn(attended, grad_branch)
    for k in range(devices):
        g_out[k] = full[k * part:(k + 1) * part].astype(bf)
    stores[0].start()
    total = lambda a: jnp.sum(f32(a), axis=0, keepdims=True)
    sums = total(grad_hidden)
    g_bias[...] = jnp.zeros_like(g_bias)
    for k in range(devices):
        g_bias[k, 0:1, 0:part_ff] = sums[:, k * part_ff:(k + 1) * part_ff]
    stack = jnp.concatenate((jnp.zeros((2, width), jnp.float32), total(grad_branch), total(grad_first * norm_one), total(grad_first),
                             total(grad_second_low), total(grad_result * norm_two), total(grad_result), jnp.zeros((120, width), jnp.float32)), axis=0)
    for n in range(width // 128):
        g_vec[n * 128:(n + 1) * 128, :] = jnp.transpose(stack[:, n * 128:(n + 1) * 128])
    for copy in stores: copy.wait()

def layer(grid, length, w_out, w_in, w_back, attended, x, cotangent, vec_all, bias_all):
    bf, f4 = jnp.bfloat16, jnp.float32
    rows, width = x.shape
    hidden = w_in.shape[1]
    devices = grid.seqs * grid.ctx
    S, M, D = jax.ShapeDtypeStruct, pltpu.VMEM, pltpu.SemaphoreType.DMA
    V, A = pl.BlockSpec(memory_space=pltpu.VMEM), pl.BlockSpec(memory_space=pl.ANY)
    grads = [(devices, width // devices, width), (devices, width // devices, hidden), (devices, hidden // devices, width)]
    return pl.pallas_call(
        functools.partial(layer_kernel, grid),
        out_shape=[S(g, bf) for g in grads] + [S((rows, width), bf), S((rows, width), bf), S((rows, width), f4), S((devices, 8, 128), f4), S((width, 128), f4)],
        in_specs=[pl.BlockSpec(memory_space=pltpu.SMEM)] + [A] * 3 + [V] * 5, out_specs=[A] * 3 + [V] * 5,
        scratch_shapes=[M(w.shape, bf) for w in (w_out, w_in, w_back)] + [M(g, bf) for g in grads] + [M((8, hidden), f4), D((3,)), D((3,))],
        compiler_params=pltpu.CompilerParams(vmem_limit_bytes=60 * 2**20),
        name="layer",
    )(length, w_out, w_in, w_back, attended, x, cotangent, vec_all, bias_all)

def deliver_kernel(*refs):
    n = len(refs) // 2
    for k, (src, dst) in enumerate(zip(refs[:n], refs[n:])):
        if k == 0:
            tall = jnp.concatenate((src[0], jnp.zeros((128 - src.shape[1], 128), jnp.float32)), axis=0)
            dst[...] = jnp.transpose(tall)[:dst.shape[0], :dst.shape[1]]
        elif len(dst.shape) == 3: dst[0] = src[...]
        else: dst[...] = src[0, :dst.shape[0], :dst.shape[1]]

def deliver(arrays, shapes):
    V = pl.BlockSpec(memory_space=pltpu.VMEM)
    return pl.pallas_call(
        deliver_kernel, out_shape=[jax.ShapeDtypeStruct(s, jnp.float32) for s in shapes],
        in_specs=[V] * len(arrays), out_specs=[V] * len(arrays), name="deliver",
    )(*arrays)

def per_device(grid, inputs, lengths, cotangent, w_qkv, w_out, w_in, w_back, vectors, ffn_bias):
    bf, f4 = jnp.bfloat16, jnp.float32
    rows_in = inputs[0]
    rows, width = rows_in.shape
    hidden_size = w_in.shape[1]
    devices = grid.seqs * grid.ctx
    part, part_ff = w_qkv.shape[0], w_back.shape[0]
    slots = grid.ctx * rows
    scale = (width // HEADS) ** -0.5

    half = 3 * width // 2
    whole = grid.depth <= 4 and part % 8 == 0 and part_ff <= 128
    if whole:
        qkv_full, vec_all, bias_all, out_all, in_all, back_all, key_all, value_all, query_scaled, attended_f, lse = fetch(
            grid, width // HEADS, lengths, rows_in, w_qkv, vectors.T, ffn_bias[None], w_out[None], w_in[None], w_back[None])
        out_full, in_full, back_full = out_all.reshape(width, width), in_all.reshape(width, hidden_size), back_all.reshape(hidden_size, width)
    else:
        everywhere = lambda a: lax.all_gather(a, ("seq", "ctx"), axis=0, tiled=True)
        qkv_full, out_full, in_full, back_full = everywhere(w_qkv), everywhere(w_out), everywhere(w_in), everywhere(w_back)
        vec = everywhere(vectors).T.astype(f4)
        ffn_full = everywhere(ffn_bias)[None].astype(f4)
        projected = jnp.dot(rows_in, qkv_full, preferred_element_type=f4)
        query_scaled = (projected[:, :width] + vec[0]).astype(bf) * jnp.asarray(scale, bf)
        key = projected[:, width:2 * width].astype(bf)
        value = (projected[:, 2 * width:] + vec[1]).astype(bf)
        key_all, value_all = (lax.all_gather(a, "ctx", axis=0, tiled=True) for a in (key, value))

    if whole:
        g_out, g_in, g_back, result, grad_attended, base, g_bias, g_vec = layer(
            grid, lengths, out_full, in_full, back_full, attended_f, rows_in, cotangent[0], vec_all, bias_all)
        d_qkv, d_out, d_in, d_back, d_bias, d_vec, grad_inputs = settle(
            grid, width // HEADS, lengths, key_all, value_all, g_out, g_in, g_back, qkv_full, query_scaled, grad_attended, attended_f, lse, rows_in, base, g_bias, g_vec)
        d_vec, grad_inputs, d_qkv, d_out, d_in, d_back, d_bias = deliver(
            (d_vec, grad_inputs, d_qkv, d_out, d_in, d_back, d_bias),
            ((8, part), (1, rows, width), (part, 3 * width), (part, width), (part, hidden_size), (part_ff, width), (1, part_ff)))
        return (result[None], grad_inputs, d_qkv, d_out, d_in, d_back, d_vec.T, d_bias[0])
    tile = min(slots, 2048)
    attended_f, lse = attend(query_scaled, key_all, value_all, lengths, HEADS, tile)
    attended = attended_f.astype(bf)
    branch = jnp.dot(attended, out_full, preferred_element_type=f4) + vec[2]
    norm_one, r_one = normalize(rows_in.astype(f4) + branch)
    first = norm_one * vec[3] + vec[4]
    first_low = first.astype(bf)
    hidden = jnp.dot(first_low, in_full, preferred_element_type=f4) + ffn_full
    active_f, slope = gelu_parts(hidden)
    active = active_f.astype(bf)
    second = jnp.dot(active, back_full, preferred_element_type=f4) + vec[5]
    norm_two, r_two = normalize(first + second)
    result = (norm_two * vec[6] + vec[7]).astype(bf)
    start = lax.axis_index("ctx") * rows
    valid = (start + jnp.arange(rows, dtype=jnp.int32) < lengths[0]).astype(f4)[:, None]
    grad_result = cotangent[0].astype(f4) * valid
    grad_second = normalize_back(grad_result, norm_two, r_two, vec[6])
    grad_second_low = grad_second.astype(bf)
    grad_active = lax.dot_general(grad_second_low, back_full, (((1,), (1,)), ((), ())), preferred_element_type=f4)
    grad_hidden = (grad_active * slope).astype(bf)
    grad_first = grad_second + lax.dot_general(grad_hidden, in_full, (((1,), (1,)), ((), ())), preferred_element_type=f4)
    grad_branch_full = normalize_back(grad_first, norm_one, r_one, vec[3])
    grad_branch = grad_branch_full.astype(bf)
    grad_attended = lax.dot_general(grad_branch, out_full, (((1,), (1,)), ((), ())), preferred_element_type=f4).astype(bf)

    def outer(a, b):
        return lax.dot_general(a, b, (((0,), (0,)), ((), ())), preferred_element_type=f4).astype(bf)
    g_back = outer(active, grad_second_low)
    g_in = outer(first_low, grad_hidden)
    g_out = outer(attended, grad_branch)
    grad_ffn = jnp.sum(grad_hidden.astype(f4), axis=0)
    sums = (jnp.sum(grad_branch.astype(f4), axis=0), jnp.sum(grad_first * norm_one, axis=0), jnp.sum(grad_first, axis=0),
            jnp.sum(grad_second_low.astype(f4), axis=0), jnp.sum(grad_result * norm_two, axis=0), jnp.sum(grad_result, axis=0))
    grad_query, g_key, g_value, sum_value = attend_back(query_scaled, key_all, value_all, grad_attended, attended_f, lse, lengths, HEADS, tile)
    sums = jnp.stack((jnp.sum(grad_query.astype(f4), axis=0), sum_value.reshape(width)) + sums)
    home = lambda a, axes: lax.psum_scatter(a.astype(f4), axes, scatter_dimension=0, tiled=True)
    own_key, own_value = (home(a, "ctx").astype(bf) for a in (g_key, g_value))
    grad_projected = jnp.concatenate((grad_query, own_key, own_value), axis=1)
    grad_inputs = grad_branch_full + lax.dot_general(grad_projected, qkv_full, (((1,), (1,)), ((), ())), preferred_element_type=f4)
    both = ("seq", "ctx")
    return (result[None], grad_inputs[None], home(outer(rows_in, grad_projected), both), home(g_out, both), home(g_in, both), home(g_back, both),
            home(sums.T, both), home(grad_ffn, both))

def solution(mesh):
    grid = Grid(mesh.shape["seq"], mesh.shape["ctx"])
    split, both = P("seq", "ctx", None), P(("seq", "ctx"), None)
    return jax.shard_map(
        functools.partial(per_device, grid), mesh=mesh,
        in_specs=(split, P("seq"), split, both, both, both, both, both, P(("seq", "ctx"))),
        out_specs=(split, split, both, both, both, both, both, P(("seq", "ctx"))),
        check_vma=False,
    )
```
